128 devices in a mesh: grp: 2 (over core), reg: 64 (over z, x, y).
Axes of the slice: x: 4, y: 4, z: 4, core: 2. Of those that a mesh axis runs over, the one named last changes fastest.
Arguments:
- cam_jacobian: bfloat16 [18, 262144], P(None, ('grp', 'reg')), may hold values from -6 to 6
- point_jacobian: bfloat16 [6, 262144], P(None, ('grp', 'reg')), may hold values from -6 to 6
- residuals: float32 [2, 262144], P(None, ('grp', 'reg')), may hold values from -48 to 48
- obs_camera: int32 [262144], P(('grp', 'reg')), may hold values from 0 to 16383, as said below
- obs_point: int32 [262144], P(('grp', 'reg')), may hold values from 0 to 255
Outputs:
- cam_step: float32 [9, 16384], P(None, ('grp', 'reg'))
- point_step: float32 [3, 32768], P(None, ('grp', 'reg'))
The draws below stay inside these ranges and needn't reach their ends.
Inputs may be any that keep to these rules, and one draw needn't show every extreme that they name: `obs_camera`: an observation in block d of 2048 rows sees a camera of block e = camera // 128 such that d // (number of reg devices) and e // (number of reg devices) may differ, but d and e differ by at most one modulo the number of reg devices (the same, the previous or the next region, never across the ends); every such block is seen.
All inputs are finite; a program needn't handle non-finite values.
Results may differ from the reference program's by a relative error of at most 0.0003.
Values sent between devices are 32-bit elements; how exact they have to be, the bound alone decides.
No kernel may reach another device: no remote copies, remote signals or barrier semaphores. Data moves between devices by JAX's collectives and lax.ppermute only.
A program may use at most 64 MiB of HBM per device.

```python
import math
import jax
import jax.numpy as jnp
import numpy as np
from jax import lax

C_DEV = 128
P_DEV = 256
OBS_DEV = 2048
ITERS = 3
CAMS = 16384
POINTS = 32768
OBSERVATIONS = 262144
N_REG = 64


def draw_obs_camera(key, part):
    rows_index = jnp.arange(OBSERVATIONS, dtype=jnp.int32)
    owner_block = rows_index // OBS_DEV
    region = owner_block % N_REG
    key_first, key_second, key_third = jax.random.split(key, 3)
    offset = jax.random.randint(key_first, (OBSERVATIONS,), -1, 2)
    target = region + offset
    target = jnp.where(target < 0, region + 1, jnp.where(target >= N_REG, region - 1, target))
    partner = jax.random.randint(key_second, (OBSERVATIONS,), 0, 2)
    column = jax.random.randint(key_third, (OBSERVATIONS,), 0, C_DEV)
    return ((partner * N_REG + target) * C_DEV + column).astype(jnp.int32)


def set_ends(array, stream_key, low, high):
    place = [jax.random.randint(jax.random.fold_in(stream_key, axis), (), 0, length) for axis, length in enumerate(array.shape)]
    longest = array.shape.index(max(array.shape))
    beside = place[:longest] + [(place[longest] + 1) % array.shape[longest]] + place[longest + 1:]
    return array.at[tuple(place)].set(low).at[tuple(beside)].set(high)


def block_scale(key, shape, cuts, smallest, top_value):
    level = 1.0
    for position, shards_of in cuts:
        steps = jax.random.uniform(jax.random.fold_in(jax.random.fold_in(key, 6), position), (shards_of,), jnp.float32, smallest / len(cuts), top_value / len(cuts))
        level = level * jnp.repeat(jnp.exp(steps), shape[position] // shards_of).reshape((-1,) + (1,) * (len(shape) - 1 - position))
    return level


def cumulative_ranks(count, lean):
    loads = [(1 << 20) // math.isqrt(standing ** lean) + 1 for standing in range(1, count + 1)]
    width = 1 + sum(loads) // (1 << 30)
    return np.cumsum(np.array([max(1, weight // width) for weight in loads]))


def ranked_ids(own_key, dims, count, skew):
    grid = cumulative_ranks(count, skew)
    pick = jax.random.randint(jax.random.fold_in(own_key, 1), dims, 0, int(grid[count - 1]))
    grade = jnp.searchsorted(jnp.asarray(grid, jnp.int32), pick, side="right")
    return jax.random.permutation(jax.random.fold_in(own_key, 2), count)[grade].astype(jnp.int32)


def gaussian(own_key, shape, deviation, limit, cuts=(), kind=jnp.bfloat16):
    factor_of = block_scale(own_key, shape, cuts, -0.22, 0.18) if cuts else 1.0
    entries = jax.random.normal(own_key, shape, jnp.float32) * deviation * factor_of
    return jnp.minimum(jnp.maximum(entries, -limit), limit).astype(kind)


def setup_inputs(seed: int = 0) -> dict:
    arg_keys = jax.random.split(jax.random.key(seed), 6)
    return {
        "cam_jacobian": gaussian(arg_keys[0], (18, OBSERVATIONS), 1.0, 6.0, ((1, 128),)),
        "point_jacobian": gaussian(arg_keys[1], (6, OBSERVATIONS), 1.0, 6.0, ((1, 128),)),
        "residuals": gaussian(arg_keys[2], (2, OBSERVATIONS), 8.0, 48.0, ((1, 128),), jnp.float32),
        "obs_camera": draw_obs_camera(jax.random.fold_in(arg_keys[5], 71), 0),
        "obs_point": set_ends(ranked_ids(arg_keys[4], (OBSERVATIONS,), P_DEV, 1), jax.random.fold_in(arg_keys[4], 3), 0, P_DEV - 1).astype(jnp.int32),
    }


DAMPING = 4.0

def inverse_three(matrix):
    a, b, c, d, e, f, g, h, i = [matrix[k] for k in range(9)]
    adjoint = [e * i - f * h, c * h - b * i, b * f - c * e, f * g - d * i, a * i - c * g, c * d - a * f, d * h - e * g, b * g - a * h, a * e - b * d]
    determinant = a * adjoint[0] + b * adjoint[3] + c * adjoint[6]
    return jnp.stack(adjoint) / determinant

def apply_three(inverse, vector):
    return jnp.stack([inverse[3 * i] * vector[0] + inverse[3 * i + 1] * vector[1] + inverse[3 * i + 2] * vector[2] for i in range(3)])

def cholesky_rows(blocks):
    factor = [[None] * 9 for i in range(9)]
    for i in range(9):
        for j in range(i + 1):
            total = blocks[9 * i + j]
            for k in range(j):
                total = total - factor[i][k] * factor[j][k]
            if i == j:
                factor[i][i] = jnp.sqrt(total)
            else:
                factor[i][j] = total / factor[j][j]
    return factor

def cholesky_apply(factor, right):
    forward = []
    for i in range(9):
        total = right[i]
        for k in range(i):
            total = total - factor[i][k] * forward[k]
        forward.append(total / factor[i][i])
    backward = [None] * 9
    for i in range(8, -1, -1):
        total = forward[i]
        for k in range(i + 1, 9):
            total = total - factor[k][i] * backward[k]
        backward[i] = total / factor[i][i]
    return jnp.stack(backward)

def eliminate(values, cam_rows, point_rows, point_slot, inverse, count):
    gathered = jnp.zeros((3, count), jnp.float32).at[:, point_slot].add(lax.optimization_barrier(jnp.sum(point_rows * values[:, None], 0)))
    solved = apply_three(inverse, gathered)
    remain = values - lax.optimization_barrier(jnp.sum(point_rows * solved[:, point_slot][None], 1))
    return lax.optimization_barrier(jnp.sum(cam_rows * remain[:, None], 0))

def reference(cam_jacobian, point_jacobian, residuals, obs_camera, obs_point):
    rows_index = jnp.arange(OBSERVATIONS, dtype=jnp.int32)
    point_slot = (obs_point + rows_index // OBS_DEV * P_DEV).astype(jnp.int32)
    cam_rows = cam_jacobian.astype(jnp.float32).reshape(2, 9, OBSERVATIONS)
    point_rows = point_jacobian.astype(jnp.float32).reshape(2, 3, OBSERVATIONS)
    pairs = lax.optimization_barrier(jnp.sum(point_rows[:, :, None] * point_rows[:, None, :], 0)).reshape(9, OBSERVATIONS)
    point_blocks = jnp.zeros((9, POINTS), jnp.float32).at[:, point_slot].add(pairs)
    point_blocks = point_blocks + DAMPING * jnp.eye(3, dtype=jnp.float32).reshape(9, 1)
    inverse = inverse_three(point_blocks)
    outer = lax.optimization_barrier(jnp.sum(cam_rows[:, :, None] * cam_rows[:, None, :], 0)).reshape(81, OBSERVATIONS)
    normal = jnp.zeros((81, CAMS), jnp.float32).at[:, obs_camera].add(outer)
    blocks = normal + DAMPING * jnp.eye(9, dtype=jnp.float32).reshape(81, 1)
    factor = cholesky_rows(blocks)
    right = -jnp.zeros((9, CAMS), jnp.float32).at[:, obs_camera].add(eliminate(residuals, cam_rows, point_rows, point_slot, inverse, POINTS))

    def reduced(direction):
        values = lax.optimization_barrier(jnp.sum(cam_rows * direction[:, obs_camera][None], 1))
        terms = eliminate(values, cam_rows, point_rows, point_slot, inverse, POINTS)
        return DAMPING * direction + jnp.zeros((9, CAMS), jnp.float32).at[:, obs_camera].add(terms)
    cam_step = jnp.zeros((9, CAMS), jnp.float32)
    residual = right
    precon = cholesky_apply(factor, residual)
    direction = precon
    current = jnp.sum(residual * precon)
    for turn in range(ITERS):
        product = reduced(direction)
        step_size = current / jnp.sum(direction * product)
        cam_step = cam_step + step_size * direction
        if turn + 1 < ITERS:
            residual = residual - step_size * product
            precon = cholesky_apply(factor, residual)
            following = jnp.sum(residual * precon)
            direction = precon + following / current * direction
            current = following
    values = residuals + lax.optimization_barrier(jnp.sum(cam_rows * cam_step[:, obs_camera][None], 1))
    gathered = jnp.zeros((3, POINTS), jnp.float32).at[:, point_slot].add(lax.optimization_barrier(jnp.sum(point_rows * values[:, None], 0)))
    point_step = -apply_three(inverse, gathered)
    return (cam_step, point_step)
```

```python
import functools

import jax
import jax.numpy as jnp
from jax import lax
from jax.experimental import pallas as pl
from jax.experimental.pallas import tpu as pltpu
from jax.sharding import Mesh
from jax.sharding import PartitionSpec as P

C_DEV = 128
P_DEV = 256
OBS = 2048
DAMPING = 4.0
WIDE = 2 * C_DEV
REG = ("reg_0", "reg_1", "reg_2")
GRP_REG = ("grp", "reg_0", "reg_1", "reg_2")
F32 = jnp.float32
BF16 = jnp.bfloat16
VMEM = pl.BlockSpec(memory_space=pltpu.VMEM)
SMEM = pl.BlockSpec(memory_space=pltpu.SMEM)


def three_parts(x):
    high = x.astype(BF16)
    rest = x - high.astype(F32)
    middle = rest.astype(BF16)
    low = (rest - middle.astype(F32)).astype(BF16)
    return high, middle, low


def stacked(x):
    high, middle, low = three_parts(x)
    parts = [high.astype(F32), middle.astype(F32), low.astype(F32)]
    return jnp.concatenate(parts, 0).astype(BF16)


def folded(x):
    rows = x.shape[0] // 3
    return x[:rows] + x[rows : 2 * rows] + x[2 * rows :]


def pick(field, onehot):
    return lax.dot_general(
        field, onehot, (((1,), (0,)), ((), ())), preferred_element_type=F32
    )


def put(terms, onehot):
    return lax.dot_general(
        terms, onehot, (((1,), (1,)), ((), ())), preferred_element_type=F32
    )


def onehot_of(index):
    ids = lax.broadcasted_iota(jnp.int32, (WIDE, index.shape[1]), 0)
    return jnp.where(ids == index, 1.0, 0.0).astype(BF16)


def total(x):
    return jnp.sum(jnp.sum(x, 0, keepdims=True), 1, keepdims=True)


def per_lane(x):
    row = jnp.sum(x, 0, keepdims=True)
    return functools.reduce(
        lambda a, b: a + b, [row[:, k : k + 128] for k in range(0, row.shape[1], 128)]
    )


def solve_points(vinv, g):
    a, b, c, d, e, f = [vinv[k : k + 1] for k in range(6)]
    x, y, z = [g[k : k + 1] for k in range(3)]
    rows = [a * x + b * y + c * z, b * x + d * y + e * z, c * x + e * y + f * z]
    return rows + [jnp.zeros((8 - 3, g.shape[1]), F32)]


def point_part(u, p, hot_p, vinv):
    g = folded(put(stacked(p[0] * u[0] + p[1] * u[1]), hot_p))
    s = jnp.concatenate(solve_points(vinv, g), 0)
    back = folded(pick(stacked(s), hot_p))
    return g, s, [jnp.sum(p[i] * back, 0, keepdims=True) for i in range(2)]


def first_kernel(cam, pnt, res, index, part, jx, px, vinv_out, gres_out):
    low, block, slot = index[0:1, :], index[1:2, :], index[2:3, :]
    hot_p = onehot_of(slot)
    camf = cam[...].astype(F32)
    pf = pnt[...].astype(F32)
    zero5 = jnp.zeros((5, OBS), F32)
    zero7 = jnp.zeros((7, OBS), F32)
    for i in range(2):
        jx[i, 0:8, :] = camf[9 * i : 9 * i + 8]
        jx[i, 8:16, :] = jnp.concatenate([camf[9 * i + 8 : 9 * i + 9], zero7], 0)
        px[i] = jnp.concatenate([pf[3 * i : 3 * i + 3], zero5], 0)
    p = [px[0], px[1]]
    a = [jx[0, 0:8, :], jx[1, 0:8, :]]
    last = [jx[0, 8:9, :], jx[1, 8:9, :]]
    r = [res[0:1, :], res[1:2, :]]
    row = lax.broadcasted_iota(jnp.int32, (8, OBS), 0)
    squares = p[0] * p[0] + p[1] * p[1]
    turned = [
        jnp.where(row == 2, jnp.broadcast_to(x[0:1], x.shape), pltpu.roll(x, 7, 0)) for x in p
    ]
    products = p[0] * turned[0] + p[1] * turned[1]
    right = p[0] * r[0] + p[1] * r[1]
    sums = folded(put(stacked(jnp.concatenate([squares, products, right], 0)), hot_p))
    v00, v11, v22 = [sums[k : k + 1] + DAMPING for k in range(3)]
    v01, v12, v02 = [sums[8 + k : 9 + k] for k in range(3)]
    g = sums[16:24]
    c00 = v11 * v22 - v12 * v12
    c01 = v02 * v12 - v01 * v22
    c02 = v01 * v12 - v02 * v11
    c11 = v00 * v22 - v02 * v02
    c12 = v01 * v02 - v00 * v12
    c22 = v00 * v11 - v01 * v01
    scale = 1.0 / (v00 * c00 + v01 * c01 + v02 * c02)
    cofactors = jnp.concatenate(
        [c00, c01, c02, c11, c12, c22, jnp.zeros((2, P_DEV), F32)], 0
    )
    vinv = cofactors * scale
    vinv_out[...] = vinv
    gres_out[...] = g
    s = jnp.concatenate(solve_points(vinv, g), 0)
    back = folded(pick(stacked(s), hot_p))
    rem = [r[i] - jnp.sum(p[i] * back, 0, keepdims=True) for i in range(2)]
    tiles = []
    for d in range(5):
        other = [x if d == 0 else pltpu.roll(x, d, 0) for x in a]
        tiles.append(a[0] * other[0] + a[1] * other[1])
    tiles.append(a[0] * last[0] + a[1] * last[1])
    tiles.append(a[0] * rem[0] + a[1] * rem[1])
    corner = last[0] * last[0] + last[1] * last[1]
    end = last[0] * rem[0] + last[1] * rem[1]
    tiles.append(jnp.where(row == 0, corner, jnp.where(row == 1, end, 0.0)))
    terms = stacked(jnp.concatenate(tiles, 0))
    hot_c = onehot_of(low)
    for k in range(3):
        mask = jnp.where(block == k, 1.0, 0.0).astype(BF16)
        part[k] = folded(put(terms * mask, hot_c))


def factor_kernel(mid, mid_other, got, got_other, factor, v, scal):
    sums = (mid[...] + mid_other[...]) + (got[...] + got_other[...])

    def entry(i, j):
        if i == 8 and j == 8:
            k = 56
        elif i == 8:
            k = 40 + j
        elif i - j <= 4:
            k = 8 * (i - j) + i
        else:
            k = 8 * (8 - (i - j)) + j
        x = sums[k : k + 1]
        return x + DAMPING if i == j else x

    b = [-sums[48 + k : 49 + k] for k in range(8)] + [-sums[57:58]]
    low = [[None] * 9 for _ in range(9)]
    work = [[entry(i, j) if j <= i else None for j in range(9)] for i in range(9)]
    inv = []
    for k in range(9):
        inv.append(1.0 / jnp.sqrt(work[k][k]))
        for i in range(k + 1, 9):
            low[i][k] = work[i][k] * inv[k]
        for i in range(k + 1, 9):
            for j in range(k + 1, i + 1):
                work[i][j] = work[i][j] - low[i][k] * low[j][k]
    rows = [low[i][j] for i in range(9) for j in range(i)] + inv
    rows.append(jnp.zeros((3, WIDE), F32))
    factor[...] = jnp.concatenate(rows, 0)
    x = solve_camera(low, inv, b)
    v[...] = jnp.concatenate(x + [jnp.zeros((7, WIDE), F32)], 0)
    dots = functools.reduce(lambda p, q: p + q, [b[k] * x[k] for k in range(9)])
    scal[...] = jnp.broadcast_to(0.5 * per_lane(dots), (8, 128))


def solve_camera(low, inv, b):
    y = list(b)
    for k in range(9):
        y[k] = y[k] * inv[k]
        for i in range(k + 1, 9):
            y[i] = y[i] - low[i][k] * y[k]
    for k in range(8, -1, -1):
        y[k] = y[k] * inv[k]
        for i in range(k):
            y[i] = y[i] - low[k][i] * y[k]
    return y


def solve_kernel(mid, mid_other, got, got_other, factor, v):
    sums = (mid[...] + mid_other[...]) + (got[...] + got_other[...])
    low = [[None] * 9 for _ in range(9)]
    at = 0
    for i in range(9):
        for j in range(i):
            low[i][j] = factor[at : at + 1, :]
            at += 1
    inv = [factor[at + k : at + k + 1, :] for k in range(9)]
    x = solve_camera(low, inv, [sums[k : k + 1] for k in range(9)])
    v[...] = jnp.concatenate(x + [jnp.zeros((7, WIDE), F32)], 0)


def apply_body(grp, v, got, got_other, index, jx, px, vinv):
    low, block, slot = index[0:1, :], index[1:2, :], index[2:3, :]
    hot_c = onehot_of(low)
    hot_p = onehot_of(slot)
    first = grp[0] == 0
    here = v[...]
    up = jnp.where(first, got[...], got_other[...])
    down = jnp.where(first, got_other[...], got[...])
    fields = jnp.concatenate([stacked(x) for x in (down, here, up)], 0)
    picked = pick(fields, hot_c)
    blocks = [folded(picked[48 * k : 48 * k + 48]) for k in range(3)]
    field = jnp.where(block == 0, blocks[0], jnp.where(block == 1, blocks[1], blocks[2]))
    u = [jnp.sum(jx[i] * field, 0, keepdims=True) for i in range(2)]
    p = [px[0], px[1]]
    g, s, ps = point_part(u, p, hot_p, vinv[...])
    return block, hot_c, u, g, s, ps


def apply_kernel(
    grp, v, got, got_other, index, jx, px, vinv, v_old, s_old, rem_old,
    part, g_out, s_out, rem_out, scal,
):
    block, hot_c, u, g, s, ps = apply_body(grp, v, got, got_other, index, jx, px, vinv)
    rem = [u[i] - ps[i] for i in range(2)]
    g_out[...] = g
    s_out[...] = s
    rem_out[...] = jnp.concatenate(rem + [jnp.zeros((6, OBS), F32)], 0)
    terms = stacked(jx[0] * ps[0] + jx[1] * ps[1])
    lhs = jnp.concatenate(
        [terms * jnp.where(block == k, 1.0, 0.0).astype(BF16) for k in range(3)], 0
    )
    out = put(lhs, hot_c)
    for k in range(3):
        part[k] = folded(out[48 * k : 48 * k + 48])
    scal[...] = scalars(v[...], v_old[...], u, rem, rem_old, g, s, s_old[...])


def scalars(v, v_old, u, rem, rem_old, g, s, s_old):
    half = 0.5 * DAMPING
    rows = [
        half * per_lane(v * v_old) + per_lane(u[0] * rem_old[0:1, :] + u[1] * rem_old[1:2, :]),
        half * per_lane(v * v) + per_lane(u[0] * rem[0] + u[1] * rem[1]),
        per_lane(g * s_old),
        per_lane(g * s),
        jnp.zeros((4, 128), F32),
    ]
    return jnp.concatenate(rows, 0)


def last_apply_kernel(
    grp, v, got, got_other, index, jx, px, vinv, v_old, s_old, rem_old, scal0, scal1, scal2,
    g_out, send,
):
    block, hot_c, u, g, s, ps = apply_body(grp, v, got, got_other, index, jx, px, vinv)
    rem = [u[i] - ps[i] for i in range(2)]
    g_out[...] = g
    scal3 = scalars(v[...], v_old[...], u, rem, rem_old, g, s, s_old[...])
    rows = jnp.concatenate([scal0[...], scal1[...], scal2[...], scal3], 0)
    ones = jnp.ones((128, 128), BF16)
    high, middle, low = three_parts(rows)
    send[...] = put(ones, high) + put(ones, middle) + put(ones, low)


def final_kernel(grp, back, v0, v1, v2, g0, g1, g2, gres, vinv, cam, pnt):
    sums = jnp.sum(back[...], 0, keepdims=True)

    def value(k):
        return sums[:, k : k + 1]

    m = [value(0), value(11), value(18), value(19), value(26)]
    s = [value(9), value(16), value(17), value(24), value(25)]

    def form(h, x):
        out = None
        for i in range(3):
            for j in range(3):
                term = x[i] * x[j] * h[i + j]
                out = term if out is None else out + term
        return out

    def ratio(x, y):
        return jnp.where(y > 0, x / jnp.where(y > 0, y, 1.0), 0.0)

    one, zero = jnp.ones((1, 1), F32), jnp.zeros((1, 1), F32)
    y = [zero, zero, zero]
    z = [one, zero, zero]
    d = list(z)
    current = m[0]
    for turn in range(3):
        step = ratio(current, form(s, d))
        y = [y[k] + step * d[k] for k in range(3)]
        if turn < 2:
            image = [d[0], d[1] - d[0], d[2] - d[1]]
            z = [z[k] - step * image[k] for k in range(3)]
            following = form(m, z)
            beta = ratio(following, current)
            d = [z[k] + beta * d[k] for k in range(3)]
            current = following
    x = y[0] * v0[...] + y[1] * v1[...] + y[2] * v2[...]
    cam[...] = jnp.where(grp[0] == 0, x[0:9, 0:C_DEV], x[0:9, C_DEV:WIDE])
    g = gres[...] + (y[0] * g0[...] + y[1] * g1[...] + y[2] * g2[...])
    rows = solve_points(vinv[...], g)
    for k in range(3):
        pnt[k : k + 1, :] = -rows[k]


def shape(*dims, dtype=F32):
    return jax.ShapeDtypeStruct(dims, dtype)


def call(kernel, outs, *args, scalar=False):
    specs = [VMEM] * len(args)
    if scalar:
        specs[0] = SMEM
    many = isinstance(outs, (tuple, list))
    return pl.pallas_call(
        kernel,
        out_shape=outs,
        in_specs=specs,
        out_specs=[VMEM] * len(outs) if many else VMEM,
        name=kernel.__name__,
    )(*args)


def local(regions, cam_jacobian, point_jacobian, residuals, obs_camera, obs_point):
    region = lax.axis_index(REG)
    group = lax.axis_index("grp")
    grp = group.reshape(1).astype(jnp.int32)
    owners = obs_camera // C_DEV
    low = owners // regions * C_DEV + obs_camera % C_DEV
    block = owners % regions - region + 1
    index = jnp.stack([low, block, obs_point] + [jnp.zeros_like(low)] * 5)

    partner = [(g * regions + r, (1 - g) * regions + r) for g in range(2) for r in range(regions)]
    up = [(r, regions + r + 1) for r in range(regions - 1)]
    cross = up + [(b, a) for a, b in up]

    def other(x):
        return lax.ppermute(x, GRP_REG, partner)

    def across(x):
        return lax.ppermute(x, GRP_REG, cross)

    def to_owner(part):
        theirs = other(part)
        outgoing = jnp.where(group == 0, part[2] + theirs[2], part[0] + theirs[0])
        got = across(outgoing)
        return part[1], theirs[1], got, other(got)

    def spread(v):
        got = across(v)
        return got, other(got)

    rows = 64
    part, jx, px, vinv, gres = call(
        first_kernel,
        [shape(3, rows, WIDE), shape(2, 16, OBS), shape(2, 8, OBS), shape(8, P_DEV), shape(8, P_DEV)],
        cam_jacobian, point_jacobian, residuals, index,
    )
    factor, v0, scal0 = call(
        factor_kernel, [shape(48, WIDE), shape(16, WIDE), shape(8, 128)], *to_owner(part)
    )
    outs = [shape(3, 16, WIDE), shape(8, P_DEV), shape(8, P_DEV), shape(8, OBS), shape(8, 128)]
    common = (index, jx, px, vinv)
    part, g0, s0, rem0, scal1 = call(
        apply_kernel, outs, grp, v0, *spread(v0), *common, v0, gres, residuals, scalar=True
    )
    v1 = call(solve_kernel, shape(16, WIDE), *to_owner(part), factor)
    part, g1, s1, rem1, scal2 = call(
        apply_kernel, outs, grp, v1, *spread(v1), *common, v0, s0, rem0, scalar=True
    )
    v2 = call(solve_kernel, shape(16, WIDE), *to_owner(part), factor)
    g2, send = call(
        last_apply_kernel,
        [shape(8, P_DEV), shape(128, 32)],
        grp, v2, *spread(v2), *common, v1, s1, rem1, scal0, scal1, scal2, scalar=True,
    )
    back = lax.all_to_all(send, GRP_REG, 0, 0, tiled=True)
    cam, pnt = call(
        final_kernel,
        [shape(9, C_DEV), shape(3, P_DEV)],
        grp, back, v0, v1, v2, g0, g1, g2, gres, vinv, scalar=True,
    )
    return cam, pnt


def solution(mesh):
    torus = Mesh(
        mesh.devices.reshape(mesh.shape["grp"], 4, 4, 4), ("grp", "reg_0", "reg_1", "reg_2")
    )
    return jax.shard_map(
        functools.partial(local, mesh.shape["reg"]),
        mesh=torus,
        in_specs=(P(None, GRP_REG), P(None, GRP_REG), P(None, GRP_REG), P(GRP_REG), P(GRP_REG)),
        out_specs=(P(None, GRP_REG), P(None, GRP_REG)),
        check_vma=False,
    )
```

```python
import functools

import jax
import jax.numpy as jnp
from jax import lax
from jax.experimental import pallas as pl
from jax.experimental.pallas import tpu as pltpu
from jax.sharding import Mesh
from jax.sharding import PartitionSpec as P

C_DEV = 128
P_DEV = 256
OBS = 2048
DAMPING = 4.0
WIDE = 2 * C_DEV
REG = ("reg_0", "reg_1", "reg_2")
GRP_REG = ("grp", "reg_0", "reg_1", "reg_2")
F32 = jnp.float32
BF16 = jnp.bfloat16
VMEM = pl.BlockSpec(memory_space=pltpu.VMEM)
SMEM = pl.BlockSpec(memory_space=pltpu.SMEM)
ROWS = 56
VMEM_LIMIT = 32 * 1024 * 1024


def three_parts(x):
    high = x.astype(BF16)
    rest = x - high.astype(F32)
    middle = rest.astype(BF16)
    low = (rest - middle.astype(F32)).astype(BF16)
    return high, middle, low


def stacked(x):
    high, middle, low = three_parts(x)
    parts = [high.astype(F32), middle.astype(F32), low.astype(F32)]
    return jnp.concatenate(parts, 0).astype(BF16)


def folded(x):
    rows = x.shape[0] // 3
    return x[:rows] + x[rows : 2 * rows] + x[2 * rows :]


def pick(field, onehot):
    return lax.dot_general(
        field, onehot, (((1,), (0,)), ((), ())), preferred_element_type=F32
    )


def put(terms, onehot):
    return lax.dot_general(
        terms, onehot, (((1,), (1,)), ((), ())), preferred_element_type=F32
    )


def onehot_of(index):
    ids = lax.broadcasted_iota(jnp.int32, (WIDE, index.shape[1]), 0)
    return jnp.where(ids == index, 1.0, 0.0).astype(BF16)


def total(x):
    return jnp.sum(jnp.sum(x, 0, keepdims=True), 1, keepdims=True)


def per_lane(x):
    row = jnp.sum(x, 0, keepdims=True)
    return functools.reduce(
        lambda a, b: a + b, [row[:, k : k + 128] for k in range(0, row.shape[1], 128)]
    )


def solve_points(vinv, g):
    a, b, c, d, e, f = [vinv[k : k + 1] for k in range(6)]
    x, y, z = [g[k : k + 1] for k in range(3)]
    rows = [a * x + b * y + c * z, b * x + d * y + e * z, c * x + e * y + f * z]
    return rows + [jnp.zeros((8 - 3, g.shape[1]), F32)]


def point_part(u, p, hot_p, vinv):
    g = folded(put(stacked(p[0] * u[0] + p[1] * u[1]), hot_p))
    s = jnp.concatenate(solve_points(vinv, g), 0)
    back = folded(pick(stacked(s), hot_p))
    return g, s, [jnp.sum(p[i] * back, 0, keepdims=True) for i in range(2)]


def position(where, regions):
    device = where[0]
    region = device & (regions - 1)
    return device >> (regions.bit_length() - 1), region, region & 1


def indices(regions, region, camera, slot):
    owners = camera[...] >> (C_DEV.bit_length() - 1)
    low = ((owners >> (regions.bit_length() - 1)) * C_DEV) | (camera[...] & (C_DEV - 1))
    return low, (owners & (regions - 1)) - region + 1, slot[...]


def split_frames(group, odd, blocks, keep, send):
    even = odd == 0
    zero = jnp.zeros_like(blocks[0])
    frames = [
        jnp.where(even, blocks[0], zero),
        jnp.where(even, blocks[1], blocks[0]),
        jnp.where(even, blocks[2], blocks[1]),
        jnp.where(even, zero, blocks[2]),
    ]
    first = group == 0
    for k in range(2):
        keep[k] = jnp.where(first, frames[2 + k], frames[k])
        send[k] = jnp.where(first, frames[k], frames[2 + k])


def to_tiles(tiles, group, here, there):
    first = group == 0
    rows = here.shape[1]
    for k in range(2):
        mine, other = here[k], there[k]
        lower = jnp.where(first, other, mine)
        upper = jnp.where(first, mine, other)
        for h in range(2):
            lanes = slice(128 * h, 128 * h + 128)
            tiles[pl.ds(2 * k + h, rows, stride=8), :] = lower[:, lanes]
            tiles[pl.ds(4 + 2 * k + h, rows, stride=8), :] = upper[:, lanes]


def tile(tiles, k):
    return tiles[8 * k : 8 * k + 8, :]


def first_kernel(
    regions, where, cam, pnt, res, camera, points, keep, send, jx, px, vinv_out, gres_out
):
    group, region, odd = position(where, regions)
    low, block, slot = indices(regions, region, camera, points)
    hot_p = onehot_of(slot)
    camf = cam[...].astype(F32)
    pf = pnt[...].astype(F32)
    zero5 = jnp.zeros((5, OBS), F32)
    zero7 = jnp.zeros((7, OBS), F32)
    for i in range(2):
        jx[i, 0:8, :] = camf[9 * i : 9 * i + 8]
        jx[i, 8:16, :] = jnp.concatenate([camf[9 * i + 8 : 9 * i + 9], zero7], 0)
        px[i] = jnp.concatenate([pf[3 * i : 3 * i + 3], zero5], 0)
    p = [px[0], px[1]]
    a = [jx[0, 0:8, :], jx[1, 0:8, :]]
    last = [jx[0, 8:9, :], jx[1, 8:9, :]]
    r = [res[0:1, :], res[1:2, :]]
    row = lax.broadcasted_iota(jnp.int32, (8, OBS), 0)
    squares = p[0] * p[0] + p[1] * p[1]
    turned = [
        jnp.where(row == 2, jnp.broadcast_to(x[0:1], x.shape), pltpu.roll(x, 7, 0)) for x in p
    ]
    products = p[0] * turned[0] + p[1] * turned[1]
    right = p[0] * r[0] + p[1] * r[1]
    sums = folded(put(stacked(jnp.concatenate([squares, products, right], 0)), hot_p))
    v00, v11, v22 = [sums[k : k + 1] + DAMPING for k in range(3)]
    v01, v12, v02 = [sums[8 + k : 9 + k] for k in range(3)]
    g = sums[16:24]
    c00 = v11 * v22 - v12 * v12
    c01 = v02 * v12 - v01 * v22
    c02 = v01 * v12 - v02 * v11
    c11 = v00 * v22 - v02 * v02
    c12 = v01 * v02 - v00 * v12
    c22 = v00 * v11 - v01 * v01
    scale = 1.0 / (v00 * c00 + v01 * c01 + v02 * c02)
    cofactors = jnp.concatenate(
        [c00, c01, c02, c11, c12, c22, jnp.zeros((2, P_DEV), F32)], 0
    )
    vinv = cofactors * scale
    vinv_out[...] = vinv
    gres_out[...] = g
    s = jnp.concatenate(solve_points(vinv, g), 0)
    back = folded(pick(stacked(s), hot_p))
    rem = [r[i] - jnp.sum(p[i] * back, 0, keepdims=True) for i in range(2)]
    rolled = []
    for d in range(5):
        other = [x if d == 0 else pltpu.roll(x, d, 0) for x in a]
        rolled.append(a[0] * other[0] + a[1] * other[1])
    corner = last[0] * last[0] + last[1] * last[1]
    end = last[0] * rem[0] + last[1] * rem[1]
    rolled[4] = jnp.where(row < 4, rolled[4], jnp.where(row == 4, corner, end))
    edge = a[0] * last[0] + a[1] * last[1]
    gradient = a[0] * rem[0] + a[1] * rem[1]
    terms = stacked(jnp.concatenate(rolled + [edge, gradient], 0))
    hot_c = onehot_of(low)
    blocks = []
    for k in range(3):
        mask = jnp.where(block == k, 1.0, 0.0).astype(BF16)
        blocks.append(folded(put(terms * mask, hot_c)))
    split_frames(group, odd, blocks, keep, send)


def solve_camera(low, inv, b):
    y = list(b)
    for k in range(9):
        y[k] = y[k] * inv[k]
        for i in range(k + 1, 9):
            y[i] = y[i] - low[i][k] * y[k]
    for k in range(8, -1, -1):
        y[k] = y[k] * inv[k]
        for i in range(k):
            y[i] = y[i] - low[k][i] * y[k]
    return y


def factor_camera(tiles, factor):
    def entry(i, j):
        if i == 8:
            k = 36 if j == 8 else 40 + j
        elif i - j < 4:
            k = 8 * (i - j) + i
        elif i - j == 4:
            k = 32 + j
        else:
            k = 8 * (8 - (i - j)) + j
        x = tile(tiles, k)
        return x + DAMPING if i == j else x

    low = [[None] * 9 for _ in range(9)]
    work = [[entry(i, j) if j <= i else None for j in range(9)] for i in range(9)]
    inv = []
    for k in range(9):
        inv.append(1.0 / jnp.sqrt(work[k][k]))
        for i in range(k + 1, 9):
            low[i][k] = work[i][k] * inv[k]
        for i in range(k + 1, 9):
            for j in range(k + 1, i + 1):
                work[i][j] = work[i][j] - low[i][k] * low[j][k]
    flat = [low[i][j] for i in range(9) for j in range(i)] + inv
    for k, x in enumerate(flat):
        factor[8 * k : 8 * k + 8, :] = x
    return low, inv


def read_factor(factor):
    low = [[None] * 9 for _ in range(9)]
    at = 0
    for i in range(9):
        for j in range(i):
            low[i][j] = tile(factor, at)
            at += 1
    return low, [tile(factor, at + k) for k in range(9)]


def apply_body(group, odd, x, field, low, block, slot, jx, px, vinv):
    hot_c = onehot_of(low)
    hot_p = onehot_of(slot)
    for k in range(9):
        field[8 * k : 8 * k + 8, :] = x[k]
    for k in range(9, 16):
        field[8 * k : 8 * k + 8, :] = jnp.zeros((8, 128), F32)
    frames = [
        jnp.concatenate([field[pl.ds(2 * f + h, 16, stride=8), :] for h in range(2)], 1)
        for f in range(4)
    ]
    seen = [jnp.where(odd == 0, frames[k], frames[k + 1]) for k in range(3)]
    v = jnp.where(group == 0, seen[1][:, 0:128], seen[1][:, 128:256])
    picked = pick(jnp.concatenate([stacked(f) for f in seen], 0), hot_c)
    blocks = [folded(picked[48 * k : 48 * k + 48]) for k in range(3)]
    values = jnp.where(block == 0, blocks[0], jnp.where(block == 1, blocks[1], blocks[2]))
    u = [jnp.sum(jx[i] * values, 0, keepdims=True) for i in range(2)]
    p = [px[0], px[1]]
    g, s, ps = point_part(u, p, hot_p, vinv[...])
    return hot_c, v, u, g, s, ps


def finish(group, odd, hot_c, block, jx, ps, keep, send):
    terms = stacked(jx[0] * ps[0] + jx[1] * ps[1])
    lhs = jnp.concatenate(
        [terms * jnp.where(block == k, 1.0, 0.0).astype(BF16) for k in range(3)], 0
    )
    out = put(lhs, hot_c)
    split_frames(
        group, odd, [folded(out[48 * k : 48 * k + 48]) for k in range(3)], keep, send
    )


def scalar_rows(pairs):
    rows = [functools.reduce(lambda a, b: a + b, [per_lane(x) for x in pair]) for pair in pairs]
    return jnp.concatenate(rows + [jnp.zeros((8 - len(rows), 128), F32)], 0)


def scalars(v, v_old, u, rem, rem_old, g, s, s_old):
    return scalar_rows(
        [
            (DAMPING * v * v_old, u[0] * rem_old[0:1, :] + u[1] * rem_old[1:2, :]),
            (DAMPING * v * v, u[0] * rem[0] + u[1] * rem[1]),
            (g * s_old,),
            (g * s,),
        ]
    )


def start_kernel(
    regions, where, here, there, camera, points, jx, px, vinv,
    keep, send, factor, v_out, g_out, s_out, rem_out, scal, tiles, field,
):
    group, region, odd = position(where, regions)
    low, block, slot = indices(regions, region, camera, points)
    to_tiles(tiles, group, here, there)
    lower, inv = factor_camera(tiles, factor)
    b = [-tile(tiles, 48 + k) for k in range(8)] + [-tile(tiles, 37)]
    x = solve_camera(lower, inv, b)
    dots = functools.reduce(lambda p, q: p + q, [b[k] * x[k] for k in range(9)])
    own = lax.broadcasted_iota(jnp.int32, (8, 128), 0) == 2 * (1 + odd) + group
    hot_c, v, u, g, s, ps = apply_body(
        group, odd, x, field, low, block, slot, jx, px, vinv
    )
    rem = [u[i] - ps[i] for i in range(2)]
    v_out[...], g_out[...], s_out[...] = v, g, s
    rem_out[...] = jnp.concatenate(rem + [jnp.zeros((6, OBS), F32)], 0)
    finish(group, odd, hot_c, block, jx, ps, keep, send)
    scal[...] = scalar_rows(
        [
            (jnp.where(own, dots, 0.0),),
            (DAMPING * v * v, u[0] * rem[0] + u[1] * rem[1]),
            (g * s,),
        ]
    )


def next_kernel(
    regions, where, here, there, factor, camera, points, jx, px, vinv, v_old, s_old, rem_old,
    keep, send, v_out, g_out, s_out, rem_out, scal, tiles, field,
):
    group, region, odd = position(where, regions)
    low, block, slot = indices(regions, region, camera, points)
    to_tiles(tiles, group, here, there)
    x = solve_camera(*read_factor(factor), [tile(tiles, k) for k in range(9)])
    hot_c, v, u, g, s, ps = apply_body(
        group, odd, x, field, low, block, slot, jx, px, vinv
    )
    rem = [u[i] - ps[i] for i in range(2)]
    v_out[...], g_out[...], s_out[...] = v, g, s
    rem_out[...] = jnp.concatenate(rem + [jnp.zeros((6, OBS), F32)], 0)
    finish(group, odd, hot_c, block, jx, ps, keep, send)
    scal[...] = scalars(v, v_old[...], u, rem, rem_old, g, s, s_old[...])


def last_kernel(
    regions, where, here, there, factor, camera, points, jx, px, vinv, v_old, s_old, rem_old,
    scal0, scal1, v_out, g_out, sums, tiles, field,
):
    group, region, odd = position(where, regions)
    low, block, slot = indices(regions, region, camera, points)
    to_tiles(tiles, group, here, there)
    x = solve_camera(*read_factor(factor), [tile(tiles, k) for k in range(9)])
    hot_c, v, u, g, s, ps = apply_body(
        group, odd, x, field, low, block, slot, jx, px, vinv
    )
    rem = [u[i] - ps[i] for i in range(2)]
    v_out[...], g_out[...] = v, g
    scal2 = scalars(v, v_old[...], u, rem, rem_old, g, s, s_old[...])
    rows = jnp.concatenate([scal0[...], scal1[...], scal2, jnp.zeros((8, 128), F32)], 0)
    ones = jnp.ones((128, 128), BF16)
    high, middle, low_part = three_parts(rows)
    sums[...] = put(ones, high) + put(ones, middle) + put(ones, low_part)


def final_kernel(back, v0, v1, v2, g0, g1, g2, gres, vinv, cam, pnt):
    sums = jnp.sum(back[...], 0, keepdims=True)

    def value(k):
        return sums[:, k : k + 1]

    m = [value(k) for k in (0, 2, 10, 11, 18)]
    s = [value(k) for k in (1, 8, 9, 16, 17)]

    def form(h, x):
        terms = [x[i] * x[j] * h[i + j] for i in range(3) for j in range(3)]
        return functools.reduce(lambda p, q: p + q, terms)

    def ratio(x, y):
        return jnp.where(y > 0, x / jnp.where(y > 0, y, 1.0), 0.0)

    one, zero = jnp.ones((1, 1), F32), jnp.zeros((1, 1), F32)
    y = [zero, zero, zero]
    z = [one, zero, zero]
    d = list(z)
    current = m[0]
    for turn in range(3):
        step = ratio(current, form(s, d))
        y = [y[k] + step * d[k] for k in range(3)]
        if turn < 2:
            image = [d[0], d[1] - d[0], d[2] - d[1]]
            z = [z[k] - step * image[k] for k in range(3)]
            following = form(m, z)
            beta = ratio(following, current)
            d = [z[k] + beta * d[k] for k in range(3)]
            current = following
    x = y[0] * v0[...] + y[1] * v1[...] + y[2] * v2[...]
    cam[...] = x[0:9]
    g = gres[...] + (y[0] * g0[...] + y[1] * g1[...] + y[2] * g2[...])
    rows = solve_points(vinv[...], g)
    for k in range(3):
        pnt[k : k + 1, :] = -rows[k]


def shape(*dims, dtype=F32):
    return jax.ShapeDtypeStruct(dims, dtype)


def call(kernel, outs, *args, scalar=False, scratch=(), regions=None):
    specs = [VMEM] * len(args)
    if scalar:
        specs[0] = SMEM
    return pl.pallas_call(
        kernel if regions is None else functools.partial(kernel, regions),
        out_shape=outs,
        in_specs=specs,
        out_specs=[VMEM] * len(outs),
        scratch_shapes=scratch,
        compiler_params=pltpu.CompilerParams(vmem_limit_bytes=VMEM_LIMIT),
        name=kernel.__name__,
    )(*args)


def local(regions, cam_jacobian, point_jacobian, residuals, obs_camera, obs_point):
    where = (lax.axis_index("grp") * regions + lax.axis_index(REG)).reshape(1)
    camera, points = obs_camera.reshape(1, OBS), obs_point.reshape(1, OBS)

    def both_ways(pairs):
        return pairs + [(b, a) for a, b in pairs]

    cores = both_ways([(r, regions + r) for r in range(regions)])
    pair = both_ways(
        [(g * regions + r, g * regions + r + 1) for g in range(2) for r in range(0, regions, 2)]
    )
    next_pair = both_ways(
        [(r + i, regions + r + 3 - i) for r in range(0, regions - 2, 2) for i in range(2)]
    )

    def swap(x, pairs):
        return lax.ppermute(x, GRP_REG, pairs)

    def totals(keep, send):
        half = keep + swap(send, cores)
        half = half + swap(half, pair)
        half = half + swap(half, next_pair)
        return half, swap(half, cores)

    def halves(rows):
        return [shape(2, rows, WIDE)] * 2

    run = functools.partial(call, scalar=True, regions=regions)
    field = pltpu.VMEM((128, 128), F32)
    per_point = shape(8, P_DEV)
    rest = [shape(16, 128), per_point, per_point, shape(8, OBS), shape(8, 128)]

    keep, send, jx, px, vinv, gres = run(
        first_kernel,
        halves(ROWS) + [shape(2, 16, OBS), shape(2, 8, OBS), per_point, per_point],
        where, cam_jacobian, point_jacobian, residuals, camera, points,
    )
    common = (camera, points, jx, px, vinv)
    keep, send, factor, v0, g0, s0, rem0, scal0 = run(
        start_kernel,
        halves(16) + [shape(45 * 8, 128)] + rest,
        where, *totals(keep, send), *common,
        scratch=[pltpu.VMEM((8 * ROWS, 128), F32), field],
    )
    keep, send, v1, g1, s1, rem1, scal1 = run(
        next_kernel,
        halves(16) + rest,
        where, *totals(keep, send), factor, *common, v0, s0, rem0,
        scratch=[field, field],
    )
    v2, g2, sums = run(
        last_kernel,
        [shape(16, 128), per_point, shape(128, 32)],
        where, *totals(keep, send), factor, *common, v1, s1, rem1, scal0, scal1,
        scratch=[field, field],
    )
    back = lax.all_to_all(sums, GRP_REG, 0, 0, tiled=True)
    return call(
        final_kernel,
        [shape(9, C_DEV), shape(3, P_DEV)],
        back, v0, v1, v2, g0, g1, g2, gres, vinv,
    )


def solution(mesh):
    torus = Mesh(
        mesh.devices.reshape(mesh.shape["grp"], 4, 4, 4), ("grp", "reg_0", "reg_1", "reg_2")
    )
    return jax.shard_map(
        functools.partial(local, mesh.shape["reg"]),
        mesh=torus,
        in_specs=(P(None, GRP_REG), P(None, GRP_REG), P(None, GRP_REG), P(GRP_REG), P(GRP_REG)),
        out_specs=(P(None, GRP_REG), P(None, GRP_REG)),
        check_vma=False,
    )
```

```python
import functools

import jax
import jax.numpy as jnp
from jax import lax
from jax.experimental import pallas as pl
from jax.experimental.pallas import tpu as pltpu
from jax.sharding import Mesh
from jax.sharding import PartitionSpec as P

C_DEV = 128
P_DEV = 256
OBS = 2048
DAMPING = 4.0
WIDE = 2 * C_DEV
REG = ("reg_0", "reg_1", "reg_2")
GRP_REG = ("grp", "reg_0", "reg_1", "reg_2")
F32 = jnp.float32
BF16 = jnp.bfloat16
VMEM = pl.BlockSpec(memory_space=pltpu.VMEM)
HBM = pl.BlockSpec(memory_space=pltpu.HBM)
SMEM = pl.BlockSpec(memory_space=pltpu.SMEM)
ROWS = 56
VMEM_LIMIT = 32 * 1024 * 1024


def three_parts(x):
    high = x.astype(BF16)
    rest = x - high.astype(F32)
    middle = rest.astype(BF16)
    low = (rest - middle.astype(F32)).astype(BF16)
    return high, middle, low


def stacked(x):
    high, middle, low = three_parts(x)
    parts = [high.astype(F32), middle.astype(F32), low.astype(F32)]
    return jnp.concatenate(parts, 0).astype(BF16)


def folded(x):
    rows = x.shape[0] // 3
    return x[:rows] + x[rows : 2 * rows] + x[2 * rows :]


def pick(field, onehot):
    return lax.dot_general(
        field, onehot, (((1,), (0,)), ((), ())), preferred_element_type=F32
    )


def put(terms, onehot):
    return lax.dot_general(
        terms, onehot, (((1,), (1,)), ((), ())), preferred_element_type=F32
    )


def onehot_of(index):
    ids = lax.broadcasted_iota(jnp.int32, (WIDE, index.shape[1]), 0)
    return jnp.where(ids == index, 1.0, 0.0).astype(BF16)


def total(x):
    return jnp.sum(jnp.sum(x, 0, keepdims=True), 1, keepdims=True)


def per_lane(x):
    row = jnp.sum(x, 0, keepdims=True)
    return functools.reduce(
        lambda a, b: a + b, [row[:, k : k + 128] for k in range(0, row.shape[1], 128)]
    )


def solve_points(vinv, g):
    a, b, c, d, e, f = [vinv[k : k + 1] for k in range(6)]
    x, y, z = [g[k : k + 1] for k in range(3)]
    rows = [a * x + b * y + c * z, b * x + d * y + e * z, c * x + e * y + f * z]
    return rows + [jnp.zeros((8 - 3, g.shape[1]), F32)]


def point_part(u, p, hot_p, vinv):
    g = folded(put(stacked(p[0] * u[0] + p[1] * u[1]), hot_p))
    s = jnp.concatenate(solve_points(vinv, g), 0)
    back = folded(pick(stacked(s), hot_p))
    return g, s, [jnp.sum(p[i] * back, 0, keepdims=True) for i in range(2)]


def position(where, regions):
    device = where[0]
    region = device & (regions - 1)
    return device >> (regions.bit_length() - 1), region, region & 1


def indices(regions, region, camera):
    owners = camera >> (C_DEV.bit_length() - 1)
    low = ((owners >> (regions.bit_length() - 1)) * C_DEV) | (camera & (C_DEV - 1))
    return low, (owners & (regions - 1)) - region + 1


def split_frames(group, odd, blocks, keep, send):
    even = odd == 0
    zero = jnp.zeros_like(blocks[0])
    frames = [
        jnp.where(even, blocks[0], zero),
        jnp.where(even, blocks[1], blocks[0]),
        jnp.where(even, blocks[2], blocks[1]),
        jnp.where(even, zero, blocks[2]),
    ]
    first = group == odd
    for k in range(2):
        keep[k] = jnp.where(first, frames[2 + k], frames[k])
        send[k] = jnp.where(first, frames[k], frames[2 + k])


def to_tiles(tiles, group, odd, here, there):
    first = group == odd
    rows = here.shape[1]
    for k in range(2):
        mine, other = here[k], there[k]
        lower = jnp.where(first, other, mine)
        upper = jnp.where(first, mine, other)
        for h in range(2):
            lanes = slice(128 * h, 128 * h + 128)
            tiles[pl.ds(2 * k + h, rows, stride=8), :] = lower[:, lanes]
            tiles[pl.ds(4 + 2 * k + h, rows, stride=8), :] = upper[:, lanes]


def tile(tiles, k):
    return tiles[8 * k : 8 * k + 8, :]


def first_kernel(
    regions, where, cam_hbm, pnt_hbm, res_hbm, camera_hbm, points_hbm,
    keep, send, jx, px, vinv_out, gres_out, index, res, cam, pnt, camera, points, sems,
):
    pairs = [(points_hbm, points), (pnt_hbm, pnt), (res_hbm, res), (camera_hbm, camera), (cam_hbm, cam)]
    copies = [pltpu.make_async_copy(a, b, sems.at[k]) for k, (a, b) in enumerate(pairs)]
    for copy in copies:
        copy.start()
    group, region, odd = position(where, regions)
    copies[0].wait()
    slot = points[...]
    hot_p = onehot_of(slot)
    for copy in copies[1:]:
        copy.wait()
    low, block = indices(regions, region, camera[...])
    index[...] = jnp.concatenate([low, block, slot] + [jnp.zeros_like(low)] * 5, 0)
    camf = cam[...].astype(F32)
    pf = pnt[...].astype(F32)
    zero5 = jnp.zeros((5, OBS), F32)
    zero7 = jnp.zeros((7, OBS), F32)
    for i in range(2):
        jx[i, 0:8, :] = camf[9 * i : 9 * i + 8]
        jx[i, 8:16, :] = jnp.concatenate([camf[9 * i + 8 : 9 * i + 9], zero7], 0)
        px[i] = jnp.concatenate([pf[3 * i : 3 * i + 3], zero5], 0)
    p = [px[0], px[1]]
    a = [jx[0, 0:8, :], jx[1, 0:8, :]]
    last = [jx[0, 8:9, :], jx[1, 8:9, :]]
    r = [res[0:1, :], res[1:2, :]]
    row = lax.broadcasted_iota(jnp.int32, (8, OBS), 0)
    squares = p[0] * p[0] + p[1] * p[1]
    turned = [
        jnp.where(row == 2, jnp.broadcast_to(x[0:1], x.shape), pltpu.roll(x, 7, 0)) for x in p
    ]
    products = p[0] * turned[0] + p[1] * turned[1]
    right = p[0] * r[0] + p[1] * r[1]
    sums = folded(put(stacked(jnp.concatenate([squares, products, right], 0)), hot_p))
    v00, v11, v22 = [sums[k : k + 1] + DAMPING for k in range(3)]
    v01, v12, v02 = [sums[8 + k : 9 + k] for k in range(3)]
    g = sums[16:24]
    c00 = v11 * v22 - v12 * v12
    c01 = v02 * v12 - v01 * v22
    c02 = v01 * v12 - v02 * v11
    c11 = v00 * v22 - v02 * v02
    c12 = v01 * v02 - v00 * v12
    c22 = v00 * v11 - v01 * v01
    scale = 1.0 / (v00 * c00 + v01 * c01 + v02 * c02)
    cofactors = jnp.concatenate(
        [c00, c01, c02, c11, c12, c22, jnp.zeros((2, P_DEV), F32)], 0
    )
    vinv = cofactors * scale
    vinv_out[...] = vinv
    gres_out[...] = g
    s = jnp.concatenate(solve_points(vinv, g), 0)
    back = folded(pick(stacked(s), hot_p))
    rem = [r[i] - jnp.sum(p[i] * back, 0, keepdims=True) for i in range(2)]
    rolled = []
    for d in range(5):
        other = [x if d == 0 else pltpu.roll(x, d, 0) for x in a]
        rolled.append(a[0] * other[0] + a[1] * other[1])
    corner = last[0] * last[0] + last[1] * last[1]
    end = last[0] * rem[0] + last[1] * rem[1]
    rolled[4] = jnp.where(row < 4, rolled[4], jnp.where(row == 4, corner, end))
    edge = a[0] * last[0] + a[1] * last[1]
    gradient = a[0] * rem[0] + a[1] * rem[1]
    terms = stacked(jnp.concatenate(rolled + [edge, gradient], 0))
    hot_c = onehot_of(low)
    blocks = []
    for k in range(3):
        mask = jnp.where(block == k, 1.0, 0.0).astype(BF16)
        blocks.append(folded(put(terms * mask, hot_c)))
    split_frames(group, odd, blocks, keep, send)


def solve_camera(low, inv, b):
    y = list(b)
    for k in range(9):
        y[k] = y[k] * inv[k]
        for i in range(k + 1, 9):
            y[i] = y[i] - low[i][k] * y[k]
    for k in range(8, -1, -1):
        y[k] = y[k] * inv[k]
        for i in range(k):
            y[i] = y[i] - low[k][i] * y[k]
    return y


def factor_camera(tiles, factor):
    def entry(i, j):
        if i == 8:
            k = 36 if j == 8 else 40 + j
        elif i - j < 4:
            k = 8 * (i - j) + i
        elif i - j == 4:
            k = 32 + j
        else:
            k = 8 * (8 - (i - j)) + j
        x = tile(tiles, k)
        return x + DAMPING if i == j else x

    low = [[None] * 9 for _ in range(9)]
    work = [[entry(i, j) if j <= i else None for j in range(9)] for i in range(9)]
    inv = []
    for k in range(9):
        inv.append(1.0 / jnp.sqrt(work[k][k]))
        for i in range(k + 1, 9):
            low[i][k] = work[i][k] * inv[k]
        for i in range(k + 1, 9):
            for j in range(k + 1, i + 1):
                work[i][j] = work[i][j] - low[i][k] * low[j][k]
    flat = [low[i][j] for i in range(9) for j in range(i)] + inv
    for k, x in enumerate(flat):
        factor[8 * k : 8 * k + 8, :] = x
    return low, inv


def read_factor(factor):
    low = [[None] * 9 for _ in range(9)]
    at = 0
    for i in range(9):
        for j in range(i):
            low[i][j] = tile(factor, at)
            at += 1
    return low, [tile(factor, at + k) for k in range(9)]


def apply_body(group, odd, x, field, low, block, slot, jx, px, vinv):
    hot_c = onehot_of(low)
    hot_p = onehot_of(slot)
    for k in range(9):
        field[8 * k : 8 * k + 8, :] = x[k]
    for k in range(9, 16):
        field[8 * k : 8 * k + 8, :] = jnp.zeros((8, 128), F32)
    frames = [
        jnp.concatenate([field[pl.ds(2 * f + h, 16, stride=8), :] for h in range(2)], 1)
        for f in range(4)
    ]
    seen = [jnp.where(odd == 0, frames[k], frames[k + 1]) for k in range(3)]
    v = jnp.where(group == 0, seen[1][:, 0:128], seen[1][:, 128:256])
    picked = pick(jnp.concatenate([stacked(f) for f in seen], 0), hot_c)
    blocks = [folded(picked[48 * k : 48 * k + 48]) for k in range(3)]
    values = jnp.where(block == 0, blocks[0], jnp.where(block == 1, blocks[1], blocks[2]))
    u = [jnp.sum(jx[i] * values, 0, keepdims=True) for i in range(2)]
    p = [px[0], px[1]]
    g, s, ps = point_part(u, p, hot_p, vinv[...])
    return hot_c, v, u, g, s, ps


def finish(group, odd, hot_c, block, jx, ps, keep, send):
    terms = stacked(jx[0] * ps[0] + jx[1] * ps[1])
    lhs = jnp.concatenate(
        [terms * jnp.where(block == k, 1.0, 0.0).astype(BF16) for k in range(3)], 0
    )
    out = put(lhs, hot_c)
    split_frames(
        group, odd, [folded(out[48 * k : 48 * k + 48]) for k in range(3)], keep, send
    )


def scalar_rows(pairs):
    rows = [functools.reduce(lambda a, b: a + b, [per_lane(x) for x in pair]) for pair in pairs]
    return jnp.concatenate(rows + [jnp.zeros((8 - len(rows), 128), F32)], 0)


def scalars(v, v_old, u, rem, rem_old, g, s, s_old):
    return scalar_rows(
        [
            (DAMPING * v * v_old, u[0] * rem_old[0:1, :] + u[1] * rem_old[1:2, :]),
            (DAMPING * v * v, u[0] * rem[0] + u[1] * rem[1]),
            (g * s_old,),
            (g * s,),
        ]
    )


def start_kernel(
    regions, where, here, there, index, jx, px, vinv,
    keep, send, factor, v_out, g_out, s_out, rem_out, scal, tiles, field,
):
    group, region, odd = position(where, regions)
    low, block, slot = index[0:1, :], index[1:2, :], index[2:3, :]
    to_tiles(tiles, group, odd, here, there)
    lower, inv = factor_camera(tiles, factor)
    b = [-tile(tiles, 48 + k) for k in range(8)] + [-tile(tiles, 37)]
    x = solve_camera(lower, inv, b)
    dots = functools.reduce(lambda p, q: p + q, [b[k] * x[k] for k in range(9)])
    own = lax.broadcasted_iota(jnp.int32, (8, 128), 0) == 2 * (1 + odd) + group
    hot_c, v, u, g, s, ps = apply_body(
        group, odd, x, field, low, block, slot, jx, px, vinv
    )
    rem = [u[i] - ps[i] for i in range(2)]
    v_out[...], g_out[...], s_out[...] = v, g, s
    rem_out[...] = jnp.concatenate(rem + [jnp.zeros((6, OBS), F32)], 0)
    finish(group, odd, hot_c, block, jx, ps, keep, send)
    scal[...] = scalar_rows(
        [
            (jnp.where(own, dots, 0.0),),
            (DAMPING * v * v, u[0] * rem[0] + u[1] * rem[1]),
            (g * s,),
        ]
    )


def next_kernel(
    regions, where, here, there, factor, index, jx, px, vinv, v_old, s_old, rem_old,
    keep, send, v_out, g_out, s_out, rem_out, scal, tiles, field,
):
    group, region, odd = position(where, regions)
    low, block, slot = index[0:1, :], index[1:2, :], index[2:3, :]
    to_tiles(tiles, group, odd, here, there)
    x = solve_camera(*read_factor(factor), [tile(tiles, k) for k in range(9)])
    hot_c, v, u, g, s, ps = apply_body(
        group, odd, x, field, low, block, slot, jx, px, vinv
    )
    rem = [u[i] - ps[i] for i in range(2)]
    v_out[...], g_out[...], s_out[...] = v, g, s
    rem_out[...] = jnp.concatenate(rem + [jnp.zeros((6, OBS), F32)], 0)
    finish(group, odd, hot_c, block, jx, ps, keep, send)
    scal[...] = scalars(v, v_old[...], u, rem, rem_old, g, s, s_old[...])


def last_kernel(
    regions, where, here, there, factor, index, jx, px, vinv, v_old, s_old, rem_old,
    scal0, scal1, v_out, g_out, sums, tiles, field,
):
    group, region, odd = position(where, regions)
    low, block, slot = index[0:1, :], index[1:2, :], index[2:3, :]
    to_tiles(tiles, group, odd, here, there)
    x = solve_camera(*read_factor(factor), [tile(tiles, k) for k in range(9)])
    hot_c, v, u, g, s, ps = apply_body(
        group, odd, x, field, low, block, slot, jx, px, vinv
    )
    rem = [u[i] - ps[i] for i in range(2)]
    v_out[...], g_out[...] = v, g
    scal2 = scalars(v, v_old[...], u, rem, rem_old, g, s, s_old[...])
    rows = jnp.concatenate([scal0[...], scal1[...], scal2, jnp.zeros((8, 128), F32)], 0)
    ones = jnp.ones((128, 128), BF16)
    high, middle, low_part = three_parts(rows)
    sums[...] = put(ones, high) + put(ones, middle) + put(ones, low_part)


def final_kernel(back, v0, v1, v2, g0, g1, g2, gres, vinv, cam, pnt):
    sums = jnp.sum(back[...], 0, keepdims=True)

    def value(k):
        return sums[:, k : k + 1]

    m = [value(k) for k in (0, 2, 10, 11, 18)]
    s = [value(k) for k in (1, 8, 9, 16, 17)]

    def form(h, x):
        terms = [x[i] * x[j] * h[i + j] for i in range(3) for j in range(3)]
        return functools.reduce(lambda p, q: p + q, terms)

    def ratio(x, y):
        return jnp.where(y > 0, x / jnp.where(y > 0, y, 1.0), 0.0)

    one, zero = jnp.ones((1, 1), F32), jnp.zeros((1, 1), F32)
    y = [zero, zero, zero]
    z = [one, zero, zero]
    d = list(z)
    current = m[0]
    for turn in range(3):
        step = ratio(current, form(s, d))
        y = [y[k] + step * d[k] for k in range(3)]
        if turn < 2:
            image = [d[0], d[1] - d[0], d[2] - d[1]]
            z = [z[k] - step * image[k] for k in range(3)]
            following = form(m, z)
            beta = ratio(following, current)
            d = [z[k] + beta * d[k] for k in range(3)]
            current = following
    x = y[0] * v0[...] + y[1] * v1[...] + y[2] * v2[...]
    cam[...] = x[0:9]
    g = gres[...] + (y[0] * g0[...] + y[1] * g1[...] + y[2] * g2[...])
    rows = solve_points(vinv[...], g)
    for k in range(3):
        pnt[k : k + 1, :] = -rows[k]


def shape(*dims, dtype=F32):
    return jax.ShapeDtypeStruct(dims, dtype)


def call(kernel, outs, *args, scalar=False, scratch=(), regions=None, inputs=VMEM):
    specs = [inputs] * len(args)
    if scalar:
        specs[0] = SMEM
    return pl.pallas_call(
        kernel if regions is None else functools.partial(kernel, regions),
        out_shape=outs,
        in_specs=specs,
        out_specs=[VMEM] * len(outs),
        scratch_shapes=scratch,
        compiler_params=pltpu.CompilerParams(vmem_limit_bytes=VMEM_LIMIT),
        name=kernel.__name__,
    )(*args)


def local(regions, cam_jacobian, point_jacobian, residuals, obs_camera, obs_point):
    where = (lax.axis_index("grp") * regions + lax.axis_index(REG)).reshape(1)
    camera, points = obs_camera.reshape(1, OBS), obs_point.reshape(1, OBS)

    def both_ways(pairs):
        return pairs + [(b, a) for a, b in pairs]

    def device(left, region):
        return ((region & 1) ^ left) * regions + region

    cores = both_ways([(r, regions + r) for r in range(regions)])
    pair = both_ways(
        [(device(h, r), device(h, r + 1)) for h in range(2) for r in range(0, regions, 2)]
    )
    ends = [(device(1, 0), device(1, 1)), (device(0, regions - 2), device(0, regions - 1))]
    next_pair = both_ways(
        [
            (device(0, r + i), device(1, r + 3 - i))
            for r in range(0, regions - 2, 2)
            for i in range(2)
        ]
        + ends
    )
    group, region = lax.axis_index("grp"), lax.axis_index(REG)
    right = group == region % 2
    alone = jnp.where(right, region >= regions - 2, region < 2)

    def swap(x, pairs):
        return lax.ppermute(x, GRP_REG, pairs)

    def totals(keep, send):
        half = keep + swap(send, cores)
        half = half + swap(half, pair)
        got = swap(half, next_pair)
        half = half + jnp.where(alone, 0.0, got)
        return half, swap(half, cores)

    def halves(rows):
        return [shape(2, rows, WIDE)] * 2

    run = functools.partial(call, scalar=True, regions=regions)
    field = pltpu.VMEM((128, 128), F32)
    per_point = shape(8, P_DEV)
    rest = [shape(16, 128), per_point, per_point, shape(8, OBS), shape(8, 128)]

    keep, send, jx, px, vinv, gres, index = run(
        first_kernel,
        halves(ROWS)
        + [shape(2, 16, OBS), shape(2, 8, OBS), per_point, per_point]
        + [shape(8, OBS, dtype=jnp.int32)],
        where, cam_jacobian, point_jacobian, residuals, camera, points,
        scratch=[
            pltpu.VMEM((2, OBS), F32), pltpu.VMEM((18, OBS), BF16), pltpu.VMEM((6, OBS), BF16),
            pltpu.VMEM((1, OBS), jnp.int32), pltpu.VMEM((1, OBS), jnp.int32),
            pltpu.SemaphoreType.DMA((5,)),
        ],
        inputs=HBM,
    )
    common = (index, jx, px, vinv)
    keep, send, factor, v0, g0, s0, rem0, scal0 = run(
        start_kernel,
        halves(16) + [shape(45 * 8, 128)] + rest,
        where, *totals(keep, send), *common,
        scratch=[pltpu.VMEM((8 * ROWS, 128), F32), field],
    )
    keep, send, v1, g1, s1, rem1, scal1 = run(
        next_kernel,
        halves(16) + rest,
        where, *totals(keep, send), factor, *common, v0, s0, rem0,
        scratch=[field, field],
    )
    v2, g2, sums = run(
        last_kernel,
        [shape(16, 128), per_point, shape(128, 32)],
        where, *totals(keep, send), factor, *common, v1, s1, rem1, scal0, scal1,
        scratch=[field, field],
    )
    back = lax.all_to_all(sums, GRP_REG, 0, 0, tiled=True)
    return call(
        final_kernel,
        [shape(9, C_DEV), shape(3, P_DEV)],
        back, v0, v1, v2, g0, g1, g2, gres, vinv,
    )


def solution(mesh):
    torus = Mesh(
        mesh.devices.reshape(mesh.shape["grp"], 4, 4, 4), ("grp", "reg_0", "reg_1", "reg_2")
    )
    return jax.shard_map(
        functools.partial(local, mesh.shape["reg"]),
        mesh=torus,
        in_specs=(P(None, GRP_REG), P(None, GRP_REG), P(None, GRP_REG), P(GRP_REG), P(GRP_REG)),
        out_specs=(P(None, GRP_REG), P(None, GRP_REG)),
        check_vma=False,
    )
```

```python
import functools

import jax
import jax.numpy as jnp
from jax import lax
from jax.experimental import pallas as pl
from jax.experimental.pallas import tpu as pltpu
from jax.sharding import Mesh
from jax.sharding import PartitionSpec as P

C_DEV = 128
P_DEV = 256
OBS = 2048
DAMPING = 4.0
WIDE = 2 * C_DEV
REG = ("reg_0", "reg_1", "reg_2")
GRP_REG = ("grp", "reg_0", "reg_1", "reg_2")
F32 = jnp.float32
BF16 = jnp.bfloat16
VMEM = pl.BlockSpec(memory_space=pltpu.VMEM)
HBM = pl.BlockSpec(memory_space=pltpu.HBM)
SMEM = pl.BlockSpec(memory_space=pltpu.SMEM)
ROWS = 56
VMEM_LIMIT = 32 * 1024 * 1024


def three_parts(x):
    high = x.astype(BF16)
    rest = x - high.astype(F32)
    middle = rest.astype(BF16)
    low = (rest - middle.astype(F32)).astype(BF16)
    return high, middle, low


def stacked(x):
    high, middle, low = three_parts(x)
    parts = [high.astype(F32), middle.astype(F32), low.astype(F32)]
    return jnp.concatenate(parts, 0).astype(BF16)


def folded(x):
    rows = x.shape[0] // 3
    return x[:rows] + x[rows : 2 * rows] + x[2 * rows :]


def pick(field, onehot):
    return lax.dot_general(
        field, onehot, (((1,), (0,)), ((), ())), preferred_element_type=F32
    )


def put(terms, onehot):
    return lax.dot_general(
        terms, onehot, (((1,), (1,)), ((), ())), preferred_element_type=F32
    )


def onehot_of(index):
    ids = lax.broadcasted_iota(jnp.int32, (WIDE, index.shape[1]), 0)
    return jnp.where(ids == index, 1.0, 0.0).astype(BF16)


def total(x):
    return jnp.sum(jnp.sum(x, 0, keepdims=True), 1, keepdims=True)


def per_lane(x):
    row = jnp.sum(x, 0, keepdims=True)
    return functools.reduce(
        lambda a, b: a + b, [row[:, k : k + 128] for k in range(0, row.shape[1], 128)]
    )


def solve_points(vinv, g):
    a, b, c, d, e, f = [vinv[k : k + 1] for k in range(6)]
    x, y, z = [g[k : k + 1] for k in range(3)]
    rows = [a * x + b * y + c * z, b * x + d * y + e * z, c * x + e * y + f * z]
    return rows + [jnp.zeros((8 - 3, g.shape[1]), F32)]


def point_part(u, p, hot_p, vinv):
    g = folded(put(stacked(p[0] * u[0] + p[1] * u[1]), hot_p))
    s = jnp.concatenate(solve_points(vinv, g), 0)
    back = folded(pick(stacked(s), hot_p))
    return g, s, [jnp.sum(p[i] * back, 0, keepdims=True) for i in range(2)]


def position(where, regions):
    device = where[0]
    region = device & (regions - 1)
    return device >> (regions.bit_length() - 1), region, region & 1


def indices(regions, region, camera):
    owners = camera >> (C_DEV.bit_length() - 1)
    low = ((owners >> (regions.bit_length() - 1)) * C_DEV) | (camera & (C_DEV - 1))
    return low, (owners & (regions - 1)) - region + 1


def split_frames(group, odd, blocks, keep, send):
    even = odd == 0
    zero = jnp.zeros_like(blocks[0])
    frames = [
        jnp.where(even, blocks[0], zero),
        jnp.where(even, blocks[1], blocks[0]),
        jnp.where(even, blocks[2], blocks[1]),
        jnp.where(even, zero, blocks[2]),
    ]
    first = group == odd
    for k in range(2):
        keep[k] = jnp.where(first, frames[2 + k], frames[k])
        send[k] = jnp.where(first, frames[k], frames[2 + k])


def to_tiles(tiles, group, odd, here, there):
    first = group == odd
    rows = here.shape[1]
    for k in range(2):
        mine, other = here[k], there[k]
        lower = jnp.where(first, other, mine)
        upper = jnp.where(first, mine, other)
        for h in range(2):
            lanes = slice(128 * h, 128 * h + 128)
            tiles[pl.ds(2 * k + h, rows, stride=8), :] = lower[:, lanes]
            tiles[pl.ds(4 + 2 * k + h, rows, stride=8), :] = upper[:, lanes]


def tile(tiles, k):
    return tiles[8 * k : 8 * k + 8, :]


def first_kernel(
    regions, where, cam_hbm, pnt_hbm, res_hbm, camera_hbm, points_hbm,
    keep, send, jx, px, vinv_out, gres_out, index, res, cam, pnt, camera, points, sems,
):
    pairs = [(points_hbm, points), (pnt_hbm, pnt), (res_hbm, res), (camera_hbm, camera), (cam_hbm, cam)]
    copies = [pltpu.make_async_copy(a, b, sems.at[k]) for k, (a, b) in enumerate(pairs)]
    for copy in copies:
        copy.start()
    group, region, odd = position(where, regions)
    copies[0].wait()
    slot = points[...]
    hot_p = onehot_of(slot)
    for copy in copies[1:]:
        copy.wait()
    low, block = indices(regions, region, camera[...])
    index[...] = jnp.concatenate([low, block, slot] + [jnp.zeros_like(low)] * 5, 0)
    camf = cam[...].astype(F32)
    pf = pnt[...].astype(F32)
    zero5 = jnp.zeros((5, OBS), F32)
    zero7 = jnp.zeros((7, OBS), F32)
    for i in range(2):
        jx[i, 0:8, :] = camf[9 * i : 9 * i + 8]
        jx[i, 8:16, :] = jnp.concatenate([camf[9 * i + 8 : 9 * i + 9], zero7], 0)
        px[i] = jnp.concatenate([pf[3 * i : 3 * i + 3], zero5], 0)
    p = [px[0], px[1]]
    a = [jx[0, 0:8, :], jx[1, 0:8, :]]
    last = [jx[0, 8:9, :], jx[1, 8:9, :]]
    r = [res[0:1, :], res[1:2, :]]
    row = lax.broadcasted_iota(jnp.int32, (8, OBS), 0)
    squares = p[0] * p[0] + p[1] * p[1]
    turned = [
        jnp.where(row == 2, jnp.broadcast_to(x[0:1], x.shape), pltpu.roll(x, 7, 0)) for x in p
    ]
    products = p[0] * turned[0] + p[1] * turned[1]
    right = p[0] * r[0] + p[1] * r[1]
    sums = folded(put(stacked(jnp.concatenate([squares, products, right], 0)), hot_p))
    v00, v11, v22 = [sums[k : k + 1] + DAMPING for k in range(3)]
    v01, v12, v02 = [sums[8 + k : 9 + k] for k in range(3)]
    g = sums[16:24]
    c00 = v11 * v22 - v12 * v12
    c01 = v02 * v12 - v01 * v22
    c02 = v01 * v12 - v02 * v11
    c11 = v00 * v22 - v02 * v02
    c12 = v01 * v02 - v00 * v12
    c22 = v00 * v11 - v01 * v01
    scale = 1.0 / (v00 * c00 + v01 * c01 + v02 * c02)
    cofactors = jnp.concatenate(
        [c00, c01, c02, c11, c12, c22, jnp.zeros((2, P_DEV), F32)], 0
    )
    vinv = cofactors * scale
    vinv_out[...] = vinv
    gres_out[...] = g
    s = jnp.concatenate(solve_points(vinv, g), 0)
    back = folded(pick(stacked(s), hot_p))
    rem = [r[i] - jnp.sum(p[i] * back, 0, keepdims=True) for i in range(2)]
    rolled = []
    for d in range(5):
        other = [x if d == 0 else pltpu.roll(x, d, 0) for x in a]
        rolled.append(a[0] * other[0] + a[1] * other[1])
    corner = last[0] * last[0] + last[1] * last[1]
    end = last[0] * rem[0] + last[1] * rem[1]
    rolled[4] = jnp.where(row < 4, rolled[4], jnp.where(row == 4, corner, end))
    edge = a[0] * last[0] + a[1] * last[1]
    gradient = a[0] * rem[0] + a[1] * rem[1]
    terms = stacked(jnp.concatenate(rolled + [edge, gradient], 0))
    hot_c = onehot_of(low)
    blocks = []
    for k in range(3):
        mask = jnp.where(block == k, 1.0, 0.0).astype(BF16)
        blocks.append(folded(put(terms * mask, hot_c)))
    split_frames(group, odd, blocks, keep, send)


def solve_camera(low, inv, b):
    y = list(b)
    for k in range(9):
        y[k] = y[k] * inv[k]
        for i in range(k + 1, 9):
            y[i] = y[i] - low[i][k] * y[k]
    for k in range(8, -1, -1):
        y[k] = y[k] * inv[k]
        for i in range(k):
            y[i] = y[i] - low[k][i] * y[k]
    return y


def factor_camera(tiles, factor):
    def entry(i, j):
        if i == 8:
            k = 36 if j == 8 else 40 + j
        elif i - j < 4:
            k = 8 * (i - j) + i
        elif i - j == 4:
            k = 32 + j
        else:
            k = 8 * (8 - (i - j)) + j
        x = tile(tiles, k)
        return x + DAMPING if i == j else x

    low = [[None] * 9 for _ in range(9)]
    work = [[entry(i, j) if j <= i else None for j in range(9)] for i in range(9)]
    inv = []
    for k in range(9):
        inv.append(1.0 / jnp.sqrt(work[k][k]))
        for i in range(k + 1, 9):
            low[i][k] = work[i][k] * inv[k]
        for i in range(k + 1, 9):
            for j in range(k + 1, i + 1):
                work[i][j] = work[i][j] - low[i][k] * low[j][k]
    flat = [low[i][j] for i in range(9) for j in range(i)] + inv
    for k, x in enumerate(flat):
        factor[8 * k : 8 * k + 8, :] = x
    return low, inv


def read_factor(factor):
    low = [[None] * 9 for _ in range(9)]
    at = 0
    for i in range(9):
        for j in range(i):
            low[i][j] = tile(factor, at)
            at += 1
    return low, [tile(factor, at + k) for k in range(9)]


def apply_body(group, odd, x, field, low, block, slot, jx, px, vinv):
    hot_c = onehot_of(low)
    hot_p = onehot_of(slot)
    for k in range(9):
        field[8 * k : 8 * k + 8, :] = x[k]
    for k in range(9, 16):
        field[8 * k : 8 * k + 8, :] = jnp.zeros((8, 128), F32)
    frames = [
        jnp.concatenate([field[pl.ds(2 * f + h, 16, stride=8), :] for h in range(2)], 1)
        for f in range(4)
    ]
    seen = [jnp.where(odd == 0, frames[k], frames[k + 1]) for k in range(3)]
    v = jnp.where(group == 0, seen[1][:, 0:128], seen[1][:, 128:256])
    picked = pick(jnp.concatenate([stacked(f) for f in seen], 0), hot_c)
    blocks = [folded(picked[48 * k : 48 * k + 48]) for k in range(3)]
    values = jnp.where(block == 0, blocks[0], jnp.where(block == 1, blocks[1], blocks[2]))
    u = [jnp.sum(jx[i] * values, 0, keepdims=True) for i in range(2)]
    p = [px[0], px[1]]
    g, s, ps = point_part(u, p, hot_p, vinv[...])
    return hot_c, v, u, g, s, ps


def finish(group, odd, hot_c, block, jx, ps, keep, send):
    terms = stacked(jx[0] * ps[0] + jx[1] * ps[1])
    lhs = jnp.concatenate(
        [terms * jnp.where(block == k, 1.0, 0.0).astype(BF16) for k in range(3)], 0
    )
    out = put(lhs, hot_c)
    split_frames(
        group, odd, [folded(out[48 * k : 48 * k + 48]) for k in range(3)], keep, send
    )


def scalar_rows(pairs):
    rows = [functools.reduce(lambda a, b: a + b, [per_lane(x) for x in pair]) for pair in pairs]
    return jnp.concatenate(rows + [jnp.zeros((8 - len(rows), 128), F32)], 0)


def scalars(v, v_old, u, rem, rem_old, g, s, s_old):
    return scalar_rows(
        [
            (DAMPING * v * v_old, u[0] * rem_old[0:1, :] + u[1] * rem_old[1:2, :]),
            (DAMPING * v * v, u[0] * rem[0] + u[1] * rem[1]),
            (g * s_old,),
            (g * s,),
        ]
    )


def start_kernel(
    regions, where, here, there, index, jx, px, vinv,
    keep, send, factor, v_out, g_out, s_out, rem_out, scal, tiles, field,
):
    group, region, odd = position(where, regions)
    low, block, slot = index[0:1, :], index[1:2, :], index[2:3, :]
    to_tiles(tiles, group, odd, here, there)
    lower, inv = factor_camera(tiles, factor)
    b = [-tile(tiles, 48 + k) for k in range(8)] + [-tile(tiles, 37)]
    x = solve_camera(lower, inv, b)
    dots = functools.reduce(lambda p, q: p + q, [b[k] * x[k] for k in range(9)])
    own = lax.broadcasted_iota(jnp.int32, (8, 128), 0) == 2 * (1 + odd) + group
    hot_c, v, u, g, s, ps = apply_body(
        group, odd, x, field, low, block, slot, jx, px, vinv
    )
    rem = [u[i] - ps[i] for i in range(2)]
    v_out[...], g_out[...], s_out[...] = v, g, s
    rem_out[...] = jnp.concatenate(rem + [jnp.zeros((6, OBS), F32)], 0)
    finish(group, odd, hot_c, block, jx, ps, keep, send)
    scal[...] = scalar_rows(
        [
            (jnp.where(own, dots, 0.0),),
            (DAMPING * v * v, u[0] * rem[0] + u[1] * rem[1]),
            (g * s,),
        ]
    )


def next_kernel(
    regions, where, here, there, factor, index, jx, px, vinv, v_old, s_old, rem_old,
    keep, send, v_out, g_out, s_out, rem_out, scal, tiles, field,
):
    group, region, odd = position(where, regions)
    low, block, slot = index[0:1, :], index[1:2, :], index[2:3, :]
    to_tiles(tiles, group, odd, here, there)
    x = solve_camera(*read_factor(factor), [tile(tiles, k) for k in range(9)])
    hot_c, v, u, g, s, ps = apply_body(
        group, odd, x, field, low, block, slot, jx, px, vinv
    )
    rem = [u[i] - ps[i] for i in range(2)]
    v_out[...], g_out[...], s_out[...] = v, g, s
    rem_out[...] = jnp.concatenate(rem + [jnp.zeros((6, OBS), F32)], 0)
    finish(group, odd, hot_c, block, jx, ps, keep, send)
    scal[...] = scalars(v, v_old[...], u, rem, rem_old, g, s, s_old[...])


def last_kernel(
    regions, where, here, there, factor, index, jx, px, vinv, v_old, s_old, rem_old,
    scal0, scal1, v_out, g_out, sums, tiles, field,
):
    group, region, odd = position(where, regions)
    low, block, slot = index[0:1, :], index[1:2, :], index[2:3, :]
    to_tiles(tiles, group, odd, here, there)
    x = solve_camera(*read_factor(factor), [tile(tiles, k) for k in range(9)])
    hot_c, v, u, g, s, ps = apply_body(
        group, odd, x, field, low, block, slot, jx, px, vinv
    )
    rem = [u[i] - ps[i] for i in range(2)]
    v_out[...], g_out[...] = v, g
    scal2 = scalars(v, v_old[...], u, rem, rem_old, g, s, s_old[...])
    rows = jnp.concatenate([scal0[...], scal1[...], scal2, jnp.zeros((8, 128), F32)], 0)
    ones = jnp.ones((128, 128), BF16)
    high, middle, low_part = three_parts(rows)
    sums[...] = put(ones, high) + put(ones, middle) + put(ones, low_part)


def final_kernel(back, v0, v1, v2, g0, g1, g2, gres, vinv, cam, pnt):
    sums = jnp.sum(back[...], 0, keepdims=True)

    def value(k):
        return sums[:, k : k + 1]

    m = [value(k) for k in (0, 2, 10, 11, 18)]
    s = [value(k) for k in (1, 8, 9, 16, 17)]

    def form(h, x):
        terms = [x[i] * x[j] * h[i + j] for i in range(3) for j in range(3)]
        return functools.reduce(lambda p, q: p + q, terms)

    def ratio(x, y):
        return jnp.where(y > 0, x / jnp.where(y > 0, y, 1.0), 0.0)

    one, zero = jnp.ones((1, 1), F32), jnp.zeros((1, 1), F32)
    y = [zero, zero, zero]
    z = [one, zero, zero]
    d = list(z)
    current = m[0]
    for turn in range(3):
        step = ratio(current, form(s, d))
        y = [y[k] + step * d[k] for k in range(3)]
        if turn < 2:
            image = [d[0], d[1] - d[0], d[2] - d[1]]
            z = [z[k] - step * image[k] for k in range(3)]
            following = form(m, z)
            beta = ratio(following, current)
            d = [z[k] + beta * d[k] for k in range(3)]
            current = following
    x = y[0] * v0[...] + y[1] * v1[...] + y[2] * v2[...]
    cam[...] = x[0:9]
    g = gres[...] + (y[0] * g0[...] + y[1] * g1[...] + y[2] * g2[...])
    rows = solve_points(vinv[...], g)
    for k in range(3):
        pnt[k : k + 1, :] = -rows[k]


def shape(*dims, dtype=F32):
    return jax.ShapeDtypeStruct(dims, dtype)


def call(kernel, outs, *args, scalar=False, scratch=(), regions=None, inputs=VMEM):
    specs = [inputs] * len(args)
    if scalar:
        specs[0] = SMEM
    return pl.pallas_call(
        kernel if regions is None else functools.partial(kernel, regions),
        out_shape=outs,
        in_specs=specs,
        out_specs=[VMEM] * len(outs),
        scratch_shapes=scratch,
        compiler_params=pltpu.CompilerParams(vmem_limit_bytes=VMEM_LIMIT),
        name=kernel.__name__,
    )(*args)


def local(regions, cam_jacobian, point_jacobian, residuals, obs_camera, obs_point):
    where = (lax.axis_index("grp") * regions + lax.axis_index(REG)).reshape(1)
    arrays = (cam_jacobian, point_jacobian, residuals)
    arrays += (obs_camera.reshape(1, OBS), obs_point.reshape(1, OBS))
    arrays = [pltpu.with_memory_space_constraint(x, pltpu.HBM) for x in arrays]

    def both_ways(pairs):
        return pairs + [(b, a) for a, b in pairs]

    def device(left, region):
        return ((region & 1) ^ left) * regions + region

    cores = both_ways([(r, regions + r) for r in range(regions)])
    pair = both_ways(
        [(device(h, r), device(h, r + 1)) for h in range(2) for r in range(0, regions, 2)]
    )
    ends = [(device(1, 0), device(1, 1)), (device(0, regions - 2), device(0, regions - 1))]
    next_pair = both_ways(
        [
            (device(0, r + i), device(1, r + 3 - i))
            for r in range(0, regions - 2, 2)
            for i in range(2)
        ]
        + ends
    )
    group, region = lax.axis_index("grp"), lax.axis_index(REG)
    right = group == region % 2
    alone = jnp.where(right, region >= regions - 2, region < 2)

    def swap(x, pairs):
        return lax.ppermute(x, GRP_REG, pairs)

    def totals(keep, send):
        half = keep + swap(send, cores)
        half = half + swap(half, pair)
        got = swap(half, next_pair)
        half = half + jnp.where(alone, 0.0, got)
        return half, swap(half, cores)

    def halves(rows):
        return [shape(2, rows, WIDE)] * 2

    run = functools.partial(call, scalar=True, regions=regions)
    field = pltpu.VMEM((128, 128), F32)
    per_point = shape(8, P_DEV)
    rest = [shape(16, 128), per_point, per_point, shape(8, OBS), shape(8, 128)]

    keep, send, jx, px, vinv, gres, index = run(
        first_kernel,
        halves(ROWS)
        + [shape(2, 16, OBS), shape(2, 8, OBS), per_point, per_point]
        + [shape(8, OBS, dtype=jnp.int32)],
        where, *arrays,
        scratch=[
            pltpu.VMEM((2, OBS), F32), pltpu.VMEM((18, OBS), BF16), pltpu.VMEM((6, OBS), BF16),
            pltpu.VMEM((1, OBS), jnp.int32), pltpu.VMEM((1, OBS), jnp.int32),
            pltpu.SemaphoreType.DMA((5,)),
        ],
        inputs=HBM,
    )
    common = (index, jx, px, vinv)
    keep, send, factor, v0, g0, s0, rem0, scal0 = run(
        start_kernel,
        halves(16) + [shape(45 * 8, 128)] + rest,
        where, *totals(keep, send), *common,
        scratch=[pltpu.VMEM((8 * ROWS, 128), F32), field],
    )
    keep, send, v1, g1, s1, rem1, scal1 = run(
        next_kernel,
        halves(16) + rest,
        where, *totals(keep, send), factor, *common, v0, s0, rem0,
        scratch=[field, field],
    )
    v2, g2, sums = run(
        last_kernel,
        [shape(16, 128), per_point, shape(128, 32)],
        where, *totals(keep, send), factor, *common, v1, s1, rem1, scal0, scal1,
        scratch=[field, field],
    )
    back = lax.all_to_all(sums, GRP_REG, 0, 0, tiled=True)
    return call(
        final_kernel,
        [shape(9, C_DEV), shape(3, P_DEV)],
        back, v0, v1, v2, g0, g1, g2, gres, vinv,
    )


def solution(mesh):
    torus = Mesh(
        mesh.devices.reshape(mesh.shape["grp"], 4, 4, 4), ("grp", "reg_0", "reg_1", "reg_2")
    )
    return jax.shard_map(
        functools.partial(local, mesh.shape["reg"]),
        mesh=torus,
        in_specs=(P(None, GRP_REG), P(None, GRP_REG), P(None, GRP_REG), P(GRP_REG), P(GRP_REG)),
        out_specs=(P(None, GRP_REG), P(None, GRP_REG)),
        check_vma=False,
    )
```

```python
import functools

import jax
import jax.numpy as jnp
from jax import lax
from jax.experimental import pallas as pl
from jax.experimental.pallas import tpu as pltpu
from jax.sharding import Mesh
from jax.sharding import PartitionSpec as P

C_DEV = 128
P_DEV = 256
OBS = 2048
DAMPING = 4.0
WIDE = 2 * C_DEV
REG = ("reg_0", "reg_1", "reg_2")
GRP_REG = ("grp", "reg_0", "reg_1", "reg_2")
F32 = jnp.float32
BF16 = jnp.bfloat16
VMEM = pl.BlockSpec(memory_space=pltpu.VMEM)
HBM = pl.BlockSpec(memory_space=pltpu.HBM)
SMEM = pl.BlockSpec(memory_space=pltpu.SMEM)
ROWS = 56
VMEM_LIMIT = 32 * 1024 * 1024


def three_parts(x):
    high = x.astype(BF16)
    rest = x - high.astype(F32)
    middle = rest.astype(BF16)
    low = (rest - middle.astype(F32)).astype(BF16)
    return high, middle, low


def stacked(x):
    high, middle, low = three_parts(x)
    parts = [high.astype(F32), middle.astype(F32), low.astype(F32)]
    return jnp.concatenate(parts, 0).astype(BF16)


def folded(x):
    rows = x.shape[0] // 3
    return x[:rows] + x[rows : 2 * rows] + x[2 * rows :]


def pick(field, onehot):
    return lax.dot_general(
        field, onehot, (((1,), (0,)), ((), ())), preferred_element_type=F32
    )


def put(terms, onehot):
    return lax.dot_general(
        terms, onehot[...], (((1,), (1,)), ((), ())), preferred_element_type=F32
    )


def put_few(terms, onehot):
    half = WIDE // 2
    parts = [
        lax.dot_general(
            terms,
            onehot[k : k + half, :],
            (((1,), (1,)), ((), ())),
            preferred_element_type=F32,
        )
        for k in (0, half)
    ]
    return jnp.concatenate(parts, 1)


def write_onehot(out, index):
    ids = lax.broadcasted_iota(jnp.int32, (16, index.shape[1]), 0)

    def step(k, carry):
        start = pl.multiple_of(k * 16, 16)
        out[pl.ds(start, 16), :] = jnp.where(ids == index - start, 1.0, 0.0).astype(BF16)
        return carry

    lax.fori_loop(0, WIDE // 16, step, 0)


def per_lane(x):
    row = jnp.sum(x, 0, keepdims=True)
    return functools.reduce(
        lambda a, b: a + b, [row[:, k : k + 128] for k in range(0, row.shape[1], 128)]
    )


def solve_points(vinv, g):
    a, b, c, d, e, f = [vinv[k : k + 1] for k in range(6)]
    x, y, z = [g[k : k + 1] for k in range(3)]
    rows = [a * x + b * y + c * z, b * x + d * y + e * z, c * x + e * y + f * z]
    return rows + [jnp.zeros((8 - 3, g.shape[1]), F32)]


def point_part(u, p, hot_p, vinv):
    g = folded(put_few(stacked(p[0] * u[0] + p[1] * u[1]), hot_p))
    s = jnp.concatenate(solve_points(vinv, g), 0)
    back = folded(pick(stacked(s), hot_p[...]))
    return g, s, [jnp.sum(p[i] * back, 0, keepdims=True) for i in range(2)]


def position(where, regions):
    device = where[0]
    region = device & (regions - 1)
    return device >> (regions.bit_length() - 1), region, region & 1


def indices(regions, region, camera):
    owners = camera >> (C_DEV.bit_length() - 1)
    low = ((owners >> (regions.bit_length() - 1)) * C_DEV) | (camera & (C_DEV - 1))
    return low, (owners & (regions - 1)) - region + 1


def split_frames(group, odd, blocks, keep, send):
    even = odd == 0
    zero = jnp.zeros_like(blocks[0])
    frames = [
        jnp.where(even, blocks[0], zero),
        jnp.where(even, blocks[1], blocks[0]),
        jnp.where(even, blocks[2], blocks[1]),
        jnp.where(even, zero, blocks[2]),
    ]
    first = group == odd
    for k in range(2):
        keep[k] = jnp.where(first, frames[2 + k], frames[k])
        send[k] = jnp.where(first, frames[k], frames[2 + k])


def to_tiles(tiles, group, odd, here, there):
    first = group == odd
    rows = here.shape[1]
    for k in range(2):
        mine, other = here[k], there[k]
        lower = jnp.where(first, other, mine)
        upper = jnp.where(first, mine, other)
        for h in range(2):
            lanes = slice(128 * h, 128 * h + 128)
            tiles[pl.ds(2 * k + h, rows, stride=8), :] = lower[:, lanes]
            tiles[pl.ds(4 + 2 * k + h, rows, stride=8), :] = upper[:, lanes]


def tile(tiles, k):
    return tiles[8 * k : 8 * k + 8, :]


def first_kernel(
    regions, where, cam_hbm, pnt_hbm, res_hbm, camera_hbm, points_hbm,
    keep, send, jx, px, vinv_out, gres_out, block_out, hot_p, hot_c, res, cam, pnt, camera, points, sems,
):
    pairs = [(points_hbm, points), (pnt_hbm, pnt), (res_hbm, res), (camera_hbm, camera), (cam_hbm, cam)]
    copies = [pltpu.make_async_copy(a, b, sems.at[k]) for k, (a, b) in enumerate(pairs)]
    for copy in copies:
        copy.start()
    group, region, odd = position(where, regions)
    copies[0].wait()
    write_onehot(hot_p, points[...])
    for copy in copies[1:]:
        copy.wait()
    low, block = indices(regions, region, camera[...])
    block_out[...] = block
    write_onehot(hot_c, low)
    camf = cam[...].astype(F32)
    pf = pnt[...].astype(F32)
    zero5 = jnp.zeros((5, OBS), F32)
    zero7 = jnp.zeros((7, OBS), F32)
    for i in range(2):
        jx[i, 0:8, :] = camf[9 * i : 9 * i + 8]
        jx[i, 8:16, :] = jnp.concatenate([camf[9 * i + 8 : 9 * i + 9], zero7], 0)
        px[i] = jnp.concatenate([pf[3 * i : 3 * i + 3], zero5], 0)
    p = [px[0], px[1]]
    a = [jx[0, 0:8, :], jx[1, 0:8, :]]
    last = [jx[0, 8:9, :], jx[1, 8:9, :]]
    r = [res[0:1, :], res[1:2, :]]
    row = lax.broadcasted_iota(jnp.int32, (8, OBS), 0)
    squares = p[0] * p[0] + p[1] * p[1]
    turned = [
        jnp.where(row == 2, jnp.broadcast_to(x[0:1], x.shape), pltpu.roll(x, 7, 0)) for x in p
    ]
    products = p[0] * turned[0] + p[1] * turned[1]
    right = p[0] * r[0] + p[1] * r[1]
    sums = folded(put_few(stacked(jnp.concatenate([squares, products, right], 0)), hot_p))
    v00, v11, v22 = [sums[k : k + 1] + DAMPING for k in range(3)]
    v01, v12, v02 = [sums[8 + k : 9 + k] for k in range(3)]
    g = sums[16:24]
    c00 = v11 * v22 - v12 * v12
    c01 = v02 * v12 - v01 * v22
    c02 = v01 * v12 - v02 * v11
    c11 = v00 * v22 - v02 * v02
    c12 = v01 * v02 - v00 * v12
    c22 = v00 * v11 - v01 * v01
    scale = 1.0 / (v00 * c00 + v01 * c01 + v02 * c02)
    cofactors = jnp.concatenate(
        [c00, c01, c02, c11, c12, c22, jnp.zeros((2, P_DEV), F32)], 0
    )
    vinv = cofactors * scale
    vinv_out[...] = vinv
    gres_out[...] = g
    s = jnp.concatenate(solve_points(vinv, g), 0)
    back = folded(pick(stacked(s), hot_p[...]))
    rem = [r[i] - jnp.sum(p[i] * back, 0, keepdims=True) for i in range(2)]
    rolled = []
    for d in range(5):
        other = [x if d == 0 else pltpu.roll(x, d, 0) for x in a]
        rolled.append(a[0] * other[0] + a[1] * other[1])
    corner = last[0] * last[0] + last[1] * last[1]
    end = last[0] * rem[0] + last[1] * rem[1]
    rolled[4] = jnp.where(row < 4, rolled[4], jnp.where(row == 4, corner, end))
    edge = a[0] * last[0] + a[1] * last[1]
    gradient = a[0] * rem[0] + a[1] * rem[1]
    terms = stacked(jnp.concatenate(rolled + [edge, gradient], 0))
    blocks = []
    for k in range(3):
        mask = jnp.where(block == k, 1.0, 0.0).astype(BF16)
        blocks.append(folded(put(terms * mask, hot_c)))
    split_frames(group, odd, blocks, keep, send)


def solve_camera(low, inv, b):
    y = list(b)
    for k in range(9):
        y[k] = y[k] * inv[k]
        for i in range(k + 1, 9):
            y[i] = y[i] - low[i][k] * y[k]
    for k in range(8, -1, -1):
        y[k] = y[k] * inv[k]
        for i in range(k):
            y[i] = y[i] - low[k][i] * y[k]
    return y


def factor_camera(tiles, factor):
    def entry(i, j):
        if i == 8:
            k = 36 if j == 8 else 40 + j
        elif i - j < 4:
            k = 8 * (i - j) + i
        elif i - j == 4:
            k = 32 + j
        else:
            k = 8 * (8 - (i - j)) + j
        x = tile(tiles, k)
        return x + DAMPING if i == j else x

    low = [[None] * 9 for _ in range(9)]
    work = [[entry(i, j) if j <= i else None for j in range(9)] for i in range(9)]
    inv = []
    for k in range(9):
        inv.append(1.0 / jnp.sqrt(work[k][k]))
        for i in range(k + 1, 9):
            low[i][k] = work[i][k] * inv[k]
        for i in range(k + 1, 9):
            for j in range(k + 1, i + 1):
                work[i][j] = work[i][j] - low[i][k] * low[j][k]
    flat = [low[i][j] for i in range(9) for j in range(i)] + inv
    for k, x in enumerate(flat):
        factor[8 * k : 8 * k + 8, :] = x
    return low, inv


def read_factor(factor):
    low = [[None] * 9 for _ in range(9)]
    at = 0
    for i in range(9):
        for j in range(i):
            low[i][j] = tile(factor, at)
            at += 1
    return low, [tile(factor, at + k) for k in range(9)]


def apply_body(group, odd, x, field, block, hot_p, hot_c, jx, px, vinv):
    for k in range(9):
        field[8 * k : 8 * k + 8, :] = x[k]
    for k in range(9, 16):
        field[8 * k : 8 * k + 8, :] = jnp.zeros((8, 128), F32)
    frames = [
        jnp.concatenate([field[pl.ds(2 * f + h, 16, stride=8), :] for h in range(2)], 1)
        for f in range(4)
    ]
    seen = [jnp.where(odd == 0, frames[k], frames[k + 1]) for k in range(3)]
    v = jnp.where(group == 0, seen[1][:, 0:128], seen[1][:, 128:256])
    picked = pick(jnp.concatenate([stacked(f) for f in seen], 0), hot_c[...])
    blocks = [folded(picked[48 * k : 48 * k + 48]) for k in range(3)]
    values = jnp.where(block == 0, blocks[0], jnp.where(block == 1, blocks[1], blocks[2]))
    u = [jnp.sum(jx[i] * values, 0, keepdims=True) for i in range(2)]
    p = [px[0], px[1]]
    g, s, ps = point_part(u, p, hot_p, vinv[...])
    return v, u, g, s, ps


def finish(group, odd, hot_c, block, jx, ps, keep, send):
    terms = stacked(jx[0] * ps[0] + jx[1] * ps[1])
    lhs = jnp.concatenate(
        [terms * jnp.where(block == k, 1.0, 0.0).astype(BF16) for k in range(3)], 0
    )
    out = put(lhs, hot_c)
    split_frames(
        group, odd, [folded(out[48 * k : 48 * k + 48]) for k in range(3)], keep, send
    )


def scalar_rows(pairs):
    rows = [functools.reduce(lambda a, b: a + b, [per_lane(x) for x in pair]) for pair in pairs]
    return jnp.concatenate(rows + [jnp.zeros((8 - len(rows), 128), F32)], 0)


def scalars(v, v_old, u, rem, rem_old, g, s, s_old):
    return scalar_rows(
        [
            (DAMPING * v * v_old, u[0] * rem_old[0:1, :] + u[1] * rem_old[1:2, :]),
            (DAMPING * v * v, u[0] * rem[0] + u[1] * rem[1]),
            (g * s_old,),
            (g * s,),
        ]
    )


def start_kernel(
    regions, where, here, there, block_in, hot_p, hot_c, jx, px, vinv,
    keep, send, factor, v_out, g_out, s_out, rem_out, scal, tiles, field,
):
    group, region, odd = position(where, regions)
    block = block_in[...]
    to_tiles(tiles, group, odd, here, there)
    lower, inv = factor_camera(tiles, factor)
    b = [-tile(tiles, 48 + k) for k in range(8)] + [-tile(tiles, 37)]
    x = solve_camera(lower, inv, b)
    dots = functools.reduce(lambda p, q: p + q, [b[k] * x[k] for k in range(9)])
    own = lax.broadcasted_iota(jnp.int32, (8, 128), 0) == 2 * (1 + odd) + group
    v, u, g, s, ps = apply_body(
        group, odd, x, field, block, hot_p, hot_c, jx, px, vinv
    )
    rem = [u[i] - ps[i] for i in range(2)]
    v_out[...], g_out[...], s_out[...] = v, g, s
    rem_out[...] = jnp.concatenate(rem + [jnp.zeros((6, OBS), F32)], 0)
    finish(group, odd, hot_c, block, jx, ps, keep, send)
    scal[...] = scalar_rows(
        [
            (jnp.where(own, dots, 0.0),),
            (DAMPING * v * v, u[0] * rem[0] + u[1] * rem[1]),
            (g * s,),
        ]
    )


def next_kernel(
    regions, where, here, there, factor, block_in, hot_p, hot_c, jx, px, vinv, v_old, s_old, rem_old,
    keep, send, v_out, g_out, s_out, rem_out, scal, tiles, field,
):
    group, region, odd = position(where, regions)
    block = block_in[...]
    to_tiles(tiles, group, odd, here, there)
    x = solve_camera(*read_factor(factor), [tile(tiles, k) for k in range(9)])
    v, u, g, s, ps = apply_body(
        group, odd, x, field, block, hot_p, hot_c, jx, px, vinv
    )
    rem = [u[i] - ps[i] for i in range(2)]
    v_out[...], g_out[...], s_out[...] = v, g, s
    rem_out[...] = jnp.concatenate(rem + [jnp.zeros((6, OBS), F32)], 0)
    finish(group, odd, hot_c, block, jx, ps, keep, send)
    scal[...] = scalars(v, v_old[...], u, rem, rem_old, g, s, s_old[...])


def last_kernel(
    regions, where, here, there, factor, block_in, hot_p, hot_c, jx, px, vinv, v_old, s_old, rem_old,
    scal0, scal1, v_out, g_out, sums, tiles, field,
):
    group, region, odd = position(where, regions)
    block = block_in[...]
    to_tiles(tiles, group, odd, here, there)
    x = solve_camera(*read_factor(factor), [tile(tiles, k) for k in range(9)])
    v, u, g, s, ps = apply_body(
        group, odd, x, field, block, hot_p, hot_c, jx, px, vinv
    )
    rem = [u[i] - ps[i] for i in range(2)]
    v_out[...], g_out[...] = v, g
    scal2 = scalars(v, v_old[...], u, rem, rem_old, g, s, s_old[...])
    rows = jnp.concatenate([scal0[...], scal1[...], scal2, jnp.zeros((8, 128), F32)], 0)
    ones = jnp.ones((128, 128), BF16)
    high, middle, low_part = three_parts(rows)
    sums[...] = sum(
        lax.dot_general(ones, x, (((1,), (1,)), ((), ())), preferred_element_type=F32)
        for x in (high, middle, low_part)
    )


def final_kernel(back, v0, v1, v2, g0, g1, g2, gres, vinv, cam, pnt):
    sums = jnp.sum(back[...], 0, keepdims=True)

    def value(k):
        return sums[:, k : k + 1]

    m = [value(k) for k in (0, 2, 10, 11, 18)]
    s = [value(k) for k in (1, 8, 9, 16, 17)]

    def form(h, x):
        terms = [x[i] * x[j] * h[i + j] for i in range(3) for j in range(3)]
        return functools.reduce(lambda p, q: p + q, terms)

    def ratio(x, y):
        return jnp.where(y > 0, x / jnp.where(y > 0, y, 1.0), 0.0)

    one, zero = jnp.ones((1, 1), F32), jnp.zeros((1, 1), F32)
    y = [zero, zero, zero]
    z = [one, zero, zero]
    d = list(z)
    current = m[0]
    for turn in range(3):
        step = ratio(current, form(s, d))
        y = [y[k] + step * d[k] for k in range(3)]
        if turn < 2:
            image = [d[0], d[1] - d[0], d[2] - d[1]]
            z = [z[k] - step * image[k] for k in range(3)]
            following = form(m, z)
            beta = ratio(following, current)
            d = [z[k] + beta * d[k] for k in range(3)]
            current = following
    x = y[0] * v0[...] + y[1] * v1[...] + y[2] * v2[...]
    cam[...] = x[0:9]
    g = gres[...] + (y[0] * g0[...] + y[1] * g1[...] + y[2] * g2[...])
    rows = solve_points(vinv[...], g)
    for k in range(3):
        pnt[k : k + 1, :] = -rows[k]


def shape(*dims, dtype=F32):
    return jax.ShapeDtypeStruct(dims, dtype)


def call(kernel, outs, *args, scalar=False, scratch=(), regions=None, inputs=VMEM):
    specs = [inputs] * len(args)
    if scalar:
        specs[0] = SMEM
    return pl.pallas_call(
        kernel if regions is None else functools.partial(kernel, regions),
        out_shape=outs,
        in_specs=specs,
        out_specs=[VMEM] * len(outs),
        scratch_shapes=scratch,
        compiler_params=pltpu.CompilerParams(vmem_limit_bytes=VMEM_LIMIT),
        name=kernel.__name__,
    )(*args)


def local(regions, cam_jacobian, point_jacobian, residuals, obs_camera, obs_point):
    where = (lax.axis_index("grp") * regions + lax.axis_index(REG)).reshape(1)
    arrays = (cam_jacobian, point_jacobian, residuals)
    arrays += (obs_camera.reshape(1, OBS), obs_point.reshape(1, OBS))
    arrays = [pltpu.with_memory_space_constraint(x, pltpu.HBM) for x in arrays]

    def both_ways(pairs):
        return pairs + [(b, a) for a, b in pairs]

    def device(left, region):
        return ((region & 1) ^ left) * regions + region

    cores = both_ways([(r, regions + r) for r in range(regions)])
    pair = both_ways(
        [(device(h, r), device(h, r + 1)) for h in range(2) for r in range(0, regions, 2)]
    )
    ends = [(device(1, 0), device(1, 1)), (device(0, regions - 2), device(0, regions - 1))]
    next_pair = both_ways(
        [
            (device(0, r + i), device(1, r + 3 - i))
            for r in range(0, regions - 2, 2)
            for i in range(2)
        ]
        + ends
    )
    group, region = lax.axis_index("grp"), lax.axis_index(REG)
    right = group == region % 2
    alone = jnp.where(right, region >= regions - 2, region < 2)

    def swap(x, pairs):
        return lax.ppermute(x, GRP_REG, pairs)

    def totals(keep, send):
        half = keep + swap(send, cores)
        half = half + swap(half, pair)
        got = swap(half, next_pair)
        half = half + jnp.where(alone, 0.0, got)
        return half, swap(half, cores)

    def halves(rows):
        return [shape(2, rows, WIDE)] * 2

    run = functools.partial(call, scalar=True, regions=regions)
    field = pltpu.VMEM((128, 128), F32)
    per_point = shape(8, P_DEV)
    rest = [shape(16, 128), per_point, per_point, shape(8, OBS), shape(8, 128)]

    keep, send, jx, px, vinv, gres, block, hot_p, hot_c = run(
        first_kernel,
        halves(ROWS)
        + [shape(2, 16, OBS), shape(2, 8, OBS), per_point, per_point]
        + [shape(1, OBS, dtype=jnp.int32)]
        + [shape(WIDE, OBS, dtype=BF16)] * 2,
        where, *arrays,
        scratch=[
            pltpu.VMEM((2, OBS), F32), pltpu.VMEM((18, OBS), BF16), pltpu.VMEM((6, OBS), BF16),
            pltpu.VMEM((1, OBS), jnp.int32), pltpu.VMEM((1, OBS), jnp.int32),
            pltpu.SemaphoreType.DMA((5,)),
        ],
        inputs=HBM,
    )
    common = (block, hot_p, hot_c, jx, px, vinv)
    keep, send, factor, v0, g0, s0, rem0, scal0 = run(
        start_kernel,
        halves(16) + [shape(45 * 8, 128)] + rest,
        where, *totals(keep, send), *common,
        scratch=[pltpu.VMEM((8 * ROWS, 128), F32), field],
    )
    keep, send, v1, g1, s1, rem1, scal1 = run(
        next_kernel,
        halves(16) + rest,
        where, *totals(keep, send), factor, *common, v0, s0, rem0,
        scratch=[field, field],
    )
    v2, g2, sums = run(
        last_kernel,
        [shape(16, 128), per_point, shape(128, 32)],
        where, *totals(keep, send), factor, *common, v1, s1, rem1, scal0, scal1,
        scratch=[field, field],
    )
    back = lax.all_to_all(sums, GRP_REG, 0, 0, tiled=True)
    return call(
        final_kernel,
        [shape(9, C_DEV), shape(3, P_DEV)],
        back, v0, v1, v2, g0, g1, g2, gres, vinv,
    )


def solution(mesh):
    torus = Mesh(
        mesh.devices.reshape(mesh.shape["grp"], 4, 4, 4), ("grp", "reg_0", "reg_1", "reg_2")
    )
    return jax.shard_map(
        functools.partial(local, mesh.shape["reg"]),
        mesh=torus,
        in_specs=(P(None, GRP_REG), P(None, GRP_REG), P(None, GRP_REG), P(GRP_REG), P(GRP_REG)),
        out_specs=(P(None, GRP_REG), P(None, GRP_REG)),
        check_vma=False,
    )
```

```python
import functools

import jax
import jax.numpy as jnp
from jax import lax
from jax.experimental import pallas as pl
from jax.experimental.pallas import tpu as pltpu
from jax.sharding import Mesh
from jax.sharding import PartitionSpec as P

C_DEV = 128
P_DEV = 256
OBS = 2048
DAMPING = 4.0
WIDE = 2 * C_DEV
REG = ("reg_0", "reg_1", "reg_2")
GRP_REG = ("grp", "reg_0", "reg_1", "reg_2")
F32 = jnp.float32
BF16 = jnp.bfloat16
VMEM = pl.BlockSpec(memory_space=pltpu.VMEM)
HBM = pl.BlockSpec(memory_space=pltpu.HBM)
SMEM = pl.BlockSpec(memory_space=pltpu.SMEM)
ROWS = 56
VMEM_LIMIT = 32 * 1024 * 1024


def three_parts(x):
    high = x.astype(BF16)
    rest = x - high.astype(F32)
    middle = rest.astype(BF16)
    low = (rest - middle.astype(F32)).astype(BF16)
    return high, middle, low


def stacked(x):
    high, middle, low = three_parts(x)
    parts = [high.astype(F32), middle.astype(F32), low.astype(F32)]
    return jnp.concatenate(parts, 0).astype(BF16)


def folded(x):
    rows = x.shape[0] // 3
    return x[:rows] + x[rows : 2 * rows] + x[2 * rows :]


def pick(field, onehot):
    return lax.dot_general(
        field, onehot, (((1,), (0,)), ((), ())), preferred_element_type=F32
    )


def put(terms, onehot):
    return lax.dot_general(
        terms, onehot[...], (((1,), (1,)), ((), ())), preferred_element_type=F32
    )


def put_few(terms, onehot):
    half = WIDE // 2
    parts = [
        lax.dot_general(
            terms,
            onehot[k : k + half, :],
            (((1,), (1,)), ((), ())),
            preferred_element_type=F32,
        )
        for k in (0, half)
    ]
    return jnp.concatenate(parts, 1)


def write_onehot(out, index):
    rows = lax.broadcasted_iota(jnp.int32, (16, 128), 0)
    here = jnp.broadcast_to(index.astype(F32), (16, OBS)).astype(BF16)
    one, zero = jnp.ones((16, 128), BF16), jnp.zeros((16, 128), BF16)

    def step(k, carry):
        start = pl.multiple_of(k * 16, 16)
        ids = (rows + start).astype(F32).astype(BF16)
        for t in range(0, OBS, 128):
            out[pl.ds(start, 16), t : t + 128] = jnp.where(ids == here[:, t : t + 128], one, zero)
        return carry

    lax.fori_loop(0, WIDE // 16, step, 0, unroll=4)


def per_lane(x):
    row = jnp.sum(x, 0, keepdims=True)
    return functools.reduce(
        lambda a, b: a + b, [row[:, k : k + 128] for k in range(0, row.shape[1], 128)]
    )


def solve_points(vinv, g):
    a, b, c, d, e, f = [vinv[k : k + 1] for k in range(6)]
    x, y, z = [g[k : k + 1] for k in range(3)]
    rows = [a * x + b * y + c * z, b * x + d * y + e * z, c * x + e * y + f * z]
    return rows + [jnp.zeros((8 - 3, g.shape[1]), F32)]


def point_part(u, p, hot_p, vinv):
    g = folded(put_few(stacked(p[0] * u[0] + p[1] * u[1]), hot_p))
    s = jnp.concatenate(solve_points(vinv, g), 0)
    back = folded(pick(stacked(s), hot_p[...]))
    return g, s, [jnp.sum(p[i] * back, 0, keepdims=True) for i in range(2)]


def position(where, regions):
    device = where[0]
    return device >> (regions.bit_length() - 1), device & (regions - 1)


def indices(regions, region, camera):
    owners = camera >> (C_DEV.bit_length() - 1)
    low = ((owners >> (regions.bit_length() - 1)) * C_DEV) | (camera & (C_DEV - 1))
    return low, (owners & (regions - 1)) - region + 1


def to_tiles(tiles, chip, near, far):
    rows = chip.shape[1]
    for k in range(3):
        sums = chip[k] + (near[k] + far[k])
        for h in range(2):
            tiles[pl.ds(2 * k + h, rows, stride=8), :] = sums[:, 128 * h : 128 * h + 128]
    for k in (6, 7):
        tiles[pl.ds(k, rows, stride=8), :] = jnp.zeros((rows, 128), F32)


def tile(tiles, k):
    return tiles[8 * k : 8 * k + 8, :]


def first_kernel(
    regions, where, cam_hbm, pnt_hbm, res_hbm, camera_hbm, points_hbm,
    part, jx, px, vinv_out, gres_out, block_out, hot_p, hot_c, res, cam, pnt, camera, points, sems,
):
    pairs = [(points_hbm, points), (pnt_hbm, pnt), (res_hbm, res), (camera_hbm, camera), (cam_hbm, cam)]
    copies = [pltpu.make_async_copy(a, b, sems.at[k]) for k, (a, b) in enumerate(pairs)]
    for copy in copies:
        copy.start()
    group, region = position(where, regions)
    copies[0].wait()
    write_onehot(hot_p, points[...])
    for copy in copies[1:]:
        copy.wait()
    low, block = indices(regions, region, camera[...])
    block_out[...] = block
    write_onehot(hot_c, low)
    camf = cam[...].astype(F32)
    pf = pnt[...].astype(F32)
    zero5 = jnp.zeros((5, OBS), F32)
    zero7 = jnp.zeros((7, OBS), F32)
    for i in range(2):
        jx[i, 0:8, :] = camf[9 * i : 9 * i + 8]
        jx[i, 8:16, :] = jnp.concatenate([camf[9 * i + 8 : 9 * i + 9], zero7], 0)
        px[i] = jnp.concatenate([pf[3 * i : 3 * i + 3], zero5], 0)
    p = [px[0], px[1]]
    a = [jx[0, 0:8, :], jx[1, 0:8, :]]
    last = [jx[0, 8:9, :], jx[1, 8:9, :]]
    r = [res[0:1, :], res[1:2, :]]
    row = lax.broadcasted_iota(jnp.int32, (8, OBS), 0)
    squares = p[0] * p[0] + p[1] * p[1]
    turned = [
        jnp.where(row == 2, jnp.broadcast_to(x[0:1], x.shape), pltpu.roll(x, 7, 0)) for x in p
    ]
    products = p[0] * turned[0] + p[1] * turned[1]
    right = p[0] * r[0] + p[1] * r[1]
    sums = folded(put_few(stacked(jnp.concatenate([squares, products, right], 0)), hot_p))
    v00, v11, v22 = [sums[k : k + 1] + DAMPING for k in range(3)]
    v01, v12, v02 = [sums[8 + k : 9 + k] for k in range(3)]
    g = sums[16:24]
    c00 = v11 * v22 - v12 * v12
    c01 = v02 * v12 - v01 * v22
    c02 = v01 * v12 - v02 * v11
    c11 = v00 * v22 - v02 * v02
    c12 = v01 * v02 - v00 * v12
    c22 = v00 * v11 - v01 * v01
    scale = 1.0 / (v00 * c00 + v01 * c01 + v02 * c02)
    cofactors = jnp.concatenate(
        [c00, c01, c02, c11, c12, c22, jnp.zeros((2, P_DEV), F32)], 0
    )
    vinv = cofactors * scale
    vinv_out[...] = vinv
    gres_out[...] = g
    s = jnp.concatenate(solve_points(vinv, g), 0)
    back = folded(pick(stacked(s), hot_p[...]))
    rem = [r[i] - jnp.sum(p[i] * back, 0, keepdims=True) for i in range(2)]
    rolled = []
    for d in range(5):
        other = [x if d == 0 else pltpu.roll(x, d, 0) for x in a]
        rolled.append(a[0] * other[0] + a[1] * other[1])
    corner = last[0] * last[0] + last[1] * last[1]
    end = last[0] * rem[0] + last[1] * rem[1]
    rolled[4] = jnp.where(row < 4, rolled[4], jnp.where(row == 4, corner, end))
    edge = a[0] * last[0] + a[1] * last[1]
    gradient = a[0] * rem[0] + a[1] * rem[1]
    terms = stacked(jnp.concatenate(rolled + [edge, gradient], 0))
    for k in range(3):
        mask = jnp.where(block == k, 1.0, 0.0).astype(BF16)
        part[k] = folded(put(terms * mask, hot_c))


def solve_camera(low, inv, b):
    y = list(b)
    for k in range(9):
        y[k] = y[k] * inv[k]
        for i in range(k + 1, 9):
            y[i] = y[i] - low[i][k] * y[k]
    for k in range(8, -1, -1):
        y[k] = y[k] * inv[k]
        for i in range(k):
            y[i] = y[i] - low[k][i] * y[k]
    return y


def factor_camera(tiles, factor):
    def entry(i, j):
        if i == 8:
            k = 36 if j == 8 else 40 + j
        elif i - j < 4:
            k = 8 * (i - j) + i
        elif i - j == 4:
            k = 32 + j
        else:
            k = 8 * (8 - (i - j)) + j
        x = tile(tiles, k)
        return x + DAMPING if i == j else x

    low = [[None] * 9 for _ in range(9)]
    work = [[entry(i, j) if j <= i else None for j in range(9)] for i in range(9)]
    inv = []
    for k in range(9):
        inv.append(1.0 / jnp.sqrt(work[k][k]))
        for i in range(k + 1, 9):
            low[i][k] = work[i][k] * inv[k]
        for i in range(k + 1, 9):
            for j in range(k + 1, i + 1):
                work[i][j] = work[i][j] - low[i][k] * low[j][k]
    flat = [low[i][j] for i in range(9) for j in range(i)] + inv
    for k, x in enumerate(flat):
        factor[8 * k : 8 * k + 8, :] = x
    return low, inv


def read_factor(factor):
    low = [[None] * 9 for _ in range(9)]
    at = 0
    for i in range(9):
        for j in range(i):
            low[i][j] = tile(factor, at)
            at += 1
    return low, [tile(factor, at + k) for k in range(9)]


def apply_body(group, x, field, block, hot_p, hot_c, jx, px, vinv):
    for k in range(9):
        field[8 * k : 8 * k + 8, :] = x[k]
    for k in range(9, 16):
        field[8 * k : 8 * k + 8, :] = jnp.zeros((8, 128), F32)
    frames = [
        jnp.concatenate([field[pl.ds(2 * f + h, 16, stride=8), :] for h in range(2)], 1)
        for f in range(3)
    ]
    v = jnp.where(group == 0, frames[1][:, 0:128], frames[1][:, 128:256])
    picked = pick(jnp.concatenate([stacked(f) for f in frames], 0), hot_c[...])
    blocks = [folded(picked[48 * k : 48 * k + 48]) for k in range(3)]
    values = jnp.where(block == 0, blocks[0], jnp.where(block == 1, blocks[1], blocks[2]))
    u = [jnp.sum(jx[i] * values, 0, keepdims=True) for i in range(2)]
    p = [px[0], px[1]]
    g, s, ps = point_part(u, p, hot_p, vinv[...])
    return v, u, g, s, ps


def finish(hot_c, block, jx, ps, part):
    terms = stacked(jx[0] * ps[0] + jx[1] * ps[1])
    lhs = jnp.concatenate(
        [terms * jnp.where(block == k, 1.0, 0.0).astype(BF16) for k in range(3)], 0
    )
    out = put(lhs, hot_c)
    for k in range(3):
        part[k] = folded(out[48 * k : 48 * k + 48])


def scalar_rows(pairs):
    rows = [functools.reduce(lambda a, b: a + b, [per_lane(x) for x in pair]) for pair in pairs]
    return jnp.concatenate(rows + [jnp.zeros((8 - len(rows), 128), F32)], 0)


def scalars(v, v_old, u, rem, rem_old, g, s, s_old):
    return scalar_rows(
        [
            (DAMPING * v * v_old, u[0] * rem_old[0:1, :] + u[1] * rem_old[1:2, :]),
            (DAMPING * v * v, u[0] * rem[0] + u[1] * rem[1]),
            (g * s_old,),
            (g * s,),
        ]
    )


def start_kernel(
    regions, where, chip, near, far, block_in, hot_p, hot_c, jx, px, vinv,
    part, factor, v_out, g_out, s_out, rem_out, scal, tiles, field,
):
    group, region = position(where, regions)
    block = block_in[...]
    to_tiles(tiles, chip, near, far)
    lower, inv = factor_camera(tiles, factor)
    b = [-tile(tiles, 48 + k) for k in range(8)] + [-tile(tiles, 37)]
    x = solve_camera(lower, inv, b)
    dots = functools.reduce(lambda p, q: p + q, [b[k] * x[k] for k in range(9)])
    own = lax.broadcasted_iota(jnp.int32, (8, 128), 0) == 2 + group
    v, u, g, s, ps = apply_body(
        group, x, field, block, hot_p, hot_c, jx, px, vinv
    )
    rem = [u[i] - ps[i] for i in range(2)]
    v_out[...], g_out[...], s_out[...] = v, g, s
    rem_out[...] = jnp.concatenate(rem + [jnp.zeros((6, OBS), F32)], 0)
    finish(hot_c, block, jx, ps, part)
    scal[...] = scalar_rows(
        [
            (jnp.where(own, dots, 0.0),),
            (DAMPING * v * v, u[0] * rem[0] + u[1] * rem[1]),
            (g * s,),
        ]
    )


def next_kernel(
    regions, where, chip, near, far, factor, block_in, hot_p, hot_c, jx, px, vinv, v_old, s_old, rem_old,
    part, v_out, g_out, s_out, rem_out, scal, tiles, field,
):
    group, region = position(where, regions)
    block = block_in[...]
    to_tiles(tiles, chip, near, far)
    x = solve_camera(*read_factor(factor), [tile(tiles, k) for k in range(9)])
    v, u, g, s, ps = apply_body(
        group, x, field, block, hot_p, hot_c, jx, px, vinv
    )
    rem = [u[i] - ps[i] for i in range(2)]
    v_out[...], g_out[...], s_out[...] = v, g, s
    rem_out[...] = jnp.concatenate(rem + [jnp.zeros((6, OBS), F32)], 0)
    finish(hot_c, block, jx, ps, part)
    scal[...] = scalars(v, v_old[...], u, rem, rem_old, g, s, s_old[...])


def last_kernel(
    regions, where, chip, near, far, factor, block_in, hot_p, hot_c, jx, px, vinv, v_old, s_old, rem_old,
    scal0, scal1, v_out, g_out, sums, tiles, field,
):
    group, region = position(where, regions)
    block = block_in[...]
    to_tiles(tiles, chip, near, far)
    x = solve_camera(*read_factor(factor), [tile(tiles, k) for k in range(9)])
    v, u, g, s, ps = apply_body(
        group, x, field, block, hot_p, hot_c, jx, px, vinv
    )
    rem = [u[i] - ps[i] for i in range(2)]
    v_out[...], g_out[...] = v, g
    scal2 = scalars(v, v_old[...], u, rem, rem_old, g, s, s_old[...])
    rows = jnp.concatenate([scal0[...], scal1[...], scal2, jnp.zeros((8, 128), F32)], 0)
    ones = jnp.ones((128, 128), BF16)
    high, middle, low_part = three_parts(rows)
    sums[...] = sum(
        lax.dot_general(ones, x, (((1,), (1,)), ((), ())), preferred_element_type=F32)
        for x in (high, middle, low_part)
    )


def final_kernel(back, v0, v1, v2, g0, g1, g2, gres, vinv, cam, pnt):
    sums = jnp.sum(back[...], 0, keepdims=True)

    def value(k):
        return sums[:, k : k + 1]

    m = [value(k) for k in (0, 2, 10, 11, 18)]
    s = [value(k) for k in (1, 8, 9, 16, 17)]

    def form(h, x):
        terms = [x[i] * x[j] * h[i + j] for i in range(3) for j in range(3)]
        return functools.reduce(lambda p, q: p + q, terms)

    def ratio(x, y):
        return jnp.where(y > 0, x / jnp.where(y > 0, y, 1.0), 0.0)

    one, zero = jnp.ones((1, 1), F32), jnp.zeros((1, 1), F32)
    y = [zero, zero, zero]
    z = [one, zero, zero]
    d = list(z)
    current = m[0]
    for turn in range(3):
        step = ratio(current, form(s, d))
        y = [y[k] + step * d[k] for k in range(3)]
        if turn < 2:
            image = [d[0], d[1] - d[0], d[2] - d[1]]
            z = [z[k] - step * image[k] for k in range(3)]
            following = form(m, z)
            beta = ratio(following, current)
            d = [z[k] + beta * d[k] for k in range(3)]
            current = following
    x = y[0] * v0[...] + y[1] * v1[...] + y[2] * v2[...]
    cam[...] = x[0:9]
    g = gres[...] + (y[0] * g0[...] + y[1] * g1[...] + y[2] * g2[...])
    rows = solve_points(vinv[...], g)
    for k in range(3):
        pnt[k : k + 1, :] = -rows[k]


def shape(*dims, dtype=F32):
    return jax.ShapeDtypeStruct(dims, dtype)


def call(kernel, outs, *args, scalar=False, scratch=(), regions=None, inputs=VMEM):
    specs = [inputs] * len(args)
    if scalar:
        specs[0] = SMEM
    return pl.pallas_call(
        kernel if regions is None else functools.partial(kernel, regions),
        out_shape=outs,
        in_specs=specs,
        out_specs=[VMEM] * len(outs),
        scratch_shapes=scratch,
        compiler_params=pltpu.CompilerParams(vmem_limit_bytes=VMEM_LIMIT),
        name=kernel.__name__,
    )(*args)


def local(regions, cam_jacobian, point_jacobian, residuals, obs_camera, obs_point):
    where = (lax.axis_index("grp") * regions + lax.axis_index(REG)).reshape(1)
    arrays = (cam_jacobian, point_jacobian, residuals)
    arrays += (obs_camera.reshape(1, OBS), obs_point.reshape(1, OBS))
    arrays = [pltpu.with_memory_space_constraint(x, pltpu.HBM) for x in arrays]

    def both_ways(pairs):
        return pairs + [(b, a) for a, b in pairs]

    def device(core, region):
        return core * regions + region

    cores = both_ways([(device(0, r), device(1, r)) for r in range(regions)])
    inner = both_ways(
        [(device(0, r), device(0, r + 1)) for r in range(0, regions, 2)]
        + [(device(1, r + i), device(1, r + i + 2)) for r in range(0, regions, 4) for i in range(2)]
    )
    first, last = 0, regions - 1
    outer = both_ways(
        [(device(0, r + 1), device(0, r + 2)) for r in range(0, regions - 2, 2)]
        + [
            (device(1, r + i + 2), device(1, r + i + 4))
            for r in range(0, regions - 4, 4)
            for i in range(2)
        ]
    )
    for ring in (
        [device(0, first), device(1, first), device(1, first + 1)],
        [device(0, last), device(1, last), device(1, last - 1)],
    ):
        outer += [(ring[k], ring[(k + 1) % 3]) for k in range(3)]
    group, region = lax.axis_index("grp"), lax.axis_index(REG)
    near_core = group == 0
    rises = jnp.where(near_core, region % 2 == 0, region % 4 < 2)
    reach = jnp.where(near_core, 1, 2)
    above, below = region + reach <= last, region - reach >= first

    def swap(x, pairs):
        return lax.ppermute(x, GRP_REG, pairs)

    def totals(part):
        chip = part + swap(part, cores)
        lower, upper = chip[0:2], chip[1:3]
        from_outer = swap(jnp.where(rises, lower, upper), outer)
        from_inner = swap(jnp.where(rises, upper, lower), inner)
        up = jnp.where(above, jnp.where(rises, from_inner, from_outer), 0.0)
        down = jnp.where(below, jnp.where(rises, from_outer, from_inner), 0.0)
        came = jnp.stack(
            [
                jnp.where(near_core, down[0], down[1]),
                jnp.where(near_core, down[1] + up[0], 0.0),
                jnp.where(near_core, up[1], up[0]),
            ]
        )
        return chip, came, swap(came, cores)

    def sums(rows):
        return [shape(3, rows, WIDE)]

    run = functools.partial(call, scalar=True, regions=regions)
    field = pltpu.VMEM((128, 128), F32)
    per_point = shape(8, P_DEV)
    rest = [shape(16, 128), per_point, per_point, shape(8, OBS), shape(8, 128)]

    part, jx, px, vinv, gres, block, hot_p, hot_c = run(
        first_kernel,
        sums(ROWS)
        + [shape(2, 16, OBS), shape(2, 8, OBS), per_point, per_point]
        + [shape(1, OBS, dtype=jnp.int32)]
        + [shape(WIDE, OBS, dtype=BF16)] * 2,
        where, *arrays,
        scratch=[
            pltpu.VMEM((2, OBS), F32), pltpu.VMEM((18, OBS), BF16), pltpu.VMEM((6, OBS), BF16),
            pltpu.VMEM((1, OBS), jnp.int32), pltpu.VMEM((1, OBS), jnp.int32),
            pltpu.SemaphoreType.DMA((5,)),
        ],
        inputs=HBM,
    )
    common = (block, hot_p, hot_c, jx, px, vinv)
    part, factor, v0, g0, s0, rem0, scal0 = run(
        start_kernel,
        sums(16) + [shape(45 * 8, 128)] + rest,
        where, *totals(part), *common,
        scratch=[pltpu.VMEM((8 * ROWS, 128), F32), field],
    )
    part, v1, g1, s1, rem1, scal1 = run(
        next_kernel,
        sums(16) + rest,
        where, *totals(part), factor, *common, v0, s0, rem0,
        scratch=[field, field],
    )
    v2, g2, scalar_sums = run(
        last_kernel,
        [shape(16, 128), per_point, shape(128, 32)],
        where, *totals(part), factor, *common, v1, s1, rem1, scal0, scal1,
        scratch=[field, field],
    )
    back = lax.all_to_all(scalar_sums, GRP_REG, 0, 0, tiled=True)
    return call(
        final_kernel,
        [shape(9, C_DEV), shape(3, P_DEV)],
        back, v0, v1, v2, g0, g1, g2, gres, vinv,
    )


def solution(mesh):
    torus = Mesh(
        mesh.devices.reshape(mesh.shape["grp"], 4, 4, 4), ("grp", "reg_0", "reg_1", "reg_2")
    )
    return jax.shard_map(
        functools.partial(local, mesh.shape["reg"]),
        mesh=torus,
        in_specs=(P(None, GRP_REG), P(None, GRP_REG), P(None, GRP_REG), P(GRP_REG), P(GRP_REG)),
        out_specs=(P(None, GRP_REG), P(None, GRP_REG)),
        check_vma=False,
    )
```

```python
import functools

import jax
import jax.numpy as jnp
from jax import lax
from jax.experimental import pallas as pl
from jax.experimental.pallas import tpu as pltpu
from jax.sharding import Mesh
from jax.sharding import PartitionSpec as P

C_DEV = 128
P_DEV = 256
OBS = 2048
DAMPING = 4.0
WIDE = 2 * C_DEV
REG = ("reg_0", "reg_1", "reg_2")
GRP_REG = ("grp", "reg_0", "reg_1", "reg_2")
F32 = jnp.float32
BF16 = jnp.bfloat16
VMEM = pl.BlockSpec(memory_space=pltpu.VMEM)
HBM = pl.BlockSpec(memory_space=pltpu.HBM)
SMEM = pl.BlockSpec(memory_space=pltpu.SMEM)
ROWS = 56
VMEM_LIMIT = 32 * 1024 * 1024


def three_parts(x):
    high = x.astype(BF16)
    rest = x - high.astype(F32)
    middle = rest.astype(BF16)
    low = (rest - middle.astype(F32)).astype(BF16)
    return high, middle, low


def stacked(x):
    high, middle, low = three_parts(x)
    parts = [high.astype(F32), middle.astype(F32), low.astype(F32)]
    return jnp.concatenate(parts, 0).astype(BF16)


def folded(x):
    rows = x.shape[0] // 3
    return x[:rows] + x[rows : 2 * rows] + x[2 * rows :]


def pick(field, onehot):
    return lax.dot_general(
        field, onehot, (((1,), (0,)), ((), ())), preferred_element_type=F32
    )


def put(terms, onehot):
    return lax.dot_general(
        terms, onehot[...], (((1,), (1,)), ((), ())), preferred_element_type=F32
    )


def put_few(terms, onehot):
    half = WIDE // 2
    parts = [
        lax.dot_general(
            terms,
            onehot[k : k + half, :],
            (((1,), (1,)), ((), ())),
            preferred_element_type=F32,
        )
        for k in (0, half)
    ]
    return jnp.concatenate(parts, 1)


def write_onehot(out, index):
    rows = lax.broadcasted_iota(jnp.int32, (16, 128), 0)
    here = jnp.broadcast_to(index.astype(F32), (16, OBS)).astype(BF16)
    one, zero = jnp.ones((16, 128), BF16), jnp.zeros((16, 128), BF16)

    def step(k, carry):
        start = pl.multiple_of(k * 16, 16)
        ids = (rows + start).astype(F32).astype(BF16)
        for t in range(0, OBS, 128):
            out[pl.ds(start, 16), t : t + 128] = jnp.where(ids == here[:, t : t + 128], one, zero)
        return carry

    lax.fori_loop(0, WIDE // 16, step, 0, unroll=4)


def per_lane(x):
    row = jnp.sum(x, 0, keepdims=True)
    return functools.reduce(
        lambda a, b: a + b, [row[:, k : k + 128] for k in range(0, row.shape[1], 128)]
    )


def solve_points(vinv, g):
    a, b, c, d, e, f = [vinv[k : k + 1] for k in range(6)]
    x, y, z = [g[k : k + 1] for k in range(3)]
    rows = [a * x + b * y + c * z, b * x + d * y + e * z, c * x + e * y + f * z]
    return rows + [jnp.zeros((8 - 3, g.shape[1]), F32)]


def point_part(u, p, hot_p, vinv):
    g = folded(put_few(stacked(p[0] * u[0] + p[1] * u[1]), hot_p))
    s = jnp.concatenate(solve_points(vinv, g), 0)
    back = folded(pick(stacked(s), hot_p[...]))
    return g, s, [jnp.sum(p[i] * back, 0, keepdims=True) for i in range(2)]


def position(where, regions):
    device = where[0]
    return device >> (regions.bit_length() - 1), device & (regions - 1)


def indices(regions, region, camera):
    owners = camera >> (C_DEV.bit_length() - 1)
    low = ((owners >> (regions.bit_length() - 1)) * C_DEV) | (camera & (C_DEV - 1))
    return low, (owners & (regions - 1)) - region + 1


def write_part(part, k, block):
    rows = part.shape[0] // 6
    for h in range(2):
        at = (2 * k + h) * rows
        part[at : at + rows, :] = block[0:rows, 128 * h : 128 * h + 128]


def to_tiles(tiles, chip, near, far):
    rows = chip.shape[0] // 6
    for k in range(6):
        run = slice(k * rows, k * rows + rows)
        tiles[pl.ds(k, rows, stride=8), :] = chip[run, :] + (near[run, :] + far[run, :])
    for k in (6, 7):
        tiles[pl.ds(k, rows, stride=8), :] = jnp.zeros((rows, 128), F32)


def tile(tiles, k):
    return tiles[8 * k : 8 * k + 8, :]


def first_kernel(
    regions, where, cam_hbm, pnt_hbm, res_hbm, camera_hbm, points_hbm,
    part, jx, px, vinv_out, gres_out, block_out, hot_p, hot_c, res, cam, pnt, camera, points, sems,
):
    pairs = [(points_hbm, points), (pnt_hbm, pnt), (res_hbm, res), (camera_hbm, camera), (cam_hbm, cam)]
    copies = [pltpu.make_async_copy(a, b, sems.at[k]) for k, (a, b) in enumerate(pairs)]
    for copy in copies:
        copy.start()
    group, region = position(where, regions)
    copies[0].wait()
    write_onehot(hot_p, points[...])
    for copy in copies[1:]:
        copy.wait()
    low, block = indices(regions, region, camera[...])
    block_out[...] = block
    write_onehot(hot_c, low)
    camf = cam[...].astype(F32)
    pf = pnt[...].astype(F32)
    zero5 = jnp.zeros((5, OBS), F32)
    zero7 = jnp.zeros((7, OBS), F32)
    for i in range(2):
        jx[i, 0:8, :] = camf[9 * i : 9 * i + 8]
        jx[i, 8:16, :] = jnp.concatenate([camf[9 * i + 8 : 9 * i + 9], zero7], 0)
        px[i] = jnp.concatenate([pf[3 * i : 3 * i + 3], zero5], 0)
    p = [px[0], px[1]]
    a = [jx[0, 0:8, :], jx[1, 0:8, :]]
    last = [jx[0, 8:9, :], jx[1, 8:9, :]]
    r = [res[0:1, :], res[1:2, :]]
    row = lax.broadcasted_iota(jnp.int32, (8, OBS), 0)
    squares = p[0] * p[0] + p[1] * p[1]
    turned = [
        jnp.where(row == 2, jnp.broadcast_to(x[0:1], x.shape), pltpu.roll(x, 7, 0)) for x in p
    ]
    products = p[0] * turned[0] + p[1] * turned[1]
    right = p[0] * r[0] + p[1] * r[1]
    sums = folded(put_few(stacked(jnp.concatenate([squares, products, right], 0)), hot_p))
    v00, v11, v22 = [sums[k : k + 1] + DAMPING for k in range(3)]
    v01, v12, v02 = [sums[8 + k : 9 + k] for k in range(3)]
    g = sums[16:24]
    c00 = v11 * v22 - v12 * v12
    c01 = v02 * v12 - v01 * v22
    c02 = v01 * v12 - v02 * v11
    c11 = v00 * v22 - v02 * v02
    c12 = v01 * v02 - v00 * v12
    c22 = v00 * v11 - v01 * v01
    scale = 1.0 / (v00 * c00 + v01 * c01 + v02 * c02)
    cofactors = jnp.concatenate(
        [c00, c01, c02, c11, c12, c22, jnp.zeros((2, P_DEV), F32)], 0
    )
    vinv = cofactors * scale
    vinv_out[...] = vinv
    gres_out[...] = g
    s = jnp.concatenate(solve_points(vinv, g), 0)
    back = folded(pick(stacked(s), hot_p[...]))
    rem = [r[i] - jnp.sum(p[i] * back, 0, keepdims=True) for i in range(2)]
    rolled = []
    for d in range(5):
        other = [x if d == 0 else pltpu.roll(x, d, 0) for x in a]
        rolled.append(a[0] * other[0] + a[1] * other[1])
    corner = last[0] * last[0] + last[1] * last[1]
    end = last[0] * rem[0] + last[1] * rem[1]
    rolled[4] = jnp.where(row < 4, rolled[4], jnp.where(row == 4, corner, end))
    edge = a[0] * last[0] + a[1] * last[1]
    gradient = a[0] * rem[0] + a[1] * rem[1]
    terms = stacked(jnp.concatenate(rolled + [edge, gradient], 0))
    lhs = jnp.concatenate(
        [terms * jnp.where(block == k, 1.0, 0.0).astype(BF16) for k in range(3)], 0
    )
    out = put(lhs, hot_c)
    for k in range(3):
        write_part(part, k, folded(out[3 * ROWS * k : 3 * ROWS * k + 3 * ROWS]))


def solve_camera(low, inv, b):
    y = list(b)
    for k in range(9):
        y[k] = y[k] * inv[k]
        for i in range(k + 1, 9):
            y[i] = y[i] - low[i][k] * y[k]
    for k in range(8, -1, -1):
        y[k] = y[k] * inv[k]
        for i in range(k):
            y[i] = y[i] - low[k][i] * y[k]
    return y


def factor_camera(tiles, factor):
    def entry(i, j):
        if i == 8:
            k = 36 if j == 8 else 40 + j
        elif i - j < 4:
            k = 8 * (i - j) + i
        elif i - j == 4:
            k = 32 + j
        else:
            k = 8 * (8 - (i - j)) + j
        x = tile(tiles, k)
        return x + DAMPING if i == j else x

    low = [[None] * 9 for _ in range(9)]
    work = [[entry(i, j) if j <= i else None for j in range(9)] for i in range(9)]
    inv = []
    for k in range(9):
        inv.append(1.0 / jnp.sqrt(work[k][k]))
        for i in range(k + 1, 9):
            low[i][k] = work[i][k] * inv[k]
        for i in range(k + 1, 9):
            for j in range(k + 1, i + 1):
                work[i][j] = work[i][j] - low[i][k] * low[j][k]
    flat = [low[i][j] for i in range(9) for j in range(i)] + inv
    for k, x in enumerate(flat):
        factor[8 * k : 8 * k + 8, :] = x
    return low, inv


def read_factor(factor):
    low = [[None] * 9 for _ in range(9)]
    at = 0
    for i in range(9):
        for j in range(i):
            low[i][j] = tile(factor, at)
            at += 1
    return low, [tile(factor, at + k) for k in range(9)]


def apply_body(group, x, field, block, hot_p, hot_c, jx, px, vinv):
    for k in range(9):
        field[8 * k : 8 * k + 8, :] = x[k]
    for k in range(9, 16):
        field[8 * k : 8 * k + 8, :] = jnp.zeros((8, 128), F32)
    frames = [
        jnp.concatenate([field[pl.ds(2 * f + h, 16, stride=8), :] for h in range(2)], 1)
        for f in range(3)
    ]
    v = jnp.where(group == 0, frames[1][:, 0:128], frames[1][:, 128:256])
    picked = pick(jnp.concatenate([stacked(f) for f in frames], 0), hot_c[...])
    blocks = [folded(picked[48 * k : 48 * k + 48]) for k in range(3)]
    values = jnp.where(block == 0, blocks[0], jnp.where(block == 1, blocks[1], blocks[2]))
    u = [jnp.sum(jx[i] * values, 0, keepdims=True) for i in range(2)]
    p = [px[0], px[1]]
    g, s, ps = point_part(u, p, hot_p, vinv[...])
    return v, u, g, s, ps


def finish(hot_c, block, jx, ps, part):
    terms = stacked(jx[0] * ps[0] + jx[1] * ps[1])
    lhs = jnp.concatenate(
        [terms * jnp.where(block == k, 1.0, 0.0).astype(BF16) for k in range(3)], 0
    )
    out = put(lhs, hot_c)
    for k in range(3):
        write_part(part, k, folded(out[48 * k : 48 * k + 48]))


def scalar_rows(pairs):
    rows = [functools.reduce(lambda a, b: a + b, [per_lane(x) for x in pair]) for pair in pairs]
    return jnp.concatenate(rows + [jnp.zeros((8 - len(rows), 128), F32)], 0)


def scalars(v, v_old, u, rem, rem_old, g, s, s_old):
    return scalar_rows(
        [
            (DAMPING * v * v_old, u[0] * rem_old[0:1, :] + u[1] * rem_old[1:2, :]),
            (DAMPING * v * v, u[0] * rem[0] + u[1] * rem[1]),
            (g * s_old,),
            (g * s,),
        ]
    )


def start_kernel(
    regions, where, chip, near, far, block_in, hot_p, hot_c, jx, px, vinv,
    part, factor, v_out, g_out, s_out, rem_out, scal, tiles, field,
):
    group, region = position(where, regions)
    block = block_in[...]
    to_tiles(tiles, chip, near, far)
    lower, inv = factor_camera(tiles, factor)
    b = [-tile(tiles, 48 + k) for k in range(8)] + [-tile(tiles, 37)]
    x = solve_camera(lower, inv, b)
    dots = functools.reduce(lambda p, q: p + q, [b[k] * x[k] for k in range(9)])
    own = lax.broadcasted_iota(jnp.int32, (8, 128), 0) == 2 + group
    v, u, g, s, ps = apply_body(
        group, x, field, block, hot_p, hot_c, jx, px, vinv
    )
    rem = [u[i] - ps[i] for i in range(2)]
    v_out[...], g_out[...], s_out[...] = v, g, s
    rem_out[...] = jnp.concatenate(rem + [jnp.zeros((6, OBS), F32)], 0)
    finish(hot_c, block, jx, ps, part)
    scal[...] = scalar_rows(
        [
            (jnp.where(own, dots, 0.0),),
            (DAMPING * v * v, u[0] * rem[0] + u[1] * rem[1]),
            (g * s,),
        ]
    )


def next_kernel(
    regions, where, chip, near, far, factor, block_in, hot_p, hot_c, jx, px, vinv, v_old, s_old, rem_old,
    part, v_out, g_out, s_out, rem_out, scal, tiles, field,
):
    group, region = position(where, regions)
    block = block_in[...]
    to_tiles(tiles, chip, near, far)
    x = solve_camera(*read_factor(factor), [tile(tiles, k) for k in range(9)])
    v, u, g, s, ps = apply_body(
        group, x, field, block, hot_p, hot_c, jx, px, vinv
    )
    rem = [u[i] - ps[i] for i in range(2)]
    v_out[...], g_out[...], s_out[...] = v, g, s
    rem_out[...] = jnp.concatenate(rem + [jnp.zeros((6, OBS), F32)], 0)
    finish(hot_c, block, jx, ps, part)
    scal[...] = scalars(v, v_old[...], u, rem, rem_old, g, s, s_old[...])


def last_kernel(
    regions, where, chip, near, far, factor, block_in, hot_p, hot_c, jx, px, vinv, v_old, s_old, rem_old,
    scal0, scal1, v_out, g_out, sums, tiles, field,
):
    group, region = position(where, regions)
    block = block_in[...]
    to_tiles(tiles, chip, near, far)
    x = solve_camera(*read_factor(factor), [tile(tiles, k) for k in range(9)])
    v, u, g, s, ps = apply_body(
        group, x, field, block, hot_p, hot_c, jx, px, vinv
    )
    rem = [u[i] - ps[i] for i in range(2)]
    v_out[...], g_out[...] = v, g
    scal2 = scalars(v, v_old[...], u, rem, rem_old, g, s, s_old[...])
    rows = jnp.concatenate([scal0[...], scal1[...], scal2, jnp.zeros((8, 128), F32)], 0)
    ones = jnp.ones((128, 128), BF16)
    high, middle, low_part = three_parts(rows)
    sums[...] = sum(
        lax.dot_general(ones, x, (((1,), (1,)), ((), ())), preferred_element_type=F32)
        for x in (high, middle, low_part)
    )


def final_kernel(back, v0, v1, v2, g0, g1, g2, gres, vinv, cam, pnt):
    sums = jnp.sum(back[...], 0, keepdims=True)

    def value(k):
        return sums[:, k : k + 1]

    m = [value(k) for k in (0, 2, 10, 11, 18)]
    s = [value(k) for k in (1, 8, 9, 16, 17)]

    def form(h, x):
        terms = [x[i] * x[j] * h[i + j] for i in range(3) for j in range(3)]
        return functools.reduce(lambda p, q: p + q, terms)

    def ratio(x, y):
        return jnp.where(y > 0, x / jnp.where(y > 0, y, 1.0), 0.0)

    one, zero = jnp.ones((1, 1), F32), jnp.zeros((1, 1), F32)
    y = [zero, zero, zero]
    z = [one, zero, zero]
    d = list(z)
    current = m[0]
    for turn in range(3):
        step = ratio(current, form(s, d))
        y = [y[k] + step * d[k] for k in range(3)]
        if turn < 2:
            image = [d[0], d[1] - d[0], d[2] - d[1]]
            z = [z[k] - step * image[k] for k in range(3)]
            following = form(m, z)
            beta = ratio(following, current)
            d = [z[k] + beta * d[k] for k in range(3)]
            current = following
    x = y[0] * v0[...] + y[1] * v1[...] + y[2] * v2[...]
    cam[...] = x[0:9]
    g = gres[...] + (y[0] * g0[...] + y[1] * g1[...] + y[2] * g2[...])
    rows = solve_points(vinv[...], g)
    for k in range(3):
        pnt[k : k + 1, :] = -rows[k]


def shape(*dims, dtype=F32):
    return jax.ShapeDtypeStruct(dims, dtype)


def call(kernel, outs, *args, scalar=False, scratch=(), regions=None, inputs=VMEM):
    specs = [inputs] * len(args)
    if scalar:
        specs[0] = SMEM
    return pl.pallas_call(
        kernel if regions is None else functools.partial(kernel, regions),
        out_shape=outs,
        in_specs=specs,
        out_specs=[VMEM] * len(outs),
        scratch_shapes=scratch,
        compiler_params=pltpu.CompilerParams(vmem_limit_bytes=VMEM_LIMIT),
        name=kernel.__name__,
    )(*args)


def local(regions, cam_jacobian, point_jacobian, residuals, obs_camera, obs_point):
    where = (lax.axis_index("grp") * regions + lax.axis_index(REG)).reshape(1)
    arrays = (cam_jacobian, point_jacobian, residuals)
    arrays += (obs_camera.reshape(1, OBS), obs_point.reshape(1, OBS))
    arrays = [pltpu.with_memory_space_constraint(x, pltpu.HBM) for x in arrays]

    def both_ways(pairs):
        return pairs + [(b, a) for a, b in pairs]

    def device(core, region):
        return core * regions + region

    cores = both_ways([(device(0, r), device(1, r)) for r in range(regions)])
    inner = both_ways(
        [(device(0, r), device(0, r + 1)) for r in range(0, regions, 2)]
        + [(device(1, r + i), device(1, r + i + 2)) for r in range(0, regions, 4) for i in range(2)]
    )
    first, last = 0, regions - 1
    outer = both_ways(
        [(device(0, r + 1), device(0, r + 2)) for r in range(0, regions - 2, 2)]
        + [
            (device(1, r + i + 2), device(1, r + i + 4))
            for r in range(0, regions - 4, 4)
            for i in range(2)
        ]
    )
    for ring in (
        [device(0, first), device(1, first), device(1, first + 1)],
        [device(0, last), device(1, last), device(1, last - 1)],
    ):
        outer += [(ring[k], ring[(k + 1) % 3]) for k in range(3)]
    group, region = lax.axis_index("grp"), lax.axis_index(REG)
    near_core = group == 0
    rises = jnp.where(near_core, region % 2 == 0, region % 4 < 2)
    reach = jnp.where(near_core, 1, 2)
    above, below = region + reach <= last, region - reach >= first

    def swap(x, pairs):
        return lax.ppermute(x, GRP_REG, pairs)

    def totals(part):
        chip = part + swap(part, cores)
        size = part.shape[0] // 3
        lower, upper = chip[: 2 * size], chip[size:]
        from_outer = swap(jnp.where(rises, lower, upper), outer)
        from_inner = swap(jnp.where(rises, upper, lower), inner)
        up = jnp.where(above, jnp.where(rises, from_inner, from_outer), 0.0)
        down = jnp.where(below, jnp.where(rises, from_outer, from_inner), 0.0)
        came = jnp.concatenate(
            [
                jnp.where(near_core, down[:size], down[size:]),
                jnp.where(near_core, down[size:] + up[:size], 0.0),
                jnp.where(near_core, up[size:], up[:size]),
            ]
        )
        return chip, came, swap(came, cores)

    def sums(rows):
        return [shape(6 * rows, 128)]

    run = functools.partial(call, scalar=True, regions=regions)
    field = pltpu.VMEM((128, 128), F32)
    per_point = shape(8, P_DEV)
    rest = [shape(16, 128), per_point, per_point, shape(8, OBS), shape(8, 128)]

    part, jx, px, vinv, gres, block, hot_p, hot_c = run(
        first_kernel,
        sums(ROWS)
        + [shape(2, 16, OBS), shape(2, 8, OBS), per_point, per_point]
        + [shape(1, OBS, dtype=jnp.int32)]
        + [shape(WIDE, OBS, dtype=BF16)] * 2,
        where, *arrays,
        scratch=[
            pltpu.VMEM((2, OBS), F32), pltpu.VMEM((18, OBS), BF16), pltpu.VMEM((6, OBS), BF16),
            pltpu.VMEM((1, OBS), jnp.int32), pltpu.VMEM((1, OBS), jnp.int32),
            pltpu.SemaphoreType.DMA((5,)),
        ],
        inputs=HBM,
    )
    common = (block, hot_p, hot_c, jx, px, vinv)
    part, factor, v0, g0, s0, rem0, scal0 = run(
        start_kernel,
        sums(9) + [shape(45 * 8, 128)] + rest,
        where, *totals(part), *common,
        scratch=[pltpu.VMEM((8 * ROWS, 128), F32), field],
    )
    part, v1, g1, s1, rem1, scal1 = run(
        next_kernel,
        sums(9) + rest,
        where, *totals(part), factor, *common, v0, s0, rem0,
        scratch=[field, field],
    )
    v2, g2, scalar_sums = run(
        last_kernel,
        [shape(16, 128), per_point, shape(128, 32)],
        where, *totals(part), factor, *common, v1, s1, rem1, scal0, scal1,
        scratch=[field, field],
    )
    back = lax.all_to_all(scalar_sums, GRP_REG, 0, 0, tiled=True)
    return call(
        final_kernel,
        [shape(9, C_DEV), shape(3, P_DEV)],
        back, v0, v1, v2, g0, g1, g2, gres, vinv,
    )


def solution(mesh):
    torus = Mesh(
        mesh.devices.reshape(mesh.shape["grp"], 4, 4, 4), ("grp", "reg_0", "reg_1", "reg_2")
    )
    return jax.shard_map(
        functools.partial(local, mesh.shape["reg"]),
        mesh=torus,
        in_specs=(P(None, GRP_REG), P(None, GRP_REG), P(None, GRP_REG), P(GRP_REG), P(GRP_REG)),
        out_specs=(P(None, GRP_REG), P(None, GRP_REG)),
        check_vma=False,
    )
```

```python
import functools

import jax
import jax.numpy as jnp
from jax import lax
from jax.experimental import pallas as pl
from jax.experimental.pallas import tpu as pltpu
from jax.sharding import Mesh
from jax.sharding import PartitionSpec as P

C_DEV = 128
P_DEV = 256
OBS = 2048
DAMPING = 4.0
WIDE = 2 * C_DEV
REG = ("reg_0", "reg_1", "reg_2")
GRP_REG = ("grp", "reg_0", "reg_1", "reg_2")
F32 = jnp.float32
BF16 = jnp.bfloat16
VMEM = pl.BlockSpec(memory_space=pltpu.VMEM)
HBM = pl.BlockSpec(memory_space=pltpu.HBM)
SMEM = pl.BlockSpec(memory_space=pltpu.SMEM)
ROWS = 56
VMEM_LIMIT = 32 * 1024 * 1024


def three_parts(x):
    high = x.astype(BF16)
    rest = x - high.astype(F32)
    middle = rest.astype(BF16)
    low = (rest - middle.astype(F32)).astype(BF16)
    return high, middle, low


def stacked(x):
    high, middle, low = three_parts(x)
    parts = [high.astype(F32), middle.astype(F32), low.astype(F32)]
    return jnp.concatenate(parts, 0).astype(BF16)


def folded(x):
    rows = x.shape[0] // 3
    return x[:rows] + x[rows : 2 * rows] + x[2 * rows :]


def pick(field, onehot):
    return lax.dot_general(
        field, onehot, (((1,), (0,)), ((), ())), preferred_element_type=F32
    )


def put(terms, onehot):
    return lax.dot_general(
        terms, onehot[...], (((1,), (1,)), ((), ())), preferred_element_type=F32
    )


def put_few(terms, onehot):
    half = WIDE // 2
    parts = [
        lax.dot_general(
            terms,
            onehot[k : k + half, :],
            (((1,), (1,)), ((), ())),
            preferred_element_type=F32,
        )
        for k in (0, half)
    ]
    return jnp.concatenate(parts, 1)


def write_onehot(out, index):
    rows = lax.broadcasted_iota(jnp.int32, (16, 128), 0)
    here = jnp.broadcast_to(index.astype(F32), (16, OBS)).astype(BF16)
    one, zero = jnp.ones((16, 128), BF16), jnp.zeros((16, 128), BF16)

    def step(k, carry):
        start = pl.multiple_of(k * 16, 16)
        ids = (rows + start).astype(F32).astype(BF16)
        for t in range(0, OBS, 128):
            out[pl.ds(start, 16), t : t + 128] = jnp.where(ids == here[:, t : t + 128], one, zero)
        return carry

    lax.fori_loop(0, WIDE // 16, step, 0, unroll=4)


def per_lane(x):
    row = jnp.sum(x, 0, keepdims=True)
    return functools.reduce(
        lambda a, b: a + b, [row[:, k : k + 128] for k in range(0, row.shape[1], 128)]
    )


def solve_points(vinv, g):
    a, b, c, d, e, f = [vinv[k : k + 1] for k in range(6)]
    x, y, z = [g[k : k + 1] for k in range(3)]
    rows = [a * x + b * y + c * z, b * x + d * y + e * z, c * x + e * y + f * z]
    return rows + [jnp.zeros((8 - 3, g.shape[1]), F32)]


def point_part(u, p, hot_p, vinv):
    g = folded(put_few(stacked(p[0] * u[0] + p[1] * u[1]), hot_p))
    s = jnp.concatenate(solve_points(vinv, g), 0)
    back = folded(pick(stacked(s), hot_p[...]))
    return g, s, [jnp.sum(p[i] * back, 0, keepdims=True) for i in range(2)]


def position(where, regions):
    device = where[0]
    return device >> (regions.bit_length() - 1), device & (regions - 1)


def indices(regions, region, camera):
    owners = camera >> (C_DEV.bit_length() - 1)
    low = ((owners >> (regions.bit_length() - 1)) * C_DEV) | (camera & (C_DEV - 1))
    return low, (owners & (regions - 1)) - region + 1


def write_part(part, k, block):
    rows = part.shape[0] // 6
    for h in range(2):
        at = (2 * k + h) * rows
        part[at : at + rows, :] = block[0:rows, 128 * h : 128 * h + 128]


def to_tiles(tiles, chip, near, far):
    rows = chip.shape[0] // 6
    for k in range(6):
        run = slice(k * rows, k * rows + rows)
        tiles[pl.ds(k, rows, stride=8), :] = chip[run, :] + (near[run, :] + far[run, :])
    for k in (6, 7):
        tiles[pl.ds(k, rows, stride=8), :] = jnp.zeros((rows, 128), F32)


def tile(tiles, k):
    return tiles[8 * k : 8 * k + 8, :]


def first_kernel(
    regions, where, cam_hbm, pnt_hbm, res_hbm, camera_hbm, points_hbm,
    part, jx, px, vinv_out, gres_out, block_out, hot_p, hot_c, res, cam, pnt, camera, points, sems,
):
    pairs = [(points_hbm, points), (pnt_hbm, pnt), (res_hbm, res), (camera_hbm, camera), (cam_hbm, cam)]
    copies = [pltpu.make_async_copy(a, b, sems.at[k]) for k, (a, b) in enumerate(pairs)]
    for copy in copies:
        copy.start()
    group, region = position(where, regions)
    copies[0].wait()
    write_onehot(hot_p, points[...])
    for copy in copies[1:]:
        copy.wait()
    low, block = indices(regions, region, camera[...])
    block_out[...] = block
    write_onehot(hot_c, low)
    camf = cam[...].astype(F32)
    pf = pnt[...].astype(F32)
    zero5 = jnp.zeros((5, OBS), F32)
    zero7 = jnp.zeros((7, OBS), F32)
    for i in range(2):
        jx[i, 0:8, :] = camf[9 * i : 9 * i + 8]
        jx[i, 8:16, :] = jnp.concatenate([camf[9 * i + 8 : 9 * i + 9], zero7], 0)
        px[i] = jnp.concatenate([pf[3 * i : 3 * i + 3], zero5], 0)
    p = [px[0], px[1]]
    a = [jx[0, 0:8, :], jx[1, 0:8, :]]
    last = [jx[0, 8:9, :], jx[1, 8:9, :]]
    r = [res[0:1, :], res[1:2, :]]
    row = lax.broadcasted_iota(jnp.int32, (8, OBS), 0)
    squares = p[0] * p[0] + p[1] * p[1]
    turned = [
        jnp.where(row == 2, jnp.broadcast_to(x[0:1], x.shape), pltpu.roll(x, 7, 0)) for x in p
    ]
    products = p[0] * turned[0] + p[1] * turned[1]
    right = p[0] * r[0] + p[1] * r[1]
    sums = folded(put_few(stacked(jnp.concatenate([squares, products, right], 0)), hot_p))
    v00, v11, v22 = [sums[k : k + 1] + DAMPING for k in range(3)]
    v01, v12, v02 = [sums[8 + k : 9 + k] for k in range(3)]
    g = sums[16:24]
    c00 = v11 * v22 - v12 * v12
    c01 = v02 * v12 - v01 * v22
    c02 = v01 * v12 - v02 * v11
    c11 = v00 * v22 - v02 * v02
    c12 = v01 * v02 - v00 * v12
    c22 = v00 * v11 - v01 * v01
    scale = 1.0 / (v00 * c00 + v01 * c01 + v02 * c02)
    cofactors = jnp.concatenate(
        [c00, c01, c02, c11, c12, c22, jnp.zeros((2, P_DEV), F32)], 0
    )
    vinv = cofactors * scale
    vinv_out[...] = vinv
    gres_out[...] = g
    s = jnp.concatenate(solve_points(vinv, g), 0)
    back = folded(pick(stacked(s), hot_p[...]))
    rem = [r[i] - jnp.sum(p[i] * back, 0, keepdims=True) for i in range(2)]
    rolled = []
    for d in range(5):
        other = [x if d == 0 else pltpu.roll(x, d, 0) for x in a]
        rolled.append(a[0] * other[0] + a[1] * other[1])
    corner = last[0] * last[0] + last[1] * last[1]
    end = last[0] * rem[0] + last[1] * rem[1]
    rolled[4] = jnp.where(row < 4, rolled[4], jnp.where(row == 4, corner, end))
    edge = a[0] * last[0] + a[1] * last[1]
    gradient = a[0] * rem[0] + a[1] * rem[1]
    terms = stacked(jnp.concatenate(rolled + [edge, gradient], 0))
    lhs = jnp.concatenate(
        [terms * jnp.where(block == k, 1.0, 0.0).astype(BF16) for k in range(3)], 0
    )
    out = put(lhs, hot_c)
    for k in range(3):
        write_part(part, k, folded(out[3 * ROWS * k : 3 * ROWS * k + 3 * ROWS]))


def solve_camera(low, inv, b):
    y = list(b)
    for k in range(9):
        y[k] = y[k] * inv[k]
        for i in range(k + 1, 9):
            y[i] = y[i] - low[i][k] * y[k]
    for k in range(8, -1, -1):
        y[k] = y[k] * inv[k]
        for i in range(k):
            y[i] = y[i] - low[k][i] * y[k]
    return y


def factor_camera(tiles, factor):
    def entry(i, j):
        if i == 8:
            k = 36 if j == 8 else 40 + j
        elif i - j < 4:
            k = 8 * (i - j) + i
        elif i - j == 4:
            k = 32 + j
        else:
            k = 8 * (8 - (i - j)) + j
        x = tile(tiles, k)
        return x + DAMPING if i == j else x

    low = [[None] * 9 for _ in range(9)]
    work = [[entry(i, j) if j <= i else None for j in range(9)] for i in range(9)]
    inv = []
    for k in range(9):
        inv.append(1.0 / jnp.sqrt(work[k][k]))
        for i in range(k + 1, 9):
            low[i][k] = work[i][k] * inv[k]
        for i in range(k + 1, 9):
            for j in range(k + 1, i + 1):
                work[i][j] = work[i][j] - low[i][k] * low[j][k]
    flat = [low[i][j] for i in range(9) for j in range(i)] + inv
    for k, x in enumerate(flat):
        factor[8 * k : 8 * k + 8, :] = x
    return low, inv


def read_factor(factor):
    low = [[None] * 9 for _ in range(9)]
    at = 0
    for i in range(9):
        for j in range(i):
            low[i][j] = tile(factor, at)
            at += 1
    return low, [tile(factor, at + k) for k in range(9)]


def parts_of(x):
    return [part.astype(F32) for part in three_parts(x)]


def apply_body(group, x, field, block, hot_p, hot_c, jx, px, vinv):
    for k in range(9):
        field[8 * k : 8 * k + 8, :] = x[k]
    frames = [
        jnp.concatenate([field[pl.ds(2 * f + h, 8, stride=8), :] for h in range(2)], 1)
        for f in range(3)
    ]
    ends = jnp.concatenate([field[pl.ds(64 + h, 4, stride=2), :] for h in range(2)], 1)
    frames.append(jnp.concatenate([ends, jnp.zeros((4, WIDE), F32)], 0))
    own = jnp.concatenate([frames[1], ends[1:2], jnp.zeros((7, WIDE), F32)], 0)
    v = jnp.where(group == 0, own[:, 0:128], own[:, 128:256])
    rows = [part for f in frames for part in parts_of(f)]
    picked = pick(jnp.concatenate(rows, 0).astype(BF16), hot_c[...])
    blocks = [folded(picked[24 * k : 24 * k + 24]) for k in range(4)]
    values = jnp.where(block == 0, blocks[0], jnp.where(block == 1, blocks[1], blocks[2]))
    end = jnp.where(lax.broadcasted_iota(jnp.int32, (8, OBS), 0) == block, blocks[3], 0.0)
    u = [
        jnp.sum(jx[i, 0:8, :] * values + jx[i, 8:9, :] * end, 0, keepdims=True)
        for i in range(2)
    ]
    p = [px[0], px[1]]
    g, s, ps = point_part(u, p, hot_p, vinv[...])
    return v, u, g, s, ps


def finish(hot_c, block, jx, ps, part):
    terms = stacked(jx[0] * ps[0] + jx[1] * ps[1])
    lhs = jnp.concatenate(
        [terms * jnp.where(block == k, 1.0, 0.0).astype(BF16) for k in range(3)], 0
    )
    out = put(lhs, hot_c)
    for k in range(3):
        write_part(part, k, folded(out[48 * k : 48 * k + 48]))


def scalar_rows(pairs):
    rows = [functools.reduce(lambda a, b: a + b, [per_lane(x) for x in pair]) for pair in pairs]
    return jnp.concatenate(rows + [jnp.zeros((8 - len(rows), 128), F32)], 0)


def scalars(v, v_old, u, rem, rem_old, g, s, s_old):
    return scalar_rows(
        [
            (DAMPING * v * v_old, u[0] * rem_old[0:1, :] + u[1] * rem_old[1:2, :]),
            (DAMPING * v * v, u[0] * rem[0] + u[1] * rem[1]),
            (g * s_old,),
            (g * s,),
        ]
    )


def start_kernel(
    regions, where, chip, near, far, block_in, hot_p, hot_c, jx, px, vinv,
    part, factor, v_out, g_out, s_out, rem_out, scal, tiles, field,
):
    group, region = position(where, regions)
    block = block_in[...]
    to_tiles(tiles, chip, near, far)
    lower, inv = factor_camera(tiles, factor)
    b = [-tile(tiles, 48 + k) for k in range(8)] + [-tile(tiles, 37)]
    x = solve_camera(lower, inv, b)
    dots = functools.reduce(lambda p, q: p + q, [b[k] * x[k] for k in range(9)])
    own = lax.broadcasted_iota(jnp.int32, (8, 128), 0) == 2 + group
    v, u, g, s, ps = apply_body(
        group, x, field, block, hot_p, hot_c, jx, px, vinv
    )
    rem = [u[i] - ps[i] for i in range(2)]
    v_out[...], g_out[...], s_out[...] = v, g, s
    rem_out[...] = jnp.concatenate(rem + [jnp.zeros((6, OBS), F32)], 0)
    finish(hot_c, block, jx, ps, part)
    scal[...] = scalar_rows(
        [
            (jnp.where(own, dots, 0.0),),
            (DAMPING * v * v, u[0] * rem[0] + u[1] * rem[1]),
            (g * s,),
        ]
    )


def next_kernel(
    regions, where, chip, near, far, factor, block_in, hot_p, hot_c, jx, px, vinv, v_old, s_old, rem_old,
    part, v_out, g_out, s_out, rem_out, scal, tiles, field,
):
    group, region = position(where, regions)
    block = block_in[...]
    to_tiles(tiles, chip, near, far)
    x = solve_camera(*read_factor(factor), [tile(tiles, k) for k in range(9)])
    v, u, g, s, ps = apply_body(
        group, x, field, block, hot_p, hot_c, jx, px, vinv
    )
    rem = [u[i] - ps[i] for i in range(2)]
    v_out[...], g_out[...], s_out[...] = v, g, s
    rem_out[...] = jnp.concatenate(rem + [jnp.zeros((6, OBS), F32)], 0)
    finish(hot_c, block, jx, ps, part)
    scal[...] = scalars(v, v_old[...], u, rem, rem_old, g, s, s_old[...])


def last_kernel(
    regions, where, chip, near, far, factor, block_in, hot_p, hot_c, jx, px, vinv, v_old, s_old, rem_old,
    scal0, scal1, v_out, g_out, sums, tiles, field,
):
    group, region = position(where, regions)
    block = block_in[...]
    to_tiles(tiles, chip, near, far)
    x = solve_camera(*read_factor(factor), [tile(tiles, k) for k in range(9)])
    v, u, g, s, ps = apply_body(
        group, x, field, block, hot_p, hot_c, jx, px, vinv
    )
    rem = [u[i] - ps[i] for i in range(2)]
    v_out[...], g_out[...] = v, g
    scal2 = scalars(v, v_old[...], u, rem, rem_old, g, s, s_old[...])
    rows = jnp.concatenate([scal0[...], scal1[...], scal2, jnp.zeros((8, 128), F32)], 0)
    ones = jnp.ones((128, 128), BF16)
    high, middle, low_part = three_parts(rows)
    sums[...] = sum(
        lax.dot_general(ones, x, (((1,), (1,)), ((), ())), preferred_element_type=F32)
        for x in (high, middle, low_part)
    )


def final_kernel(back, v0, v1, v2, g0, g1, g2, gres, vinv, cam_hbm, pnt_hbm, cam, pnt, sems):
    sums = jnp.sum(back[...], 0, keepdims=True)

    def value(k):
        return jnp.broadcast_to(sums[:, k : k + 1], (1, 128))

    m = [value(k) for k in (0, 2, 10, 11, 18)]
    s = [value(k) for k in (1, 8, 9, 16, 17)]

    def added(terms):
        while len(terms) > 1:
            pairs = [terms[k] + terms[k + 1] for k in range(0, len(terms) - 1, 2)]
            terms = pairs + terms[len(pairs) * 2 :]
        return terms[0]

    def form(h, x):
        n = len(x)
        squares = [
            added([x[i] * x[k - i] for i in range(n) if 0 <= k - i < n]) for k in range(2 * n - 1)
        ]
        return added([h[k] * squares[k] for k in range(2 * n - 1)])

    def ratio(x, y):
        return jnp.where(y > 0, x / jnp.where(y > 0, y, 1.0), 0.0)

    step = ratio(m[0], s[0])
    y = [step]
    z = [1.0 - step, step]
    d = [jnp.ones((1, 128), F32)]
    current = m[0]
    for turn in range(2):
        following = form(m, z)
        beta = ratio(following, current)
        d = [p + beta * q for p, q in zip(z, d)] + [z[-1]]
        current = following
        step = ratio(current, form(s, d))
        y = [p + step * q for p, q in zip(y, d)] + [step * d[-1]]
        if turn == 0:
            image = [d[0], d[1] - d[0], -d[1]]
            z = [p - step * q for p, q in zip(z + [0.0], image)]
    x = y[0] * v0[...] + y[1] * v1[...] + y[2] * v2[...]
    cam[...] = x[0:9]
    copies = [
        pltpu.make_async_copy(a, b, sems.at[k])
        for k, (a, b) in enumerate([(cam, cam_hbm), (pnt, pnt_hbm)])
    ]
    copies[0].start()
    y = [jnp.concatenate([c, c], 1) for c in y]
    g = gres[...] + (y[0] * g0[...] + y[1] * g1[...] + y[2] * g2[...])
    rows = solve_points(vinv[...], g)
    for k in range(3):
        pnt[k : k + 1, :] = -rows[k]
    copies[1].start()
    for copy in copies:
        copy.wait()


def shape(*dims, dtype=F32):
    return jax.ShapeDtypeStruct(dims, dtype)


def call(
    kernel, outs, *args, scalar=False, scratch=(), regions=None, inputs=VMEM, outputs=VMEM
):
    specs = [inputs] * len(args)
    if scalar:
        specs[0] = SMEM
    return pl.pallas_call(
        kernel if regions is None else functools.partial(kernel, regions),
        out_shape=outs,
        in_specs=specs,
        out_specs=[outputs] * len(outs),
        scratch_shapes=scratch,
        compiler_params=pltpu.CompilerParams(vmem_limit_bytes=VMEM_LIMIT),
        name=kernel.__name__,
    )(*args)


def local(regions, cam_jacobian, point_jacobian, residuals, obs_camera, obs_point):
    where = (lax.axis_index("grp") * regions + lax.axis_index(REG)).reshape(1)
    arrays = (cam_jacobian, point_jacobian, residuals)
    arrays += (obs_camera.reshape(1, OBS), obs_point.reshape(1, OBS))
    arrays = [pltpu.with_memory_space_constraint(x, pltpu.HBM) for x in arrays]

    def both_ways(pairs):
        return pairs + [(b, a) for a, b in pairs]

    def device(core, region):
        return core * regions + region

    cores = both_ways([(device(0, r), device(1, r)) for r in range(regions)])
    inner = both_ways(
        [(device(0, r), device(0, r + 1)) for r in range(0, regions, 2)]
        + [(device(1, r + i), device(1, r + i + 2)) for r in range(0, regions, 4) for i in range(2)]
    )
    first, last = 0, regions - 1
    outer = both_ways(
        [(device(0, r + 1), device(0, r + 2)) for r in range(0, regions - 2, 2)]
        + [
            (device(1, r + i + 2), device(1, r + i + 4))
            for r in range(0, regions - 4, 4)
            for i in range(2)
        ]
    )
    for ring in (
        [device(0, first), device(1, first), device(1, first + 1)],
        [device(0, last), device(1, last), device(1, last - 1)],
    ):
        outer += [(ring[k], ring[(k + 1) % 3]) for k in range(3)]
    group, region = lax.axis_index("grp"), lax.axis_index(REG)
    near_core = group == 0
    rises = jnp.where(near_core, region % 2 == 0, region % 4 < 2)
    reach = jnp.where(near_core, 1, 2)
    above, below = region + reach <= last, region - reach >= first

    def swap(x, pairs):
        return lax.ppermute(x, GRP_REG, pairs)

    def totals(part):
        chip = part + swap(part, cores)
        size = part.shape[0] // 3
        lower, upper = chip[: 2 * size], chip[size:]
        from_outer = swap(jnp.where(rises, lower, upper), outer)
        from_inner = swap(jnp.where(rises, upper, lower), inner)
        up = jnp.where(above, jnp.where(rises, from_inner, from_outer), 0.0)
        down = jnp.where(below, jnp.where(rises, from_outer, from_inner), 0.0)
        came = jnp.concatenate(
            [
                jnp.where(near_core, down[:size], down[size:]),
                jnp.where(near_core, down[size:] + up[:size], 0.0),
                jnp.where(near_core, up[size:], up[:size]),
            ]
        )
        return chip, came, swap(came, cores)

    def sums(rows):
        return [shape(6 * rows, 128)]

    run = functools.partial(call, scalar=True, regions=regions)
    field = pltpu.VMEM((128, 128), F32)
    per_point = shape(8, P_DEV)
    rest = [shape(16, 128), per_point, per_point, shape(8, OBS), shape(8, 128)]

    part, jx, px, vinv, gres, block, hot_p, hot_c = run(
        first_kernel,
        sums(ROWS)
        + [shape(2, 16, OBS), shape(2, 8, OBS), per_point, per_point]
        + [shape(1, OBS, dtype=jnp.int32)]
        + [shape(WIDE, OBS, dtype=BF16)] * 2,
        where, *arrays,
        scratch=[
            pltpu.VMEM((2, OBS), F32), pltpu.VMEM((18, OBS), BF16), pltpu.VMEM((6, OBS), BF16),
            pltpu.VMEM((1, OBS), jnp.int32), pltpu.VMEM((1, OBS), jnp.int32),
            pltpu.SemaphoreType.DMA((5,)),
        ],
        inputs=HBM,
    )
    common = (block, hot_p, hot_c, jx, px, vinv)
    part, factor, v0, g0, s0, rem0, scal0 = run(
        start_kernel,
        sums(9) + [shape(45 * 8, 128)] + rest,
        where, *totals(part), *common,
        scratch=[pltpu.VMEM((8 * ROWS, 128), F32), field],
    )
    part, v1, g1, s1, rem1, scal1 = run(
        next_kernel,
        sums(9) + rest,
        where, *totals(part), factor, *common, v0, s0, rem0,
        scratch=[field, field],
    )
    v2, g2, scalar_sums = run(
        last_kernel,
        [shape(16, 128), per_point, shape(128, 32)],
        where, *totals(part), factor, *common, v1, s1, rem1, scal0, scal1,
        scratch=[field, field],
    )
    back = lax.all_to_all(scalar_sums, GRP_REG, 0, 0, tiled=True)
    return call(
        final_kernel,
        [shape(9, C_DEV), shape(3, P_DEV)],
        back, v0, v1, v2, g0, g1, g2, gres, vinv,
        scratch=[
            pltpu.VMEM((9, C_DEV), F32), pltpu.VMEM((3, P_DEV), F32),
            pltpu.SemaphoreType.DMA((2,)),
        ],
        outputs=HBM,
    )


def solution(mesh):
    torus = Mesh(
        mesh.devices.reshape(mesh.shape["grp"], 4, 4, 4), ("grp", "reg_0", "reg_1", "reg_2")
    )
    return jax.shard_map(
        functools.partial(local, mesh.shape["reg"]),
        mesh=torus,
        in_specs=(P(None, GRP_REG), P(None, GRP_REG), P(None, GRP_REG), P(GRP_REG), P(GRP_REG)),
        out_specs=(P(None, GRP_REG), P(None, GRP_REG)),
        check_vma=False,
    )
```

```python
import functools

import jax
import jax.numpy as jnp
from jax import lax
from jax.experimental import pallas as pl
from jax.experimental.pallas import tpu as pltpu
from jax.sharding import Mesh
from jax.sharding import PartitionSpec as P

C_DEV = 128
P_DEV = 256
OBS = 2048
DAMPING = 4.0
WIDE = 2 * C_DEV
REG = ("reg_0", "reg_1", "reg_2")
GRP_REG = ("grp", "reg_0", "reg_1", "reg_2")
F32 = jnp.float32
BF16 = jnp.bfloat16
VMEM = pl.BlockSpec(memory_space=pltpu.VMEM)
HBM = pl.BlockSpec(memory_space=pltpu.HBM)
SMEM = pl.BlockSpec(memory_space=pltpu.SMEM)
ROWS = 56
VMEM_LIMIT = 32 * 1024 * 1024


def three_parts(x):
    high = x.astype(BF16)
    rest = x - high.astype(F32)
    middle = rest.astype(BF16)
    low = (rest - middle.astype(F32)).astype(BF16)
    return high, middle, low


def stacked(x):
    high, middle, low = three_parts(x)
    parts = [high.astype(F32), middle.astype(F32), low.astype(F32)]
    return jnp.concatenate(parts, 0).astype(BF16)


def folded(x):
    rows = x.shape[0] // 3
    return x[:rows] + x[rows : 2 * rows] + x[2 * rows :]


def pick(field, onehot):
    return lax.dot_general(
        field, onehot, (((1,), (0,)), ((), ())), preferred_element_type=F32
    )


def put(terms, onehot):
    return lax.dot_general(
        terms, onehot[...], (((1,), (1,)), ((), ())), preferred_element_type=F32
    )


def put_few(terms, onehot):
    half = WIDE // 2
    parts = [
        lax.dot_general(
            terms,
            onehot[k : k + half, :],
            (((1,), (1,)), ((), ())),
            preferred_element_type=F32,
        )
        for k in (0, half)
    ]
    return jnp.concatenate(parts, 1)


def write_onehot(out, index):
    rows = lax.broadcasted_iota(jnp.int32, (16, 128), 0)
    here = jnp.broadcast_to(index.astype(F32), (16, OBS)).astype(BF16)
    one, zero = jnp.ones((16, 128), BF16), jnp.zeros((16, 128), BF16)

    def step(k, carry):
        start = pl.multiple_of(k * 16, 16)
        ids = (rows + start).astype(F32).astype(BF16)
        for t in range(0, OBS, 128):
            out[pl.ds(start, 16), t : t + 128] = jnp.where(ids == here[:, t : t + 128], one, zero)
        return carry

    lax.fori_loop(0, WIDE // 16, step, 0, unroll=4)


def per_lane(x):
    row = jnp.sum(x, 0, keepdims=True)
    return functools.reduce(
        lambda a, b: a + b, [row[:, k : k + 128] for k in range(0, row.shape[1], 128)]
    )


def solve_points(vinv, g):
    return vinv[0:8] * g[0:1] + vinv[8:16] * g[1:2] + vinv[16:24] * g[2:3]


def point_part(u, p, hot_p, vinv):
    g = folded(put_few(stacked(p[0] * u[0] + p[1] * u[1]), hot_p))
    s = solve_points(vinv, g)
    back = folded(pick(stacked(s), hot_p[...]))
    return g, s, [jnp.sum(p[i] * back, 0, keepdims=True) for i in range(2)]


def position(where, regions):
    device = where[0]
    return device >> (regions.bit_length() - 1), device & (regions - 1)


def indices(regions, region, camera):
    owners = camera >> (C_DEV.bit_length() - 1)
    low = ((owners >> (regions.bit_length() - 1)) * C_DEV) | (camera & (C_DEV - 1))
    return low, (owners & (regions - 1)) - region + 1


def write_part(part, k, block):
    rows = part.shape[0] // 6
    for h in range(2):
        at = (2 * k + h) * rows
        part[at : at + rows, :] = block[0:rows, 128 * h : 128 * h + 128]


def to_tiles(tiles, chip, near, far):
    rows = chip.shape[0] // 6
    for k in range(6):
        run = slice(k * rows, k * rows + rows)
        tiles[pl.ds(k, rows, stride=8), :] = chip[run, :] + (near[run, :] + far[run, :])
    for k in (6, 7):
        tiles[pl.ds(k, rows, stride=8), :] = jnp.zeros((rows, 128), F32)


def tile(tiles, k):
    return tiles[8 * k : 8 * k + 8, :]


def first_kernel(
    regions, where, cam_hbm, pnt_hbm, res_hbm, camera_hbm, points_hbm,
    part, jx, px, vinv_out, gres_out, block_out, hot_p, hot_c, res, cam, pnt, camera, points, sems,
):
    pairs = [(points_hbm, points), (pnt_hbm, pnt), (res_hbm, res), (camera_hbm, camera), (cam_hbm, cam)]
    copies = [pltpu.make_async_copy(a, b, sems.at[k]) for k, (a, b) in enumerate(pairs)]
    for copy in copies:
        copy.start()
    group, region = position(where, regions)
    copies[0].wait()
    write_onehot(hot_p, points[...])
    for copy in copies[1:]:
        copy.wait()
    low, block = indices(regions, region, camera[...])
    block_out[...] = block
    write_onehot(hot_c, low)
    camf = cam[...].astype(F32)
    pf = pnt[...].astype(F32)
    zero5 = jnp.zeros((5, OBS), F32)
    zero7 = jnp.zeros((7, OBS), F32)
    for i in range(2):
        jx[i, 0:8, :] = camf[9 * i : 9 * i + 8]
        jx[i, 8:16, :] = jnp.concatenate([camf[9 * i + 8 : 9 * i + 9], zero7], 0)
        px[i] = jnp.concatenate([pf[3 * i : 3 * i + 3], zero5], 0)
    p = [px[0], px[1]]
    a = [jx[0, 0:8, :], jx[1, 0:8, :]]
    last = [jx[0, 8:9, :], jx[1, 8:9, :]]
    r = [res[0:1, :], res[1:2, :]]
    row = lax.broadcasted_iota(jnp.int32, (8, OBS), 0)
    squares = p[0] * p[0] + p[1] * p[1]
    turned = [
        jnp.where(row == 2, jnp.broadcast_to(x[0:1], x.shape), pltpu.roll(x, 7, 0)) for x in p
    ]
    products = p[0] * turned[0] + p[1] * turned[1]
    right = p[0] * r[0] + p[1] * r[1]
    sums = folded(put_few(stacked(jnp.concatenate([squares, products, right], 0)), hot_p))
    v00, v11, v22 = [sums[k : k + 1] + DAMPING for k in range(3)]
    v01, v12, v02 = [sums[8 + k : 9 + k] for k in range(3)]
    g = sums[16:24]
    c00 = v11 * v22 - v12 * v12
    c01 = v02 * v12 - v01 * v22
    c02 = v01 * v12 - v02 * v11
    c11 = v00 * v22 - v02 * v02
    c12 = v01 * v02 - v00 * v12
    c22 = v00 * v11 - v01 * v01
    scale = 1.0 / (v00 * c00 + v01 * c01 + v02 * c02)
    rest = [jnp.zeros((5, P_DEV), F32)]
    columns = [c00, c01, c02] + rest + [c01, c11, c12] + rest + [c02, c12, c22] + rest
    cofactors = jnp.concatenate(columns, 0)
    vinv = cofactors * scale
    vinv_out[...] = vinv
    gres_out[...] = g
    s = solve_points(vinv, g)
    back = folded(pick(stacked(s), hot_p[...]))
    rem = [r[i] - jnp.sum(p[i] * back, 0, keepdims=True) for i in range(2)]
    rolled = []
    for d in range(5):
        other = [x if d == 0 else pltpu.roll(x, d, 0) for x in a]
        rolled.append(a[0] * other[0] + a[1] * other[1])
    corner = last[0] * last[0] + last[1] * last[1]
    end = last[0] * rem[0] + last[1] * rem[1]
    rolled[4] = jnp.where(row < 4, rolled[4], jnp.where(row == 4, corner, end))
    edge = a[0] * last[0] + a[1] * last[1]
    gradient = a[0] * rem[0] + a[1] * rem[1]
    terms = stacked(jnp.concatenate(rolled + [edge, gradient], 0))
    lhs = jnp.concatenate(
        [terms * jnp.where(block == k, 1.0, 0.0).astype(BF16) for k in range(3)], 0
    )
    out = put(lhs, hot_c)
    for k in range(3):
        write_part(part, k, folded(out[3 * ROWS * k : 3 * ROWS * k + 3 * ROWS]))


def solve_camera(low, inv, b):
    y = list(b)
    for k in range(9):
        y[k] = y[k] * inv[k]
        for i in range(k + 1, 9):
            y[i] = y[i] - low[i][k] * y[k]
    for k in range(8, -1, -1):
        y[k] = y[k] * inv[k]
        for i in range(k):
            y[i] = y[i] - low[k][i] * y[k]
    return y


def factor_camera(tiles, factor):
    def entry(i, j):
        if i == 8:
            k = 36 if j == 8 else 40 + j
        elif i - j < 4:
            k = 8 * (i - j) + i
        elif i - j == 4:
            k = 32 + j
        else:
            k = 8 * (8 - (i - j)) + j
        x = tile(tiles, k)
        return x + DAMPING if i == j else x

    low = [[None] * 9 for _ in range(9)]
    work = [[entry(i, j) if j <= i else None for j in range(9)] for i in range(9)]
    inv = []
    for k in range(9):
        inv.append(1.0 / jnp.sqrt(work[k][k]))
        for i in range(k + 1, 9):
            low[i][k] = work[i][k] * inv[k]
        for i in range(k + 1, 9):
            for j in range(k + 1, i + 1):
                work[i][j] = work[i][j] - low[i][k] * low[j][k]
    flat = [low[i][j] for i in range(9) for j in range(i)] + inv
    for k, x in enumerate(flat):
        factor[8 * k : 8 * k + 8, :] = x
    return low, inv


def read_factor(factor):
    low = [[None] * 9 for _ in range(9)]
    at = 0
    for i in range(9):
        for j in range(i):
            low[i][j] = tile(factor, at)
            at += 1
    return low, [tile(factor, at + k) for k in range(9)]


def parts_of(x):
    return [part.astype(F32) for part in three_parts(x)]


def apply_body(group, x, field, block, hot_p, hot_c, jx, px, vinv):
    for k in range(9):
        field[8 * k : 8 * k + 8, :] = x[k]
    frames = [
        jnp.concatenate([field[pl.ds(2 * f + h, 8, stride=8), :] for h in range(2)], 1)
        for f in range(3)
    ]
    ends = jnp.concatenate([field[pl.ds(64 + h, 4, stride=2), :] for h in range(2)], 1)
    frames.append(jnp.concatenate([ends, jnp.zeros((4, WIDE), F32)], 0))
    own = jnp.concatenate([frames[1], ends[1:2], jnp.zeros((7, WIDE), F32)], 0)
    v = jnp.where(group == 0, own[:, 0:128], own[:, 128:256])
    rows = [part for f in frames for part in parts_of(f)]
    picked = pick(jnp.concatenate(rows, 0).astype(BF16), hot_c[...])
    blocks = [folded(picked[24 * k : 24 * k + 24]) for k in range(4)]
    values = jnp.where(block == 0, blocks[0], jnp.where(block == 1, blocks[1], blocks[2]))
    end = jnp.where(lax.broadcasted_iota(jnp.int32, (8, OBS), 0) == block, blocks[3], 0.0)
    u = [
        jnp.sum(jx[i, 0:8, :] * values + jx[i, 8:9, :] * end, 0, keepdims=True)
        for i in range(2)
    ]
    p = [px[0], px[1]]
    g, s, ps = point_part(u, p, hot_p, vinv[...])
    return v, u, g, s, ps


def finish(hot_c, block, jx, ps, part):
    terms = stacked(jx[0] * ps[0] + jx[1] * ps[1])
    lhs = jnp.concatenate(
        [terms * jnp.where(block == k, 1.0, 0.0).astype(BF16) for k in range(3)], 0
    )
    out = put(lhs, hot_c)
    for k in range(3):
        write_part(part, k, folded(out[48 * k : 48 * k + 48]))


def scalar_rows(pairs):
    rows = [functools.reduce(lambda a, b: a + b, [per_lane(x) for x in pair]) for pair in pairs]
    return jnp.concatenate(rows + [jnp.zeros((8 - len(rows), 128), F32)], 0)


def scalars(v, v_old, u, rem, rem_old, g, s, s_old):
    return scalar_rows(
        [
            (DAMPING * v * v_old, u[0] * rem_old[0:1, :] + u[1] * rem_old[1:2, :]),
            (DAMPING * v * v, u[0] * rem[0] + u[1] * rem[1]),
            (g * s_old,),
            (g * s,),
        ]
    )


def start_kernel(
    regions, where, chip, near, far, block_in, hot_p, hot_c, jx, px, vinv,
    part, factor, v_out, g_out, s_out, rem_out, scal, tiles, field,
):
    group, region = position(where, regions)
    block = block_in[...]
    to_tiles(tiles, chip, near, far)
    lower, inv = factor_camera(tiles, factor)
    b = [-tile(tiles, 48 + k) for k in range(8)] + [-tile(tiles, 37)]
    x = solve_camera(lower, inv, b)
    dots = functools.reduce(lambda p, q: p + q, [b[k] * x[k] for k in range(9)])
    own = lax.broadcasted_iota(jnp.int32, (8, 128), 0) == 2 + group
    v, u, g, s, ps = apply_body(
        group, x, field, block, hot_p, hot_c, jx, px, vinv
    )
    rem = [u[i] - ps[i] for i in range(2)]
    v_out[...], g_out[...], s_out[...] = v, g, s
    rem_out[...] = jnp.concatenate(rem + [jnp.zeros((6, OBS), F32)], 0)
    finish(hot_c, block, jx, ps, part)
    scal[...] = scalar_rows(
        [
            (jnp.where(own, dots, 0.0),),
            (DAMPING * v * v, u[0] * rem[0] + u[1] * rem[1]),
            (g * s,),
        ]
    )


def next_kernel(
    regions, where, chip, near, far, factor, block_in, hot_p, hot_c, jx, px, vinv, v_old, s_old, rem_old,
    part, v_out, g_out, s_out, rem_out, scal, tiles, field,
):
    group, region = position(where, regions)
    block = block_in[...]
    to_tiles(tiles, chip, near, far)
    x = solve_camera(*read_factor(factor), [tile(tiles, k) for k in range(9)])
    v, u, g, s, ps = apply_body(
        group, x, field, block, hot_p, hot_c, jx, px, vinv
    )
    rem = [u[i] - ps[i] for i in range(2)]
    v_out[...], g_out[...], s_out[...] = v, g, s
    rem_out[...] = jnp.concatenate(rem + [jnp.zeros((6, OBS), F32)], 0)
    finish(hot_c, block, jx, ps, part)
    scal[...] = scalars(v, v_old[...], u, rem, rem_old, g, s, s_old[...])


def last_kernel(
    regions, where, chip, near, far, factor, block_in, hot_p, hot_c, jx, px, vinv, v_old, s_old, rem_old,
    scal0, scal1, v_out, g_out, sums, tiles, field,
):
    group, region = position(where, regions)
    block = block_in[...]
    to_tiles(tiles, chip, near, far)
    x = solve_camera(*read_factor(factor), [tile(tiles, k) for k in range(9)])
    v, u, g, s, ps = apply_body(
        group, x, field, block, hot_p, hot_c, jx, px, vinv
    )
    rem = [u[i] - ps[i] for i in range(2)]
    v_out[...], g_out[...] = v, g
    scal2 = scalars(v, v_old[...], u, rem, rem_old, g, s, s_old[...])
    rows = jnp.concatenate([scal0[...], scal1[...], scal2, jnp.zeros((8, 128), F32)], 0)
    ones = jnp.ones((128, 128), BF16)
    high, middle, low_part = three_parts(rows)
    sums[...] = sum(
        lax.dot_general(ones, x, (((1,), (1,)), ((), ())), preferred_element_type=F32)
        for x in (high, middle, low_part)
    )


def final_kernel(back, v0, v1, v2, g0, g1, g2, gres, vinv, cam_hbm, pnt_hbm, cam, pnt, sems):
    sums = jnp.sum(back[...], 0, keepdims=True)

    def value(k):
        return jnp.broadcast_to(sums[:, k : k + 1], (1, 128))

    m = [value(k) for k in (0, 2, 10, 11, 18)]
    s = [value(k) for k in (1, 8, 9, 16, 17)]

    def added(terms):
        while len(terms) > 1:
            pairs = [terms[k] + terms[k + 1] for k in range(0, len(terms) - 1, 2)]
            terms = pairs + terms[len(pairs) * 2 :]
        return terms[0]

    def form(h, x):
        n = len(x)
        squares = [
            added([x[i] * x[k - i] for i in range(n) if 0 <= k - i < n]) for k in range(2 * n - 1)
        ]
        return added([h[k] * squares[k] for k in range(2 * n - 1)])

    def ratio(x, y):
        return jnp.where(y > 0, x / jnp.where(y > 0, y, 1.0), 0.0)

    step = ratio(m[0], s[0])
    y = [step]
    z = [1.0 - step, step]
    d = [jnp.ones((1, 128), F32)]
    current = m[0]
    for turn in range(2):
        following = form(m, z)
        beta = ratio(following, current)
        d = [p + beta * q for p, q in zip(z, d)] + [z[-1]]
        current = following
        step = ratio(current, form(s, d))
        y = [p + step * q for p, q in zip(y, d)] + [step * d[-1]]
        if turn == 0:
            image = [d[0], d[1] - d[0], -d[1]]
            z = [p - step * q for p, q in zip(z + [0.0], image)]
    x = y[0] * v0[...] + y[1] * v1[...] + y[2] * v2[...]
    cam[...] = x[0:9]
    copies = [
        pltpu.make_async_copy(a, b, sems.at[k])
        for k, (a, b) in enumerate([(cam, cam_hbm), (pnt, pnt_hbm)])
    ]
    copies[0].start()
    y = [jnp.concatenate([c, c], 1) for c in y]
    g = gres[...] + (y[0] * g0[...] + y[1] * g1[...] + y[2] * g2[...])
    pnt[...] = -solve_points(vinv[...], g)[0:3]
    copies[1].start()
    for copy in copies:
        copy.wait()


def shape(*dims, dtype=F32):
    return jax.ShapeDtypeStruct(dims, dtype)


def call(
    kernel, outs, *args, scalar=False, scratch=(), regions=None, inputs=VMEM, outputs=VMEM
):
    specs = [inputs] * len(args)
    if scalar:
        specs[0] = SMEM
    return pl.pallas_call(
        kernel if regions is None else functools.partial(kernel, regions),
        out_shape=outs,
        in_specs=specs,
        out_specs=[outputs] * len(outs),
        scratch_shapes=scratch,
        compiler_params=pltpu.CompilerParams(vmem_limit_bytes=VMEM_LIMIT),
        name=kernel.__name__,
    )(*args)


def local(regions, cam_jacobian, point_jacobian, residuals, obs_camera, obs_point):
    where = (lax.axis_index("grp") * regions + lax.axis_index(REG)).reshape(1)
    arrays = (cam_jacobian, point_jacobian, residuals)
    arrays += (obs_camera.reshape(1, OBS), obs_point.reshape(1, OBS))
    arrays = [pltpu.with_memory_space_constraint(x, pltpu.HBM) for x in arrays]

    def both_ways(pairs):
        return pairs + [(b, a) for a, b in pairs]

    def device(core, region):
        return core * regions + region

    cores = both_ways([(device(0, r), device(1, r)) for r in range(regions)])
    inner = both_ways(
        [(device(0, r), device(0, r + 1)) for r in range(0, regions, 2)]
        + [(device(1, r + i), device(1, r + i + 2)) for r in range(0, regions, 4) for i in range(2)]
    )
    first, last = 0, regions - 1
    outer = both_ways(
        [(device(0, r + 1), device(0, r + 2)) for r in range(0, regions - 2, 2)]
        + [
            (device(1, r + i + 2), device(1, r + i + 4))
            for r in range(0, regions - 4, 4)
            for i in range(2)
        ]
    )
    for ring in (
        [device(0, first), device(1, first), device(1, first + 1)],
        [device(0, last), device(1, last), device(1, last - 1)],
    ):
        outer += [(ring[k], ring[(k + 1) % 3]) for k in range(3)]
    group, region = lax.axis_index("grp"), lax.axis_index(REG)
    near_core = group == 0
    rises = jnp.where(near_core, region % 2 == 0, region % 4 < 2)
    reach = jnp.where(near_core, 1, 2)
    above, below = region + reach <= last, region - reach >= first

    def swap(x, pairs):
        return lax.ppermute(x, GRP_REG, pairs)

    def totals(part):
        chip = part + swap(part, cores)
        size = part.shape[0] // 3
        lower, upper = chip[: 2 * size], chip[size:]
        from_outer = swap(jnp.where(rises, lower, upper), outer)
        from_inner = swap(jnp.where(rises, upper, lower), inner)
        up = jnp.where(above, jnp.where(rises, from_inner, from_outer), 0.0)
        down = jnp.where(below, jnp.where(rises, from_outer, from_inner), 0.0)
        came = jnp.concatenate(
            [
                jnp.where(near_core, down[:size], down[size:]),
                jnp.where(near_core, down[size:] + up[:size], 0.0),
                jnp.where(near_core, up[size:], up[:size]),
            ]
        )
        return chip, came, swap(came, cores)

    def sums(rows):
        return [shape(6 * rows, 128)]

    run = functools.partial(call, scalar=True, regions=regions)
    field = pltpu.VMEM((128, 128), F32)
    per_point = shape(8, P_DEV)
    rest = [shape(16, 128), per_point, per_point, shape(8, OBS), shape(8, 128)]

    part, jx, px, vinv, gres, block, hot_p, hot_c = run(
        first_kernel,
        sums(ROWS)
        + [shape(2, 16, OBS), shape(2, 8, OBS), shape(24, P_DEV), per_point]
        + [shape(1, OBS, dtype=jnp.int32)]
        + [shape(WIDE, OBS, dtype=BF16)] * 2,
        where, *arrays,
        scratch=[
            pltpu.VMEM((2, OBS), F32), pltpu.VMEM((18, OBS), BF16), pltpu.VMEM((6, OBS), BF16),
            pltpu.VMEM((1, OBS), jnp.int32), pltpu.VMEM((1, OBS), jnp.int32),
            pltpu.SemaphoreType.DMA((5,)),
        ],
        inputs=HBM,
    )
    common = (block, hot_p, hot_c, jx, px, vinv)
    part, factor, v0, g0, s0, rem0, scal0 = run(
        start_kernel,
        sums(9) + [shape(45 * 8, 128)] + rest,
        where, *totals(part), *common,
        scratch=[pltpu.VMEM((8 * ROWS, 128), F32), field],
    )
    part, v1, g1, s1, rem1, scal1 = run(
        next_kernel,
        sums(9) + rest,
        where, *totals(part), factor, *common, v0, s0, rem0,
        scratch=[field, field],
    )
    v2, g2, scalar_sums = run(
        last_kernel,
        [shape(16, 128), per_point, shape(128, 32)],
        where, *totals(part), factor, *common, v1, s1, rem1, scal0, scal1,
        scratch=[field, field],
    )
    back = lax.all_to_all(scalar_sums, GRP_REG, 0, 0, tiled=True)
    return call(
        final_kernel,
        [shape(9, C_DEV), shape(3, P_DEV)],
        back, v0, v1, v2, g0, g1, g2, gres, vinv,
        scratch=[
            pltpu.VMEM((9, C_DEV), F32), pltpu.VMEM((3, P_DEV), F32),
            pltpu.SemaphoreType.DMA((2,)),
        ],
        outputs=HBM,
    )


def solution(mesh):
    torus = Mesh(
        mesh.devices.reshape(mesh.shape["grp"], 4, 4, 4), ("grp", "reg_0", "reg_1", "reg_2")
    )
    return jax.shard_map(
        functools.partial(local, mesh.shape["reg"]),
        mesh=torus,
        in_specs=(P(None, GRP_REG), P(None, GRP_REG), P(None, GRP_REG), P(GRP_REG), P(GRP_REG)),
        out_specs=(P(None, GRP_REG), P(None, GRP_REG)),
        check_vma=False,
    )
```
